128 devices in a mesh: dp: 8 (over x, core), sy: 4 (over z), sx: 4 (over y).
Axes of the slice: x: 4, y: 4, z: 4, core: 2. Of those that a mesh axis runs over, the one named last changes fastest.
Arguments:
- features: bfloat16 [8, 64, 256, 768], P('dp', 'sy', 'sx'), may hold values from -100 to 100
- depth_weight: float32 [7, 7, 768], replicated, may hold values from -0.875 to 0.875
- depth_bias: float32 [768], replicated, may hold values from -3 to 3
- reduce_weight: bfloat16 [768, 256], replicated, may hold values from -0.21875 to 0.21875
- reduce_bias: float32 [256], replicated, may hold values from -3 to 3
- class_weight: bfloat16 [10, 256, 256], replicated, may hold values from -0.375 to 0.375
- class_bias: float32 [10], replicated, may hold values from -4 to 4
- labels: int32 [8], P('dp'), may hold values from 0 to 9
Outputs:
- loss: float32 [], replicated
- depth_weight_grad: float32 [7, 7, 768], replicated
- depth_bias_grad: float32 [768], replicated
- reduce_weight_grad: float32 [768, 256], replicated
- reduce_bias_grad: float32 [256], replicated
- class_weight_grad: float32 [10, 256, 256], replicated
- class_bias_grad: float32 [10], replicated
The draws below stay inside these ranges and needn't reach their ends.
All inputs are finite; a program needn't handle non-finite values.
Results may differ from the reference program's by a relative error of at most 0.006.
Values may be sent and summed in bfloat16 or wider, within the bound.
A program may use at most 64 MiB of HBM per device.

```python
import jax
import jax.numpy as jnp
from jax import lax

CHANNELS = 768
REDUCED = 256
CLASSES = 10
KERNEL = 7
NEWTON_STEPS = 5
IMAGES = 8
ROWS_ALL = 64
COLS_ALL = 256


def draw_features(key, part):
    subkeys = jax.random.split(key, 4)
    shape = (IMAGES, ROWS_ALL, COLS_ALL, CHANNELS)
    channel_scale = jnp.exp(jax.random.uniform(subkeys[1], (IMAGES, 1, 1, CHANNELS), jnp.float32, jnp.log(0.3), jnp.log(3.0)))
    patch_scale = jnp.exp(jax.random.uniform(subkeys[2], (IMAGES, ROWS_ALL // 4, COLS_ALL // 4, 1), jnp.float32, jnp.log(0.6), jnp.log(1.6)))
    patch_scale = jnp.repeat(jnp.repeat(patch_scale, 4, axis=1), 4, axis=2)
    pixel_scale = jax.random.uniform(subkeys[3], (IMAGES, ROWS_ALL, COLS_ALL, 1), jnp.float32, 0.7, 1.4)
    row_place = (jnp.arange(ROWS_ALL, dtype=jnp.float32) / ROWS_ALL).reshape(1, ROWS_ALL, 1, 1)
    col_place = (jnp.arange(COLS_ALL, dtype=jnp.float32) / COLS_ALL).reshape(1, 1, COLS_ALL, 1)
    noise_field = jnp.clip(jax.random.normal(subkeys[0], shape, jnp.float32), -4.0, 4.0)
    row_trend = jnp.power(3.0, row_place) + 0.0 * col_place
    values = noise_field * channel_scale * patch_scale * pixel_scale * row_trend
    return values.astype(jnp.bfloat16)


def with_ends(result, own_key, smallest, high):
    longest = result.shape.index(max(result.shape))
    spots = []
    for shift in (0, 1):
        where = [jax.random.randint(jax.random.fold_in(own_key, axis), (), 0, length) for axis, length in enumerate(result.shape)]
        where[longest] = (where[longest] + shift) % result.shape[longest]
        spots.append(tuple(where))
    return result.at[spots[0]].set(smallest).at[spots[1]].set(high)


def normal_values(stream_key, extent, deviation, bound, held_as=jnp.bfloat16):
    return jnp.clip(deviation * jax.random.normal(stream_key, extent, jnp.float32), -bound, bound).astype(held_as)


def setup_inputs(seed: int = 0) -> dict:
    arg_keys = jax.random.split(jax.random.key(seed), 9)
    return {
        "features": draw_features(jax.random.fold_in(arg_keys[8], 71), 0),
        "depth_weight": normal_values(arg_keys[1], (KERNEL, KERNEL, CHANNELS), (KERNEL * KERNEL) ** -0.5, 0.875, jnp.float32),
        "depth_bias": normal_values(arg_keys[2], (CHANNELS,), 0.5, 3.0, jnp.float32),
        "reduce_weight": normal_values(arg_keys[3], (CHANNELS, REDUCED), CHANNELS ** -0.5, 0.21875),
        "reduce_bias": normal_values(arg_keys[4], (REDUCED,), 0.5, 3.0, jnp.float32),
        "class_weight": normal_values(arg_keys[5], (CLASSES, REDUCED, REDUCED), REDUCED ** -0.5, 0.375),
        "class_bias": normal_values(arg_keys[6], (CLASSES,), 1.0, 4.0, jnp.float32),
        "labels": with_ends(jax.random.randint(arg_keys[7], (IMAGES,), 0, CLASSES), jax.random.fold_in(arg_keys[7], 1), 0, CLASSES - 1).astype(jnp.int32),
    }


epsilon = 1e-05
loss_scale = 64.0
highest = lax.Precision.HIGHEST

def matrix_root(sigma):
    identity = jnp.eye(sigma.shape[0], dtype=sigma.dtype)
    trace_value = jnp.trace(sigma) + epsilon
    current = sigma / trace_value
    inverse = identity
    for iteration in range(NEWTON_STEPS):
        factor = 0.5 * (3.0 * identity - jnp.dot(inverse, current, precision=highest))
        current = jnp.dot(current, factor, precision=highest)
        inverse = jnp.dot(factor, inverse, precision=highest)
    return jnp.sqrt(trace_value) * current

def taps_conv(padded, tile_rows, tile_cols, depth_weight, depth_bias):
    total = jnp.zeros((tile_rows, tile_cols, padded.shape[2]), depth_weight.dtype) + depth_bias
    for row_tap in range(KERNEL):
        for col_tap in range(KERNEL):
            window = padded[row_tap:row_tap + tile_rows, col_tap:col_tap + tile_cols, :]
            total = total + window.astype(depth_weight.dtype) * depth_weight[row_tap, col_tap]
    return total.astype(jnp.bfloat16)

def forward(flat_conv, reduce_weight, reduce_bias):
    before = jnp.dot(flat_conv, reduce_weight, preferred_element_type=jnp.float32) + reduce_bias
    return (before, jax.nn.silu(before).astype(jnp.bfloat16))

def local_front(image, depth_weight, depth_bias, reduce_weight, reduce_bias):
    half = KERNEL // 2
    padded = jnp.pad(image, ((half, half), (half, half), (0, 0)))
    conv_out = taps_conv(padded, image.shape[0], image.shape[1], depth_weight, depth_bias)
    flat_conv = conv_out.reshape(-1, conv_out.shape[2])
    before, feat = forward(flat_conv, reduce_weight, reduce_bias)
    return (padded, flat_conv, before, feat)

def head(gram, colsum, label, class_weight, class_bias, count, image_count):
    mean_vec = colsum / count
    sigma = gram / count - jnp.outer(mean_vec, mean_vec)
    root, pullback = jax.vjp(matrix_root, sigma)
    weight_full = class_weight.astype(root.dtype)
    logits = jnp.einsum('kij,ij->k', weight_full, root, precision=highest) + class_bias
    onehot = (jnp.arange(logits.shape[0], dtype=jnp.int32) == label).astype(root.dtype)
    loss_part = jnp.sum(jax.nn.softplus(logits)) - jnp.sum(onehot * logits)
    logit_grad = loss_scale * (jax.nn.sigmoid(logits) - onehot) / image_count
    root_grad = jnp.einsum('k,kij->ij', logit_grad, weight_full, precision=highest)
    sigma_grad = pullback(root_grad)[0]
    symmetric = ((sigma_grad + sigma_grad.T) / count).astype(jnp.bfloat16)
    return (loss_part, logit_grad, root, symmetric, mean_vec)

def local_back(padded, flat_conv, before, feat, symmetric, mean_vec, reduce_weight, tile_rows, tile_cols):
    mean_term = jnp.dot(mean_vec, symmetric.astype(mean_vec.dtype), precision=highest)
    feat_grad = jnp.dot(feat, symmetric, preferred_element_type=jnp.float32) - mean_term
    gate = jax.nn.sigmoid(before)
    pre_grad = (feat_grad * gate * (1.0 + before * (1.0 - gate))).astype(jnp.bfloat16)
    weight_grad = lax.dot_general(flat_conv, pre_grad, (((0,), (0,)), ((), ())), preferred_element_type=jnp.float32)
    bias_grad = lax.optimization_barrier(jnp.sum(pre_grad.astype(jnp.float32), axis=0))
    conv_grad = lax.dot_general(pre_grad, reduce_weight, (((1,), (1,)), ((), ())), preferred_element_type=jnp.float32)
    conv_grad = conv_grad.astype(jnp.bfloat16).reshape(tile_rows, tile_cols, -1)
    depth_rows = []
    for row_tap in range(KERNEL):
        depth_cols = []
        for col_tap in range(KERNEL):
            window = padded[row_tap:row_tap + tile_rows, col_tap:col_tap + tile_cols, :]
            depth_cols.append(lax.optimization_barrier(jnp.sum(window.astype(jnp.float32) * conv_grad.astype(jnp.float32), axis=(0, 1))))
        depth_rows.append(jnp.stack(depth_cols))
    depth_grad = jnp.stack(depth_rows)
    depth_bias_grad = lax.optimization_barrier(jnp.sum(conv_grad.astype(jnp.float32), axis=(0, 1)))
    return (weight_grad, bias_grad, depth_grad, depth_bias_grad)

def reference(features, depth_weight, depth_bias, reduce_weight, reduce_bias, class_weight, class_bias, labels):
    count = ROWS_ALL * COLS_ALL

    def first_pass(image):
        padded, flat_conv, before, feat = local_front(image, depth_weight, depth_bias, reduce_weight, reduce_bias)
        gram = lax.dot_general(feat, feat, (((0,), (0,)), ((), ())), preferred_element_type=jnp.float32)
        colsum = lax.optimization_barrier(jnp.sum(feat.astype(jnp.float32), axis=0))
        return (gram, colsum)
    grams, colsums = lax.map(first_pass, features)

    def head_one(packed):
        return head(packed[0], packed[1], packed[2], class_weight, class_bias, count, IMAGES)
    loss_parts, logit_grads, roots, symmetrics, mean_vecs = lax.map(head_one, (grams, colsums, labels))

    def second_pass(packed):
        image, symmetric, mean_vec = packed
        padded, flat_conv, before, feat = local_front(image, depth_weight, depth_bias, reduce_weight, reduce_bias)
        return local_back(padded, flat_conv, before, feat, symmetric, mean_vec, reduce_weight, ROWS_ALL, COLS_ALL)
    weight_grads, bias_grads, depth_grads, depth_bias_grads = lax.map(second_pass, (features, symmetrics, mean_vecs))
    loss = jnp.sum(loss_parts) / IMAGES
    class_weight_grad = jnp.einsum('mk,mij->kij', logit_grads, roots, precision=highest)
    class_bias_grad = lax.optimization_barrier(jnp.sum(logit_grads, axis=0))
    return (loss, lax.optimization_barrier(jnp.sum(depth_grads, axis=0)), lax.optimization_barrier(jnp.sum(depth_bias_grads, axis=0)), lax.optimization_barrier(jnp.sum(weight_grads, axis=0)), lax.optimization_barrier(jnp.sum(bias_grads, axis=0)), class_weight_grad, class_bias_grad)
```

```python
import functools

import jax
import jax.numpy as jnp
from jax import lax
from jax.experimental import pallas as pl
from jax.experimental.pallas import tpu as pltpu
from jax.sharding import PartitionSpec as P

MESH = pl.DeviceIdType.MESH
KERNEL = 7
NEWTON_STEPS = 5
ROWS = 16
COLS = 64
TILES = 6
CHANNELS = 768
REDUCED = 256
CLASSES = 10
PITCH = 80
BLOCK0 = 8
epsilon = 1e-05
loss_scale = 64.0
f32 = jnp.float32
bf16 = jnp.bfloat16


def lanes_of(tile):
    return pl.ds(pl.multiple_of(tile * 128, 128), 128)


def split(value):
    high = value.astype(bf16)
    return high, (value - high.astype(f32)).astype(bf16)


def products(*pairs):
    left, right = [], []
    for (a_high, a_low), (b_high, b_low) in pairs:
        left += [a_low, a_high, a_high]
        right += [b_high, b_low, b_high]
    return jnp.dot(
        jnp.concatenate(left, axis=1), jnp.concatenate(right, axis=0), preferred_element_type=f32
    )


def main_kernel(
    x_ref, w_ref, db_ref, rw_ref, rb_ref, cw_ref, cb_ref, lab_ref,
    wg_out, dg_out, root_out, small_out,
    image, conv32, conv, before, feat, pre, cgrad,
    csend, ksend, hrow, hcol, hcor,
    gram, grecv, gfull, colsum, crecv,
    ys, zs, ts, sym, mean_term,
    wsend, wrecv, wx, depth, dsend, drecv, dx,
    halo_send, halo_recv, g_send, g_recv, c_send, c_recv, a_send, a_recv,
    x_send, x_recv, s_send, s_recv, w_send, w_recv, wx_send, wx_recv, wa_send, wa_recv,
    d_send, d_recv, dx_send, dx_recv, da_send, da_recv,
):
    idp, iz, iy = lax.axis_index("dp"), lax.axis_index("sy"), lax.axis_index("sx")
    images = 8
    count = ROWS * COLS * 16
    me = iz * 4 + iy

    def plane(offset, sign=1):
        dz, dy = divmod(offset, 4)
        pz, py = lax.rem(iz + 4 + sign * dz, 4), lax.rem(iy + 4 + sign * dy, 4)
        return (idp, pz, py), pz * 4 + py

    def line(offset, sign=1):
        other = lax.rem(idp + 8 + sign * offset, 8)
        return (other, iz, iy), other

    def send(src, dst, send_sem, recv_sem, device):
        copy = pltpu.make_async_remote_copy(
            src_ref=src, dst_ref=dst, send_sem=send_sem, recv_sem=recv_sem,
            device_id=device, device_id_type=MESH,
        )
        return copy

    barrier = pltpu.get_barrier_semaphore()
    for offset in range(1, 16):
        pl.semaphore_signal(barrier, inc=1, device_id=plane(offset)[0], device_id_type=MESH)
    for offset in range(1, 8):
        pl.semaphore_signal(barrier, inc=1, device_id=line(offset)[0], device_id_type=MESH)

    def fill(tile, carry):
        lanes = lanes_of(tile)
        for row in range(ROWS):
            start = (row + 3) * PITCH + BLOCK0
            image[tile, start : start + COLS, :] = x_ref[0, row, :, lanes].astype(f32)
        for side in range(2):
            for col in range(3):
                at = BLOCK0 + col + (0 if side == 0 else COLS - 3)
                strip = image[tile, pl.ds(3 * PITCH + at, ROWS, stride=PITCH), :]
                csend[side, col, :, lanes] = strip.astype(bf16)
                for end in range(2):
                    ksend[end * 2 + side, col, :, lanes] = strip[8 * end : 8 * end + 8].astype(bf16)
        return carry

    lax.fori_loop(0, TILES, fill, 0)
    pl.semaphore_wait(barrier, 22)

    up, down = lax.rem(iz + 3, 4), lax.rem(iz + 1, 4)
    left, right = lax.rem(iy + 3, 4), lax.rem(iy + 1, 4)
    halo = [
        (x_ref.at[0, pl.ds(ROWS - 3, 3)], hrow.at[0], (idp, down, iy)),
        (x_ref.at[0, pl.ds(0, 3)], hrow.at[1], (idp, up, iy)),
        (csend.at[1], hcol.at[0], (idp, iz, right)),
        (csend.at[0], hcol.at[1], (idp, iz, left)),
        (ksend.at[3], hcor.at[0], (idp, down, right)),
        (ksend.at[2], hcor.at[1], (idp, down, left)),
        (ksend.at[1], hcor.at[2], (idp, up, right)),
        (ksend.at[0], hcor.at[3], (idp, up, left)),
    ]
    copies = [
        send(src, dst, halo_send.at[i], halo_recv.at[i], device)
        for i, (src, dst, device) in enumerate(halo)
    ]
    for copy in copies:
        copy.start()
    for copy in copies:
        copy.wait()
    has_up, has_down, has_left, has_right = iz > 0, iz < 3, iy > 0, iy < 3

    def edges(tile, carry):
        lanes = lanes_of(tile)
        for end in range(2):
            has_row = (has_up, has_down)[end]
            for row in range(3):
                start = (row + 19 * end) * PITCH + BLOCK0
                strip = hrow[end, row, :, lanes].astype(f32)
                image[tile, start : start + COLS, :] = jnp.where(has_row, strip, 0.0)
        for side in range(2):
            has_col = (has_left, has_right)[side]
            for col in range(3):
                at = BLOCK0 - 3 + col + side * (COLS + 3)
                strip = hcol[side, col, :, lanes].astype(f32)
                image[tile, pl.ds(3 * PITCH + at, ROWS, stride=PITCH), :] = jnp.where(
                    has_col, strip, 0.0
                )
                for end in range(2):
                    has_both = jnp.logical_and((has_up, has_down)[end], has_col)
                    strip = hcor[end * 2 + side, col, :, lanes].astype(f32)
                    strip = jnp.where(has_both, strip, 0.0)
                    strip = strip[5:8] if end == 0 else strip[0:3]
                    image[tile, pl.ds(19 * end * PITCH + at, 3, stride=PITCH), :] = strip
        return carry

    lax.fori_loop(0, TILES, edges, 0)

    def conv_tile(tile, carry):
        lanes = lanes_of(tile)

        def group(jg, inner):
            acc = [jnp.broadcast_to(db_ref[:, lanes], (8, 128))] * ROWS
            for b in range(KERNEL):
                taps = [jnp.broadcast_to(w_ref[a, pl.ds(b, 1), lanes], (8, 128)) for a in range(KERNEL)]
                for row in range(ROWS + 6):
                    x = image[tile, pl.ds(jg * 8 + (row * PITCH + BLOCK0 - 3 + b), 8), :]
                    for a in range(KERNEL):
                        if 0 <= row - a < ROWS:
                            acc[row - a] = acc[row - a] + x * taps[a]
            for row in range(ROWS):
                conv32[pl.ds(pl.multiple_of(jg * 8 + row * COLS, 8), 8), :] = acc[row]
            return inner

        lax.fori_loop(0, COLS // 8, group, 0)
        conv[:, lanes] = conv32[...].astype(bf16)
        return carry

    lax.fori_loop(0, TILES, conv_tile, 0)

    colsum[...] = jnp.zeros_like(colsum)
    for part in range(4):
        rows = pl.ds(part * 256, 256)
        value = jnp.dot(conv[rows, :], rw_ref[...], preferred_element_type=f32) + rb_ref[...]
        before[rows, :] = value
        active = (value / (1.0 + jnp.exp(-value))).astype(bf16)
        feat[rows, :] = active
        colsum[...] += jnp.sum(active.astype(f32), axis=0, keepdims=True)
    total = lax.dot_general(
        feat[...], feat[...], (((0,), (0,)), ((), ())), preferred_element_type=f32
    )
    gram[...] = total.reshape(16, 16, REDUCED)
    crecv[me] = colsum[...]

    copies = []
    for offset in range(1, 16):
        device, index = plane(offset)
        copies.append(send(gram.at[index], grecv.at[offset], g_send.at[offset], g_recv.at[offset], device))
        copies.append(send(colsum, crecv.at[me], c_send.at[offset], c_recv.at[offset], device))
    for copy in copies:
        copy.start()
    for offset in range(1, 16):
        _, source = plane(offset, -1)
        send(gram.at[0], grecv.at[offset], g_send.at[offset], g_recv.at[offset], plane(offset)[0]).wait_recv()
        send(colsum, crecv.at[source], c_send.at[offset], c_recv.at[offset], plane(offset)[0]).wait_recv()
    mine = gram[me]
    for offset in range(1, 16):
        mine = mine + grecv[offset]
    gfull[me] = mine
    gathers = []
    for offset in range(1, 16):
        device, _ = plane(offset)
        gathers.append(send(gfull.at[me], gfull.at[me], a_send.at[offset], a_recv.at[offset], device))
    for copy in gathers:
        copy.start()
    for copy in copies:
        copy.wait_send()
    for offset in range(1, 16):
        _, source = plane(offset, -1)
        send(gfull.at[source], gfull.at[source], a_send.at[offset], a_recv.at[offset], plane(offset)[0]).wait_recv()
    for copy in gathers:
        copy.wait_send()

    mean = crecv[0]
    for index in range(1, 16):
        mean = mean + crecv[index]
    mean = mean * (1.0 / count)
    wide = jnp.broadcast_to(mean, (REDUCED, REDUCED))
    sigma = gfull[...].reshape(REDUCED, REDUCED) * (1.0 / count) - wide.T * wide
    row_id = lax.broadcasted_iota(jnp.int32, (REDUCED, REDUCED), 0)
    col_id = lax.broadcasted_iota(jnp.int32, (REDUCED, REDUCED), 1)
    diagonal = row_id == col_id
    identity15 = jnp.where(diagonal, 1.5, 0.0)
    trace = jnp.sum(
        jnp.sum(jnp.where(diagonal, sigma, 0.0), axis=0, keepdims=True), axis=1, keepdims=True
    ) + epsilon
    start = sigma / trace

    def keep(ref, step, value):
        high, low = split(value)
        ref[step, 0] = high
        ref[step, 1] = low

    def kept(ref, step):
        return ref[step, 0], ref[step, 1]

    keep(ys, 0, start)
    keep(ts, 0, identity15 - 0.5 * start)
    keep(ys, 1, products((kept(ys, 0), kept(ts, 0))))
    for step in range(1, NEWTON_STEPS):
        inverse = kept(ts, 0) if step == 1 else kept(zs, step)
        factor = identity15 - 0.5 * products((inverse, kept(ys, step)))
        keep(ts, step, factor)
        if step < NEWTON_STEPS - 1:
            keep(zs, step + 1, products((kept(ts, step), inverse)))
            keep(ys, step + 1, products((kept(ys, step), kept(ts, step))))
    last = products((kept(ys, NEWTON_STEPS - 1), kept(ts, NEWTON_STEPS - 1)))
    root_scale = jnp.sqrt(trace)
    root = root_scale * last
    root_out[idp] = root.astype(bf16)

    class_id = lax.broadcasted_iota(jnp.int32, (1, CLASSES), 1)
    logits = cb_ref[...]
    for k in range(CLASSES):
        weighted = jnp.sum(cw_ref[k].astype(f32) * root, axis=0, keepdims=True)
        logits = logits + jnp.where(class_id == k, jnp.sum(weighted, axis=1, keepdims=True), 0.0)
    onehot = jnp.where(class_id == lab_ref[0], 1.0, 0.0)
    softplus = jnp.maximum(logits, 0.0) + jnp.log(1.0 + jnp.exp(-jnp.abs(logits)))
    loss = jnp.sum(softplus - onehot * logits, axis=1, keepdims=True)
    logit_grad = (loss_scale / images) * (1.0 / (1.0 + jnp.exp(-logits)) - onehot)
    small_out[idp] = jnp.zeros((8, 128), f32)
    small_out[idp, 0:1, 0:CLASSES] = logit_grad
    small_out[idp, 1:2, :] = jnp.broadcast_to(loss, (1, 128))
    roots, smalls = [], []
    for offset in range(1, 8):
        device, _ = line(offset)
        roots.append(send(root_out.at[idp], root_out.at[idp], x_send.at[offset], x_recv.at[offset], device))
        smalls.append(send(small_out.at[idp], small_out.at[idp], s_send.at[offset], s_recv.at[offset], device))
    for copy in smalls + roots:
        copy.start()

    root_grad = jnp.zeros((REDUCED, REDUCED), f32)
    for k in range(CLASSES):
        root_grad = root_grad + logit_grad[:, k : k + 1] * cw_ref[k].astype(f32)
    root_grad = 0.5 * (root_grad + root_grad.T)
    trace_grad = jnp.sum(jnp.sum(root_grad * last, axis=0, keepdims=True), axis=1, keepdims=True)
    trace_grad = trace_grad * 0.5 / root_scale
    seed = root_scale * root_grad
    d_y = split(seed)
    d_t = split(-0.5 * seed)
    d_z = d_t
    d_y = split(products((d_y, kept(ts, 0)), (kept(ys, 0), d_t)))
    for step in range(1, NEWTON_STEPS):
        inverse = kept(ts, 0) if step == 1 else kept(zs, step)
        d_t = split(-0.5 * products((d_z, kept(ys, step)), (inverse, d_y)))
        if step < NEWTON_STEPS - 1:
            d_z = split(products((d_t, inverse), (kept(ts, step), d_z)))
            d_y = split(products((d_y, kept(ts, step)), (kept(ys, step), d_t)))
    start_grad = products((d_y, kept(ts, NEWTON_STEPS - 1)), (kept(ys, NEWTON_STEPS - 1), d_t))
    start_grad = 0.5 * (start_grad + start_grad.T)
    start_value = ys[0, 0].astype(f32) + ys[0, 1].astype(f32)
    inner = jnp.sum(jnp.sum(start_grad * start_value, axis=0, keepdims=True), axis=1, keepdims=True)
    trace_grad = trace_grad - inner / trace
    sigma_grad = start_grad / trace + jnp.where(diagonal, trace_grad, 0.0)
    symmetric = (sigma_grad * (2.0 / count)).astype(bf16)
    sym[...] = symmetric
    mean_high, mean_low = split(jnp.broadcast_to(mean, (8, REDUCED)))
    mean_term[...] = jnp.dot(mean_high, symmetric, preferred_element_type=f32) + jnp.dot(
        mean_low, symmetric, preferred_element_type=f32
    )

    depth[...] = jnp.zeros_like(depth)
    bias_grad = jnp.zeros((1, REDUCED), f32)
    for part in range(4):
        rows = pl.ds(part * 256, 256)
        feat_grad = jnp.dot(feat[rows, :], sym[...], preferred_element_type=f32) - mean_term[0:1, :]
        value = before[rows, :]
        gate = 1.0 / (1.0 + jnp.exp(-value))
        pre_grad = (feat_grad * gate * (1.0 + value * (1.0 - gate))).astype(bf16)
        pre[rows, :] = pre_grad
        bias_grad = bias_grad + jnp.sum(pre_grad.astype(f32), axis=0, keepdims=True)
        conv_grad = lax.dot_general(
            pre_grad, rw_ref[...], (((1,), (1,)), ((), ())), preferred_element_type=f32
        ).astype(bf16).astype(f32)
        for tile in range(TILES):
            cgrad[tile, rows, :] = conv_grad[:, tile * 128 : tile * 128 + 128]
    weight_grad = lax.dot_general(
        conv[...], pre[...], (((0,), (0,)), ((), ())), preferred_element_type=f32
    )
    wsend[...] = weight_grad.astype(bf16).reshape(16, 48, REDUCED)
    depth[0, 15:16, :] = bias_grad[:, 0:128]
    depth[1, 15:16, :] = bias_grad[:, 128:256]

    w_copies = []
    for offset in range(1, 16):
        device, index = plane(offset)
        w_copies.append(send(wsend.at[index], wrecv.at[offset], w_send.at[offset], w_recv.at[offset], device))
    for copy in w_copies:
        copy.start()

    def depth_tile(tile, carry):
        for b in range(KERNEL):

            def group(jg, acc):
                acc = list(acc)
                grads = [
                    cgrad[tile, pl.ds(pl.multiple_of(jg * 8 + row * COLS, 8), 8), :]
                    for row in range(ROWS)
                ]
                for row in range(ROWS + 6):
                    x = image[tile, pl.ds(jg * 8 + (row * PITCH + BLOCK0 - 3 + b), 8), :]
                    for a in range(KERNEL):
                        if 0 <= row - a < ROWS:
                            acc[a] = acc[a] + x * grads[row - a]
                if b == 0:
                    partial = grads[0]
                    for row in range(1, ROWS):
                        partial = partial + grads[row]
                    acc[KERNEL] = acc[KERNEL] + partial
                return tuple(acc)

            zero = jnp.zeros((8, 128), f32)
            sums = lax.fori_loop(0, COLS // 8, group, (zero,) * (KERNEL + (b == 0)))
            for a in range(KERNEL):
                depth[tile, a * 8 + b : a * 8 + b + 1, :] = jnp.sum(sums[a], axis=0, keepdims=True)
            if b == 0:
                depth[tile, 7:8, :] = jnp.sum(sums[KERNEL], axis=0, keepdims=True)
        return carry

    lax.fori_loop(0, 3, depth_tile, 0)

    for copy in w_copies:
        copy.wait()
    w_sum = wsend[me].astype(f32)
    for offset in range(1, 16):
        w_sum = w_sum + wrecv[offset].astype(f32)
    wx[idp] = w_sum.astype(bf16)
    wx_copies = []
    for offset in range(1, 8):
        device, _ = line(offset)
        wx_copies.append(send(wx.at[idp], wx.at[idp], wx_send.at[offset], wx_recv.at[offset], device))
    for copy in wx_copies:
        copy.start()
    lax.fori_loop(3, 5, depth_tile, 0)
    for offset in range(1, 8):
        _, source = line(offset, -1)
        send(wx.at[source], wx.at[source], wx_send.at[offset], wx_recv.at[offset], line(offset)[0]).wait_recv()
    for copy in wx_copies:
        copy.wait_send()
    w_sum = wx[0].astype(f32)
    for index in range(1, 8):
        w_sum = w_sum + wx[index].astype(f32)
    wg_out[me] = w_sum.astype(bf16)
    wa_copies = []
    for offset in range(1, 16):
        device, _ = plane(offset)
        wa_copies.append(send(wg_out.at[me], wg_out.at[me], wa_send.at[offset], wa_recv.at[offset], device))
    for copy in wa_copies:
        copy.start()
    lax.fori_loop(5, 6, depth_tile, 0)

    for group8 in range(8):
        for half in range(2):
            for third in range(3):
                dsend[group8 * 2 + half, :, third * 128 : third * 128 + 128] = depth[
                    half * 3 + third, group8 * 8 : group8 * 8 + 8, :
                ].astype(bf16)
    d_copies = []
    for offset in range(1, 16):
        device, index = plane(offset)
        d_copies.append(send(dsend.at[index], drecv.at[offset], d_send.at[offset], d_recv.at[offset], device))
    for copy in d_copies:
        copy.start()
    for copy in d_copies:
        copy.wait()
    d_sum = dsend[me].astype(f32)
    for offset in range(1, 16):
        d_sum = d_sum + drecv[offset].astype(f32)
    dx[idp] = d_sum.astype(bf16)
    dx_copies = []
    for offset in range(1, 8):
        device, _ = line(offset)
        dx_copies.append(send(dx.at[idp], dx.at[idp], dx_send.at[offset], dx_recv.at[offset], device))
    for copy in dx_copies:
        copy.start()
    for offset in range(1, 8):
        _, source = line(offset, -1)
        send(dx.at[source], dx.at[source], dx_send.at[offset], dx_recv.at[offset], line(offset)[0]).wait_recv()
    for copy in dx_copies:
        copy.wait_send()
    d_sum = dx[0].astype(f32)
    for index in range(1, 8):
        d_sum = d_sum + dx[index].astype(f32)
    dg_out[me] = d_sum.astype(bf16)
    da_copies = []
    for offset in range(1, 16):
        device, _ = plane(offset)
        da_copies.append(send(dg_out.at[me], dg_out.at[me], da_send.at[offset], da_recv.at[offset], device))
    for copy in da_copies:
        copy.start()
    for offset in range(1, 16):
        _, source = plane(offset, -1)
        device = plane(offset)[0]
        send(wg_out.at[source], wg_out.at[source], wa_send.at[offset], wa_recv.at[offset], device).wait_recv()
        send(dg_out.at[source], dg_out.at[source], da_send.at[offset], da_recv.at[offset], device).wait_recv()
    for offset in range(1, 8):
        _, source = line(offset, -1)
        device = line(offset)[0]
        send(root_out.at[source], root_out.at[source], x_send.at[offset], x_recv.at[offset], device).wait_recv()
        send(small_out.at[source], small_out.at[source], s_send.at[offset], s_recv.at[offset], device).wait_recv()
    for copy in wa_copies + da_copies + roots + smalls:
        copy.wait_send()


def finish_kernel(wg, dg, roots, smalls, loss, depth_grad, depth_bias, weight, bias, class_weight, class_bias):
    k = pl.program_id(0)
    lane = lax.broadcasted_iota(jnp.int32, (1, 128), 1)
    total = jnp.zeros((REDUCED, REDUCED), f32)
    for image in range(8):
        factor = jnp.sum(jnp.where(lane == k, smalls[image, 0:1, :], 0.0), axis=1, keepdims=True)
        total = total + factor * roots[image].astype(f32)
    class_weight[0] = total

    @pl.when(k == 0)
    def _():
        weight[...] = wg[...].astype(f32).reshape(CHANNELS, REDUCED)
        for half in range(2):
            lanes = slice(half * 384, half * 384 + 384)
            for a in range(KERNEL):
                depth_grad[a, :, lanes] = dg[a * 2 + half, 0:7, :].astype(f32)
            depth_bias[:, lanes] = dg[half, 7:8, :].astype(f32)
        bias[:, 0:128] = dg[2, 7:8, 0:128].astype(f32)
        bias[:, 128:256] = dg[2, 7:8, 128:256].astype(f32)
        small = smalls[0]
        for image in range(1, 8):
            small = small + smalls[image]
        class_bias[...] = small[0:1, 0:CLASSES]
        loss[...] = small[1:2, 0:1] * (1.0 / 8)


def body(
    features, depth_weight, depth_bias, reduce_weight, reduce_bias, class_weight, class_bias, labels
):
    vmem = pl.BlockSpec(memory_space=pltpu.VMEM)
    smem = pl.BlockSpec(memory_space=pltpu.SMEM)
    dma = pltpu.SemaphoreType.DMA
    scratch = [
        pltpu.VMEM((TILES, (ROWS + 6) * PITCH, 128), f32),
        pltpu.VMEM((ROWS * COLS, 128), f32),
        pltpu.VMEM((ROWS * COLS, CHANNELS), bf16),
        pltpu.VMEM((ROWS * COLS, REDUCED), f32),
        pltpu.VMEM((ROWS * COLS, REDUCED), bf16),
        pltpu.VMEM((ROWS * COLS, REDUCED), bf16),
        pltpu.VMEM((TILES, ROWS * COLS, 128), f32),
        pltpu.VMEM((2, 3, 16, CHANNELS), bf16),
        pltpu.VMEM((4, 3, 8, CHANNELS), bf16),
        pltpu.VMEM((2, 3, COLS, CHANNELS), bf16),
        pltpu.VMEM((2, 3, 16, CHANNELS), bf16),
        pltpu.VMEM((4, 3, 8, CHANNELS), bf16),
        pltpu.VMEM((16, 16, REDUCED), f32),
        pltpu.VMEM((16, 16, REDUCED), f32),
        pltpu.VMEM((16, 16, REDUCED), f32),
        pltpu.VMEM((1, REDUCED), f32),
        pltpu.VMEM((16, 1, REDUCED), f32),
        pltpu.VMEM((NEWTON_STEPS, 2, REDUCED, REDUCED), bf16),
        pltpu.VMEM((NEWTON_STEPS, 2, REDUCED, REDUCED), bf16),
        pltpu.VMEM((NEWTON_STEPS, 2, REDUCED, REDUCED), bf16),
        pltpu.VMEM((REDUCED, REDUCED), bf16),
        pltpu.VMEM((8, REDUCED), f32),
        pltpu.VMEM((16, 48, REDUCED), bf16),
        pltpu.VMEM((16, 48, REDUCED), bf16),
        pltpu.VMEM((8, 48, REDUCED), bf16),
        pltpu.VMEM((TILES, 64, 128), f32),
        pltpu.VMEM((16, 8, 384), bf16),
        pltpu.VMEM((16, 8, 384), bf16),
        pltpu.VMEM((8, 8, 384), bf16),
        dma((8,)), dma((8,)),
        dma((16,)), dma((16,)), dma((16,)), dma((16,)), dma((16,)), dma((16,)),
        dma((8,)), dma((8,)), dma((8,)), dma((8,)),
        dma((16,)), dma((16,)), dma((8,)), dma((8,)), dma((16,)), dma((16,)),
        dma((16,)), dma((16,)), dma((8,)), dma((8,)), dma((16,)), dma((16,)),
    ]
    wg, dg, roots, smalls = pl.pallas_call(
        main_kernel,
        out_shape=(
            jax.ShapeDtypeStruct((16, 48, REDUCED), bf16),
            jax.ShapeDtypeStruct((16, 8, 384), bf16),
            jax.ShapeDtypeStruct((8, REDUCED, REDUCED), bf16),
            jax.ShapeDtypeStruct((8, 8, 128), f32),
        ),
        in_specs=[vmem] * 7 + [smem],
        out_specs=(vmem,) * 4,
        scratch_shapes=scratch,
        compiler_params=pltpu.CompilerParams(
            collective_id=0, has_side_effects=True, vmem_limit_bytes=50 << 20
        ),
        name="pooling_step",
    )(
        features, depth_weight, depth_bias.reshape(1, CHANNELS), reduce_weight,
        reduce_bias.reshape(1, REDUCED), class_weight, class_bias.reshape(1, CLASSES), labels,
    )
    whole = lambda *shape: pl.BlockSpec(shape, lambda k: (0,) * len(shape))
    loss, depth_grad, depth_bias_grad, weight_grad, bias_grad, class_grad, class_bias_grad = pl.pallas_call(
        finish_kernel,
        grid=(CLASSES,),
        out_shape=(
            jax.ShapeDtypeStruct((1, 1), f32),
            jax.ShapeDtypeStruct((KERNEL, KERNEL, CHANNELS), f32),
            jax.ShapeDtypeStruct((1, CHANNELS), f32),
            jax.ShapeDtypeStruct((CHANNELS, REDUCED), f32),
            jax.ShapeDtypeStruct((1, REDUCED), f32),
            jax.ShapeDtypeStruct((CLASSES, REDUCED, REDUCED), f32),
            jax.ShapeDtypeStruct((1, CLASSES), f32),
        ),
        in_specs=[whole(16, 48, REDUCED), whole(16, 8, 384), whole(8, REDUCED, REDUCED), whole(8, 8, 128)],
        out_specs=(
            whole(1, 1), whole(KERNEL, KERNEL, CHANNELS), whole(1, CHANNELS), whole(CHANNELS, REDUCED),
            whole(1, REDUCED), pl.BlockSpec((1, REDUCED, REDUCED), lambda k: (k, 0, 0)), whole(1, CLASSES),
        ),
        compiler_params=pltpu.CompilerParams(vmem_limit_bytes=24 << 20),
        name="outputs",
    )(wg, dg, roots, smalls)
    return (
        loss.reshape(()), depth_grad, depth_bias_grad.reshape(CHANNELS), weight_grad,
        bias_grad.reshape(REDUCED), class_grad, class_bias_grad.reshape(CLASSES),
    )


def solution(mesh):
    placed = (P("dp", "sy", "sx", None), P(), P(), P(), P(), P(), P(), P("dp"))
    return jax.shard_map(
        body,
        mesh=mesh,
        in_specs=placed,
        out_specs=(P(), P(), P(), P(), P(), P(), P()),
        check_vma=False,
    )
```

```python
import functools

import jax
import jax.numpy as jnp
from jax import lax
from jax.experimental import pallas as pl
from jax.experimental.pallas import tpu as pltpu
from jax.sharding import PartitionSpec as P

MESH = pl.DeviceIdType.MESH
KERNEL = 7
NEWTON_STEPS = 5
ROWS = 16
COLS = 64
TILES = 6
CHANNELS = 768
REDUCED = 256
CLASSES = 10
PITCH = 80
BLOCK0 = 8
epsilon = 1e-05
loss_scale = 64.0
f32 = jnp.float32
bf16 = jnp.bfloat16


def lanes_of(tile):
    return pl.ds(pl.multiple_of(tile * 128, 128), 128)


def split(value):
    high = value.astype(bf16)
    return high, (value - high.astype(f32)).astype(bf16)


def products(*pairs):
    left, right = [], []
    for (a_high, a_low), (b_high, b_low) in pairs:
        left += [a_low, a_high, a_high]
        right += [b_high, b_low, b_high]
    return jnp.dot(
        jnp.concatenate(left, axis=1), jnp.concatenate(right, axis=0), preferred_element_type=f32
    )


def main_kernel(
    x_hbm, w_hbm, db_hbm, rw_hbm, rb_hbm, cw_hbm, cb_hbm, lab_ref,
    wg_out, dg_out, small_out, class_hbm,
    class_out,
    x_ref, w_ref, db_ref, rw_ref, rb_ref, cw_ref, cb_ref, root_out, factors,
    image, border, conv, before, feat, pre, cgrad,
    csend, ksend, hrow, hcol, hcor,
    gram, grecv, gfull, colsum, crecv,
    ys, zs, ts, sym, mean_term,
    wsend, wrecv, wx, depth, dsend, drecv, dx,
    in_sem, out_sem, halo_send, halo_recv, g_send, g_recv, c_send, c_recv, a_send, a_recv,
    x_send, x_recv, s_send, s_recv, w_send, w_recv, wx_send, wx_recv, wa_send, wa_recv,
    d_send, d_recv, dx_send, dx_recv, da_send, da_recv,
):
    idp, iz, iy = lax.axis_index("dp"), lax.axis_index("sy"), lax.axis_index("sx")
    images = 8
    count = ROWS * COLS * 16
    me = iz * 4 + iy

    def plane(offset, sign=1):
        dz, dy = divmod(offset, 4)
        pz, py = lax.rem(iz + 4 + sign * dz, 4), lax.rem(iy + 4 + sign * dy, 4)
        return (idp, pz, py), pz * 4 + py

    def line(offset, sign=1):
        other = lax.rem(idp + 8 + sign * offset, 8)
        return (other, iz, iy), other

    def send(src, dst, send_sem, recv_sem, device):
        copy = pltpu.make_async_remote_copy(
            src_ref=src, dst_ref=dst, send_sem=send_sem, recv_sem=recv_sem,
            device_id=device, device_id_type=MESH,
        )
        return copy

    barrier = pltpu.get_barrier_semaphore()
    for offset in range(1, 16):
        pl.semaphore_signal(barrier, inc=1, device_id=plane(offset)[0], device_id_type=MESH)
    for offset in range(1, 8):
        pl.semaphore_signal(barrier, inc=1, device_id=line(offset)[0], device_id_type=MESH)

    loads = [
        pltpu.make_async_copy(src, dst, in_sem.at[i])
        for i, (src, dst) in enumerate([
            (x_hbm.at[0], x_ref), (w_hbm, w_ref), (db_hbm, db_ref), (rw_hbm, rw_ref),
            (rb_hbm, rb_ref), (cw_hbm, cw_ref), (cb_hbm, cb_ref),
        ])
    ]
    for load in loads:
        load.start()
    loads[0].wait()

    def fill(tile, carry):
        lanes = lanes_of(tile)
        blank = jnp.zeros((8, 128), f32)
        for row in range(ROWS):
            start = (row + 3) * PITCH + BLOCK0
            image[tile, start : start + COLS, :] = x_ref[row, :, lanes].astype(f32)
            image[tile, start - 8 : start, :] = blank
            image[tile, start + COLS : start + COLS + 8, :] = blank
            border[tile, row * 32 : row * 32 + 32, :] = jnp.zeros((32, 128), f32)
        for side in range(2):
            for col in range(3):
                at = BLOCK0 + col + (0 if side == 0 else COLS - 3)
                strip = image[tile, pl.ds(3 * PITCH + at, ROWS, stride=PITCH), :]
                csend[side, col, :, lanes] = strip.astype(bf16)
                for end in range(2):
                    ksend[end * 2 + side, col, :, lanes] = strip[8 * end : 8 * end + 8].astype(bf16)
        return carry

    lax.fori_loop(0, TILES, fill, 0)
    loads[1].wait()
    loads[2].wait()

    def taps_of(lanes, b):
        return [jnp.broadcast_to(w_ref[a, pl.ds(b, 1), lanes], (8, 128)) for a in range(KERNEL)]

    def accumulate(acc, x, row, taps):
        for a in range(KERNEL):
            if 0 <= row - a < ROWS:
                acc[row - a] = acc[row - a] + x * taps[a]

    def conv_tile(tile, carry):
        lanes = lanes_of(tile)

        def group(jg, inner):
            acc = [jnp.broadcast_to(db_ref[lanes].reshape(1, 128), (8, 128))] * ROWS
            for b in range(KERNEL):
                taps = taps_of(lanes, b)
                for row in range(3, ROWS + 3):
                    x = image[tile, pl.ds(jg * 8 + (row * PITCH + BLOCK0 - 3 + b), 8), :]
                    accumulate(acc, x, row, taps)
            for row in range(ROWS):
                cgrad[tile, pl.ds(pl.multiple_of(jg * 8 + row * COLS, 8), 8), :] = acc[row]
            return inner

        lax.fori_loop(0, COLS // 8, group, 0)
        return carry

    lax.fori_loop(0, 2, conv_tile, 0)
    pl.semaphore_wait(barrier, 22)

    up, down = lax.rem(iz + 3, 4), lax.rem(iz + 1, 4)
    left, right = lax.rem(iy + 3, 4), lax.rem(iy + 1, 4)
    halo = [
        (x_ref.at[pl.ds(ROWS - 3, 3)], hrow.at[0], (idp, down, iy)),
        (x_ref.at[pl.ds(0, 3)], hrow.at[1], (idp, up, iy)),
        (csend.at[1], hcol.at[0], (idp, iz, right)),
        (csend.at[0], hcol.at[1], (idp, iz, left)),
        (ksend.at[3], hcor.at[0], (idp, down, right)),
        (ksend.at[2], hcor.at[1], (idp, down, left)),
        (ksend.at[1], hcor.at[2], (idp, up, right)),
        (ksend.at[0], hcor.at[3], (idp, up, left)),
    ]
    copies = [
        send(src, dst, halo_send.at[i], halo_recv.at[i], device)
        for i, (src, dst, device) in enumerate(halo)
    ]
    for copy in copies:
        copy.start()
    lax.fori_loop(2, TILES, conv_tile, 0)
    for copy in copies:
        copy.wait()
    has_up, has_down, has_left, has_right = iz > 0, iz < 3, iy > 0, iy < 3

    def edges(tile, carry):
        lanes = lanes_of(tile)
        for end in range(2):
            has_row = (has_up, has_down)[end]
            for row in range(3):
                start = (row + 19 * end) * PITCH + BLOCK0
                strip = hrow[end, row, :, lanes].astype(f32)
                image[tile, start : start + COLS, :] = jnp.where(has_row, strip, 0.0)
        for side in range(2):
            has_col = (has_left, has_right)[side]
            for col in range(3):
                at = BLOCK0 - 3 + col + side * (COLS + 3)
                strip = hcol[side, col, :, lanes].astype(f32)
                strip = jnp.where(has_col, strip, 0.0)
                image[tile, pl.ds(3 * PITCH + at, ROWS, stride=PITCH), :] = strip
                spot = 21 + col if side == 0 else 8 + col
                border[tile, pl.ds(spot, ROWS, stride=32), :] = strip
                for end in range(2):
                    has_both = jnp.logical_and((has_up, has_down)[end], has_col)
                    strip = hcor[end * 2 + side, col, :, lanes].astype(f32)
                    strip = jnp.where(has_both, strip, 0.0)
                    strip = strip[5:8] if end == 0 else strip[0:3]
                    image[tile, pl.ds(19 * end * PITCH + at, 3, stride=PITCH), :] = strip

        def load_rows(start, rows):
            return {
                row: cgrad[tile, pl.ds(pl.multiple_of(start + row * COLS, 8), 8), :] for row in rows
            }

        def store_rows(start, acc):
            for row, value in acc.items():
                cgrad[tile, pl.ds(pl.multiple_of(start + row * COLS, 8), 8), :] = value

        def group(jg, inner):
            acc = load_rows(jg * 8, (0, 1, 2, 13, 14, 15))
            for b in range(KERNEL):
                taps = taps_of(lanes, b)
                for row in (0, 1, 2, 19, 20, 21):
                    x = image[tile, pl.ds(jg * 8 + (row * PITCH + BLOCK0 - 3 + b), 8), :]
                    accumulate(acc, x, row, taps)
            store_rows(jg * 8, acc)
            return inner

        lax.fori_loop(0, COLS // 8, group, 0)
        for side in range(2):
            acc = load_rows(side * (COLS - 8), range(ROWS))
            for b in (range(3), range(4, 7))[side]:
                taps = taps_of(lanes, b)
                for row in range(ROWS):
                    spot = row * 32 + (21 + b if side == 0 else b - 3)
                    accumulate(acc, border[tile, spot : spot + 8, :], row + 3, taps)
            store_rows(side * (COLS - 8), acc)
        conv[:, lanes] = cgrad[tile].astype(bf16)
        return carry

    lax.fori_loop(0, TILES, edges, 0)

    colsum[...] = jnp.zeros_like(colsum)
    loads[3].wait()
    loads[4].wait()
    for part in range(4):
        rows = pl.ds(part * 256, 256)
        value = jnp.dot(conv[rows, :], rw_ref[...], preferred_element_type=f32) + rb_ref[...].reshape(1, REDUCED)
        before[rows, :] = value
        active = (value / (1.0 + jnp.exp(-value))).astype(bf16)
        feat[rows, :] = active
        colsum[...] += jnp.sum(active.astype(f32), axis=0, keepdims=True)
    total = lax.dot_general(
        feat[...], feat[...], (((0,), (0,)), ((), ())), preferred_element_type=f32
    )
    gram[...] = total.reshape(16, 16, REDUCED)
    crecv[me] = colsum[...]

    copies = []
    for offset in range(1, 16):
        device, index = plane(offset)
        copies.append(send(gram.at[index], grecv.at[offset], g_send.at[offset], g_recv.at[offset], device))
        copies.append(send(colsum, crecv.at[me], c_send.at[offset], c_recv.at[offset], device))
    for copy in copies:
        copy.start()
    for offset in range(1, 16):
        _, source = plane(offset, -1)
        send(gram.at[0], grecv.at[offset], g_send.at[offset], g_recv.at[offset], plane(offset)[0]).wait_recv()
        send(colsum, crecv.at[source], c_send.at[offset], c_recv.at[offset], plane(offset)[0]).wait_recv()
    mine = gram[me]
    for offset in range(1, 16):
        mine = mine + grecv[offset]
    gfull[me] = mine
    gathers = []
    for offset in range(1, 16):
        device, _ = plane(offset)
        gathers.append(send(gfull.at[me], gfull.at[me], a_send.at[offset], a_recv.at[offset], device))
    for copy in gathers:
        copy.start()
    for copy in copies:
        copy.wait_send()
    for offset in range(1, 16):
        _, source = plane(offset, -1)
        send(gfull.at[source], gfull.at[source], a_send.at[offset], a_recv.at[offset], plane(offset)[0]).wait_recv()
    for copy in gathers:
        copy.wait_send()

    mean = crecv[0]
    for index in range(1, 16):
        mean = mean + crecv[index]
    mean = mean * (1.0 / count)
    wide = jnp.broadcast_to(mean, (REDUCED, REDUCED))
    sigma = gfull[...].reshape(REDUCED, REDUCED) * (1.0 / count) - wide.T * wide
    row_id = lax.broadcasted_iota(jnp.int32, (REDUCED, REDUCED), 0)
    col_id = lax.broadcasted_iota(jnp.int32, (REDUCED, REDUCED), 1)
    diagonal = row_id == col_id
    identity15 = jnp.where(diagonal, 1.5, 0.0)
    trace = jnp.sum(
        jnp.sum(jnp.where(diagonal, sigma, 0.0), axis=0, keepdims=True), axis=1, keepdims=True
    ) + epsilon
    start = sigma / trace

    def keep(ref, step, value):
        high, low = split(value)
        ref[step, 0] = high
        ref[step, 1] = low

    def kept(ref, step):
        return ref[step, 0], ref[step, 1]

    keep(ys, 0, start)
    keep(ts, 0, identity15 - 0.5 * start)
    keep(ys, 1, products((kept(ys, 0), kept(ts, 0))))
    for step in range(1, NEWTON_STEPS):
        inverse = kept(ts, 0) if step == 1 else kept(zs, step)
        factor = identity15 - 0.5 * products((inverse, kept(ys, step)))
        keep(ts, step, factor)
        if step < NEWTON_STEPS - 1:
            keep(zs, step + 1, products((kept(ts, step), inverse)))
            keep(ys, step + 1, products((kept(ys, step), kept(ts, step))))
    last = products((kept(ys, NEWTON_STEPS - 1), kept(ts, NEWTON_STEPS - 1)))
    root_scale = jnp.sqrt(trace)
    root = root_scale * last
    root_out[idp] = root.astype(bf16)

    loads[5].wait()
    loads[6].wait()
    class_id = lax.broadcasted_iota(jnp.int32, (1, CLASSES), 1)
    logits = cb_ref[...].reshape(1, CLASSES)
    for k in range(CLASSES):
        weighted = jnp.sum(cw_ref[k].astype(f32) * root, axis=0, keepdims=True)
        logits = logits + jnp.where(class_id == k, jnp.sum(weighted, axis=1, keepdims=True), 0.0)
    onehot = jnp.where(class_id == lab_ref[0], 1.0, 0.0)
    softplus = jnp.maximum(logits, 0.0) + jnp.log(1.0 + jnp.exp(-jnp.abs(logits)))
    loss = jnp.sum(softplus - onehot * logits, axis=1, keepdims=True)
    logit_grad = (loss_scale / images) * (1.0 / (1.0 + jnp.exp(-logits)) - onehot)
    small_out[idp] = jnp.zeros((8, 128), f32)
    small_out[idp, 0:1, 0:CLASSES] = logit_grad
    small_out[idp, 1:2, :] = jnp.broadcast_to(loss, (1, 128))
    roots, smalls = [], []
    for offset in range(1, 8):
        device, _ = line(offset)
        roots.append(send(root_out.at[idp], root_out.at[idp], x_send.at[offset], x_recv.at[offset], device))
        smalls.append(send(small_out.at[idp], small_out.at[idp], s_send.at[offset], s_recv.at[offset], device))
    for copy in smalls + roots:
        copy.start()

    root_grad = jnp.zeros((REDUCED, REDUCED), f32)
    for k in range(CLASSES):
        root_grad = root_grad + logit_grad[:, k : k + 1] * cw_ref[k].astype(f32)
    root_grad = 0.5 * (root_grad + root_grad.T)
    trace_grad = jnp.sum(jnp.sum(root_grad * last, axis=0, keepdims=True), axis=1, keepdims=True)
    trace_grad = trace_grad * 0.5 / root_scale
    seed = root_scale * root_grad
    d_y = split(seed)
    d_t = split(-0.5 * seed)
    d_z = d_t
    d_y = split(products((d_y, kept(ts, 0)), (kept(ys, 0), d_t)))
    for step in range(1, NEWTON_STEPS):
        inverse = kept(ts, 0) if step == 1 else kept(zs, step)
        d_t = split(-0.5 * products((d_z, kept(ys, step)), (inverse, d_y)))
        if step < NEWTON_STEPS - 1:
            d_z = split(products((d_t, inverse), (kept(ts, step), d_z)))
            d_y = split(products((d_y, kept(ts, step)), (kept(ys, step), d_t)))
    start_grad = products((d_y, kept(ts, NEWTON_STEPS - 1)), (kept(ys, NEWTON_STEPS - 1), d_t))
    start_grad = 0.5 * (start_grad + start_grad.T)
    start_value = ys[0, 0].astype(f32) + ys[0, 1].astype(f32)
    inner = jnp.sum(jnp.sum(start_grad * start_value, axis=0, keepdims=True), axis=1, keepdims=True)
    trace_grad = trace_grad - inner / trace
    sigma_grad = start_grad / trace + jnp.where(diagonal, trace_grad, 0.0)
    symmetric = (sigma_grad * (2.0 / count)).astype(bf16)
    sym[...] = symmetric
    mean_high, mean_low = split(jnp.broadcast_to(mean, (8, REDUCED)))
    mean_term[...] = jnp.dot(mean_high, symmetric, preferred_element_type=f32) + jnp.dot(
        mean_low, symmetric, preferred_element_type=f32
    )

    depth[...] = jnp.zeros_like(depth)
    bias_grad = jnp.zeros((1, REDUCED), f32)
    for part in range(4):
        rows = pl.ds(part * 256, 256)
        feat_grad = jnp.dot(feat[rows, :], sym[...], preferred_element_type=f32) - mean_term[0:1, :]
        value = before[rows, :]
        gate = 1.0 / (1.0 + jnp.exp(-value))
        pre_grad = (feat_grad * gate * (1.0 + value * (1.0 - gate))).astype(bf16)
        pre[rows, :] = pre_grad
        bias_grad = bias_grad + jnp.sum(pre_grad.astype(f32), axis=0, keepdims=True)
        conv_grad = lax.dot_general(
            pre_grad, rw_ref[...], (((1,), (1,)), ((), ())), preferred_element_type=f32
        ).astype(bf16).astype(f32)
        for tile in range(TILES):
            cgrad[tile, rows, :] = conv_grad[:, tile * 128 : tile * 128 + 128]
    weight_grad = lax.dot_general(
        conv[...], pre[...], (((0,), (0,)), ((), ())), preferred_element_type=f32
    )
    wsend[...] = weight_grad.astype(bf16).reshape(16, 48, REDUCED)
    depth[0, 15:16, :] = bias_grad[:, 0:128]
    depth[1, 15:16, :] = bias_grad[:, 128:256]

    w_copies = []
    for offset in range(1, 16):
        device, index = plane(offset)
        w_copies.append(send(wsend.at[index], wrecv.at[offset], w_send.at[offset], w_recv.at[offset], device))
    for copy in w_copies:
        copy.start()

    def depth_tile(tile, carry):
        for b in range(KERNEL):

            def group(jg, acc):
                acc = list(acc)
                grads = [
                    cgrad[tile, pl.ds(pl.multiple_of(jg * 8 + row * COLS, 8), 8), :]
                    for row in range(ROWS)
                ]
                for row in range(ROWS + 6):
                    x = image[tile, pl.ds(jg * 8 + (row * PITCH + BLOCK0 - 3 + b), 8), :]
                    for a in range(KERNEL):
                        if 0 <= row - a < ROWS:
                            acc[a] = acc[a] + x * grads[row - a]
                if b == 0:
                    partial = grads[0]
                    for row in range(1, ROWS):
                        partial = partial + grads[row]
                    acc[KERNEL] = acc[KERNEL] + partial
                return tuple(acc)

            zero = jnp.zeros((8, 128), f32)
            sums = lax.fori_loop(0, COLS // 8, group, (zero,) * (KERNEL + (b == 0)))
            for a in range(KERNEL):
                depth[tile, a * 8 + b : a * 8 + b + 1, :] = jnp.sum(sums[a], axis=0, keepdims=True)
            if b == 0:
                depth[tile, 7:8, :] = jnp.sum(sums[KERNEL], axis=0, keepdims=True)
        return carry

    lax.fori_loop(0, 3, depth_tile, 0)

    for copy in w_copies:
        copy.wait()
    w_sum = wsend[me].astype(f32)
    for offset in range(1, 16):
        w_sum = w_sum + wrecv[offset].astype(f32)
    wx[idp] = w_sum.astype(bf16)
    wx_copies = []
    for offset in range(1, 8):
        device, _ = line(offset)
        wx_copies.append(send(wx.at[idp], wx.at[idp], wx_send.at[offset], wx_recv.at[offset], device))
    for copy in wx_copies:
        copy.start()
    lax.fori_loop(3, 5, depth_tile, 0)
    for offset in range(1, 8):
        _, source = line(offset, -1)
        send(wx.at[source], wx.at[source], wx_send.at[offset], wx_recv.at[offset], line(offset)[0]).wait_recv()
    for copy in wx_copies:
        copy.wait_send()
    w_sum = wx[0].astype(f32)
    for index in range(1, 8):
        w_sum = w_sum + wx[index].astype(f32)
    wg_out[me] = w_sum.astype(bf16)
    wa_copies = []
    for offset in range(1, 16):
        device, _ = plane(offset)
        wa_copies.append(send(wg_out.at[me], wg_out.at[me], wa_send.at[offset], wa_recv.at[offset], device))
    for copy in wa_copies:
        copy.start()
    lax.fori_loop(5, 6, depth_tile, 0)

    for group8 in range(8):
        for half in range(2):
            for third in range(3):
                dsend[group8 * 2 + half, :, third * 128 : third * 128 + 128] = depth[
                    half * 3 + third, group8 * 8 : group8 * 8 + 8, :
                ].astype(bf16)
    d_copies = []
    for offset in range(1, 16):
        device, index = plane(offset)
        d_copies.append(send(dsend.at[index], drecv.at[offset], d_send.at[offset], d_recv.at[offset], device))
    for copy in d_copies:
        copy.start()

    for offset in range(1, 8):
        _, source = line(offset, -1)
        device = line(offset)[0]
        send(root_out.at[source], root_out.at[source], x_send.at[offset], x_recv.at[offset], device).wait_recv()
        send(small_out.at[source], small_out.at[source], s_send.at[offset], s_recv.at[offset], device).wait_recv()
    for index in range(8):
        for k in range(CLASSES):
            factors[index * CLASSES + k] = jnp.broadcast_to(small_out[index, 0:1, k : k + 1], (8, 128))

    def class_rows(block, carry):
        rows = pl.ds(pl.multiple_of(block * 16, 16), 16)
        for half in range(2):
            lanes = slice(half * 128, half * 128 + 128)
            blocks = [root_out[index, rows, lanes].astype(f32).reshape(2, 8, 128) for index in range(8)]
            for k in range(CLASSES):
                total = blocks[0] * factors[k]
                for index in range(1, 8):
                    total = total + blocks[index] * factors[index * CLASSES + k]
                class_out[k, rows, lanes] = total.reshape(16, 128)
        return carry

    lax.fori_loop(0, 16, class_rows, 0)
    store = pltpu.make_async_copy(class_out, class_hbm, out_sem)
    store.start()
    for copy in d_copies:
        copy.wait()
    d_sum = dsend[me].astype(f32)
    for offset in range(1, 16):
        d_sum = d_sum + drecv[offset].astype(f32)
    dx[idp] = d_sum.astype(bf16)
    dx_copies = []
    for offset in range(1, 8):
        device, _ = line(offset)
        dx_copies.append(send(dx.at[idp], dx.at[idp], dx_send.at[offset], dx_recv.at[offset], device))
    for copy in dx_copies:
        copy.start()
    for offset in range(1, 8):
        _, source = line(offset, -1)
        send(dx.at[source], dx.at[source], dx_send.at[offset], dx_recv.at[offset], line(offset)[0]).wait_recv()
    for copy in dx_copies:
        copy.wait_send()
    d_sum = dx[0].astype(f32)
    for index in range(1, 8):
        d_sum = d_sum + dx[index].astype(f32)
    dg_out[me] = d_sum.astype(bf16)
    da_copies = []
    for offset in range(1, 16):
        device, _ = plane(offset)
        da_copies.append(send(dg_out.at[me], dg_out.at[me], da_send.at[offset], da_recv.at[offset], device))
    for copy in da_copies:
        copy.start()
    for offset in range(1, 16):
        _, source = plane(offset, -1)
        device = plane(offset)[0]
        send(wg_out.at[source], wg_out.at[source], wa_send.at[offset], wa_recv.at[offset], device).wait_recv()
        send(dg_out.at[source], dg_out.at[source], da_send.at[offset], da_recv.at[offset], device).wait_recv()
    for copy in wa_copies + da_copies + roots + smalls:
        copy.wait_send()
    store.wait()


def finish_kernel(
    wg_hbm, dg_hbm, smalls_hbm, grads, loss, depth_grad, depth_bias, weight, bias, class_weight, class_bias,
    wg, dg, smalls, sem,
):
    copy = pltpu.make_async_copy(grads, class_weight, sem.at[0])
    copy.start()
    loads = [
        pltpu.make_async_copy(src, dst, sem.at[i + 1])
        for i, (src, dst) in enumerate([(wg_hbm, wg), (dg_hbm, dg), (smalls_hbm, smalls)])
    ]
    for load in loads:
        load.start()
    for load in loads:
        load.wait()
    weight[...] = wg[...].astype(f32).reshape(CHANNELS, REDUCED)
    for half in range(2):
        lanes = slice(half * 384, half * 384 + 384)
        for a in range(KERNEL):
            depth_grad[a, :, lanes] = dg[a * 2 + half, 0:7, :].astype(f32)
        depth_bias[lanes] = dg[half, 7:8, :].astype(f32).reshape(384)
    bias[...] = dg[2, 7:8, 0:REDUCED].astype(f32).reshape(REDUCED)
    small = smalls[0]
    for image in range(1, 8):
        small = small + smalls[image]
    class_bias[...] = small[0:1, 0:CLASSES].reshape(CLASSES)
    loss[...] = small[1:2, 0:1] * (1.0 / 8)
    copy.wait()


def body(
    features, depth_weight, depth_bias, reduce_weight, reduce_bias, class_weight, class_bias, labels
):
    vmem = pl.BlockSpec(memory_space=pltpu.VMEM)
    smem = pl.BlockSpec(memory_space=pltpu.SMEM)
    dma = pltpu.SemaphoreType.DMA
    hbm = pl.BlockSpec(memory_space=pltpu.HBM)
    scratch = [
        pltpu.VMEM((CLASSES, REDUCED, REDUCED), f32),
        pltpu.VMEM((ROWS, COLS, CHANNELS), bf16),
        pltpu.VMEM((KERNEL, KERNEL, CHANNELS), f32),
        pltpu.VMEM((CHANNELS,), f32),
        pltpu.VMEM((CHANNELS, REDUCED), bf16),
        pltpu.VMEM((REDUCED,), f32),
        pltpu.VMEM((CLASSES, REDUCED, REDUCED), bf16),
        pltpu.VMEM((CLASSES,), f32),
        pltpu.VMEM((8, REDUCED, REDUCED), bf16),
        pltpu.VMEM((8 * CLASSES, 8, 128), f32),
        pltpu.VMEM((TILES, (ROWS + 6) * PITCH, 128), f32),
        pltpu.VMEM((TILES, ROWS * 32, 128), f32),
        pltpu.VMEM((ROWS * COLS, CHANNELS), bf16),
        pltpu.VMEM((ROWS * COLS, REDUCED), f32),
        pltpu.VMEM((ROWS * COLS, REDUCED), bf16),
        pltpu.VMEM((ROWS * COLS, REDUCED), bf16),
        pltpu.VMEM((TILES, ROWS * COLS, 128), f32),
        pltpu.VMEM((2, 3, 16, CHANNELS), bf16),
        pltpu.VMEM((4, 3, 8, CHANNELS), bf16),
        pltpu.VMEM((2, 3, COLS, CHANNELS), bf16),
        pltpu.VMEM((2, 3, 16, CHANNELS), bf16),
        pltpu.VMEM((4, 3, 8, CHANNELS), bf16),
        pltpu.VMEM((16, 16, REDUCED), f32),
        pltpu.VMEM((16, 16, REDUCED), f32),
        pltpu.VMEM((16, 16, REDUCED), f32),
        pltpu.VMEM((1, REDUCED), f32),
        pltpu.VMEM((16, 1, REDUCED), f32),
        pltpu.VMEM((NEWTON_STEPS, 2, REDUCED, REDUCED), bf16),
        pltpu.VMEM((NEWTON_STEPS, 2, REDUCED, REDUCED), bf16),
        pltpu.VMEM((NEWTON_STEPS, 2, REDUCED, REDUCED), bf16),
        pltpu.VMEM((REDUCED, REDUCED), bf16),
        pltpu.VMEM((8, REDUCED), f32),
        pltpu.VMEM((16, 48, REDUCED), bf16),
        pltpu.VMEM((16, 48, REDUCED), bf16),
        pltpu.VMEM((8, 48, REDUCED), bf16),
        pltpu.VMEM((TILES, 64, 128), f32),
        pltpu.VMEM((16, 8, 384), bf16),
        pltpu.VMEM((16, 8, 384), bf16),
        pltpu.VMEM((8, 8, 384), bf16),
        dma((7,)), dma, dma((8,)), dma((8,)),
        dma((16,)), dma((16,)), dma((16,)), dma((16,)), dma((16,)), dma((16,)),
        dma((8,)), dma((8,)), dma((8,)), dma((8,)),
        dma((16,)), dma((16,)), dma((8,)), dma((8,)), dma((16,)), dma((16,)),
        dma((16,)), dma((16,)), dma((8,)), dma((8,)), dma((16,)), dma((16,)),
    ]
    partial = pl.pallas_call(
        main_kernel,
        out_shape=(
            jax.ShapeDtypeStruct((16, 48, REDUCED), bf16),
            jax.ShapeDtypeStruct((16, 8, 384), bf16),
            jax.ShapeDtypeStruct((8, 8, 128), f32),
            jax.ShapeDtypeStruct((CLASSES, REDUCED, REDUCED), f32),
        ),
        in_specs=[hbm] * 7 + [smem],
        out_specs=(vmem,) * 3 + (hbm,),
        scratch_shapes=scratch,
        compiler_params=pltpu.CompilerParams(
            collective_id=0, has_side_effects=True, vmem_limit_bytes=63 << 20
        ),
        name="pooling_step",
    )(
        features, depth_weight, depth_bias, reduce_weight, reduce_bias, class_weight, class_bias, labels
    )
    loss, *grads = pl.pallas_call(
        finish_kernel,
        out_shape=(
            jax.ShapeDtypeStruct((1, 1), f32),
            jax.ShapeDtypeStruct((KERNEL, KERNEL, CHANNELS), f32),
            jax.ShapeDtypeStruct((CHANNELS,), f32),
            jax.ShapeDtypeStruct((CHANNELS, REDUCED), f32),
            jax.ShapeDtypeStruct((REDUCED,), f32),
            jax.ShapeDtypeStruct((CLASSES, REDUCED, REDUCED), f32),
            jax.ShapeDtypeStruct((CLASSES,), f32),
        ),
        in_specs=[hbm] * 4,
        out_specs=(vmem,) * 5 + (hbm, vmem),
        scratch_shapes=[
            pltpu.VMEM((16, 48, REDUCED), bf16), pltpu.VMEM((16, 8, 384), bf16), pltpu.VMEM((8, 8, 128), f32),
            dma((4,)),
        ],
        compiler_params=pltpu.CompilerParams(vmem_limit_bytes=63 << 20),
        name="outputs",
    )(*partial)
    return (loss.reshape(()), *grads)


def solution(mesh):
    placed = (P("dp", "sy", "sx", None), P(), P(), P(), P(), P(), P(), P("dp"))
    return jax.shard_map(
        body,
        mesh=mesh,
        in_specs=placed,
        out_specs=(P(), P(), P(), P(), P(), P(), P()),
        check_vma=False,
    )
```

```python
import functools

import jax
import jax.numpy as jnp
from jax import lax
from jax.experimental import pallas as pl
from jax.experimental.pallas import tpu as pltpu
from jax.sharding import PartitionSpec as P

MESH = pl.DeviceIdType.MESH
KERNEL = 7
NEWTON_STEPS = 5
ROWS = 16
COLS = 64
TILES = 6
CHANNELS = 768
REDUCED = 256
CLASSES = 10
PITCH = 80
BLOCK0 = 8
epsilon = 1e-05
loss_scale = 64.0
f32 = jnp.float32
bf16 = jnp.bfloat16


def lanes_of(tile):
    return pl.ds(pl.multiple_of(tile * 128, 128), 128)


def split(value):
    high = value.astype(bf16)
    return high, (value - high.astype(f32)).astype(bf16)


def products(*pairs):
    left, right = [], []
    for (a_high, a_low), (b_high, b_low) in pairs:
        left += [a_low, a_high, a_high]
        right += [b_high, b_low, b_high]
    return jnp.dot(
        jnp.concatenate(left, axis=1), jnp.concatenate(right, axis=0), preferred_element_type=f32
    )


def main_kernel(
    x_hbm, w_hbm, db_hbm, rw_hbm, rb_hbm, cw_hbm, cb_hbm, lab_ref,
    wg_out, dg_out, small_out, class_hbm,
    class_out,
    x_ref, w_ref, db_ref, rw_ref, rb_ref, cw_ref, cb_ref, root_out, factors,
    image, border, conv, before, feat, pre, cgrad,
    csend, ksend, hrow, hcol, hcor,
    gram, grecv, square, gfull, colsum, crecv,
    ys, zs, ts, sym, mean_term,
    wsend, wrecv, wx, depth, dsend, drecv, dx,
    in_sem, out_sem, halo_send, halo_recv, g_send, g_recv, c_send, c_recv, a_send, a_recv,
    x_send, x_recv, s_send, s_recv, w_send, w_recv, wx_send, wx_recv, wa_send, wa_recv,
    d_send, d_recv, dx_send, dx_recv, da_send, da_recv,
):
    idp, iz, iy = lax.axis_index("dp"), lax.axis_index("sy"), lax.axis_index("sx")
    images = 8
    count = ROWS * COLS * 16
    me = iz * 4 + iy

    def plane(offset, sign=1):
        dz, dy = divmod(offset, 4)
        pz, py = lax.rem(iz + 4 + sign * dz, 4), lax.rem(iy + 4 + sign * dy, 4)
        return (idp, pz, py), pz * 4 + py

    def line(offset, sign=1):
        other = lax.rem(idp + 8 + sign * offset, 8)
        return (other, iz, iy), other

    def send(src, dst, send_sem, recv_sem, device):
        copy = pltpu.make_async_remote_copy(
            src_ref=src, dst_ref=dst, send_sem=send_sem, recv_sem=recv_sem,
            device_id=device, device_id_type=MESH,
        )
        return copy

    barrier = pltpu.get_barrier_semaphore()
    for offset in range(1, 16):
        pl.semaphore_signal(barrier, inc=1, device_id=plane(offset)[0], device_id_type=MESH)
    for offset in range(1, 8):
        pl.semaphore_signal(barrier, inc=1, device_id=line(offset)[0], device_id_type=MESH)

    loads = [
        pltpu.make_async_copy(src, dst, in_sem.at[i])
        for i, (src, dst) in enumerate([
            (x_hbm.at[0], x_ref), (w_hbm, w_ref), (db_hbm, db_ref), (rw_hbm, rw_ref),
            (rb_hbm, rb_ref), (cw_hbm, cw_ref), (cb_hbm, cb_ref),
        ])
    ]
    for load in loads:
        load.start()
    loads[0].wait()

    def fill(tile, carry):
        lanes = lanes_of(tile)
        blank = jnp.zeros((8, 128), f32)
        for row in range(ROWS):
            start = (row + 3) * PITCH + BLOCK0
            image[tile, start : start + COLS, :] = x_ref[row, :, lanes].astype(f32)
            image[tile, start - 8 : start, :] = blank
            image[tile, start + COLS : start + COLS + 8, :] = blank
            border[tile, row * 32 : row * 32 + 32, :] = jnp.zeros((32, 128), f32)
        for side in range(2):
            for col in range(3):
                at = BLOCK0 + col + (0 if side == 0 else COLS - 3)
                strip = image[tile, pl.ds(3 * PITCH + at, ROWS, stride=PITCH), :]
                csend[side, col, :, lanes] = strip.astype(bf16)
                for end in range(2):
                    ksend[end * 2 + side, col, :, lanes] = strip[8 * end : 8 * end + 8].astype(bf16)
        return carry

    lax.fori_loop(0, TILES, fill, 0)
    loads[1].wait()
    loads[2].wait()

    def taps_of(lanes, b):
        return [jnp.broadcast_to(w_ref[a, pl.ds(b, 1), lanes], (8, 128)) for a in range(KERNEL)]

    def accumulate(acc, x, row, taps):
        for a in range(KERNEL):
            if 0 <= row - a < ROWS:
                acc[row - a] = acc[row - a] + x * taps[a]

    def conv_tile(tile, carry):
        lanes = lanes_of(tile)

        def group(jg, inner):
            acc = [jnp.broadcast_to(db_ref[lanes].reshape(1, 128), (8, 128))] * ROWS
            for b in range(KERNEL):
                taps = taps_of(lanes, b)
                for row in range(3, ROWS + 3):
                    x = image[tile, pl.ds(jg * 8 + (row * PITCH + BLOCK0 - 3 + b), 8), :]
                    accumulate(acc, x, row, taps)
            for row in range(ROWS):
                cgrad[tile, pl.ds(pl.multiple_of(jg * 8 + row * COLS, 8), 8), :] = acc[row]
            return inner

        lax.fori_loop(0, COLS // 8, group, 0)
        return carry

    lax.fori_loop(0, 2, conv_tile, 0)
    pl.semaphore_wait(barrier, 22)

    up, down = lax.rem(iz + 3, 4), lax.rem(iz + 1, 4)
    left, right = lax.rem(iy + 3, 4), lax.rem(iy + 1, 4)
    strips = [
        (csend.at[1], hcol.at[0], (idp, iz, right)),
        (csend.at[0], hcol.at[1], (idp, iz, left)),
        (ksend.at[3], hcor.at[0], (idp, down, right)),
        (ksend.at[2], hcor.at[1], (idp, down, left)),
        (ksend.at[1], hcor.at[2], (idp, up, right)),
        (ksend.at[0], hcor.at[3], (idp, up, left)),
    ]
    for part in range(3):
        lanes = pl.ds(part * 256, 256)
        strips += [
            (x_ref.at[pl.ds(ROWS - 3, 3), :, lanes], hrow.at[0, :, :, lanes], (idp, down, iy)),
            (x_ref.at[pl.ds(0, 3), :, lanes], hrow.at[1, :, :, lanes], (idp, up, iy)),
        ]
    halo = [
        send(src, dst, halo_send.at[i], halo_recv.at[i], device)
        for i, (src, dst, device) in enumerate(strips)
    ]
    for copy in halo:
        copy.start()
    lax.fori_loop(2, TILES, conv_tile, 0)
    has_up, has_down, has_left, has_right = iz > 0, iz < 3, iy > 0, iy < 3

    def edges(tile, carry):
        lanes = lanes_of(tile)
        for end in range(2):
            has_row = (has_up, has_down)[end]
            for row in range(3):
                start = (row + 19 * end) * PITCH + BLOCK0
                strip = hrow[end, row, :, lanes].astype(f32)
                image[tile, start : start + COLS, :] = jnp.where(has_row, strip, 0.0)
        for side in range(2):
            has_col = (has_left, has_right)[side]
            for col in range(3):
                at = BLOCK0 - 3 + col + side * (COLS + 3)
                strip = hcol[side, col, :, lanes].astype(f32)
                strip = jnp.where(has_col, strip, 0.0)
                image[tile, pl.ds(3 * PITCH + at, ROWS, stride=PITCH), :] = strip
                spot = 21 + col if side == 0 else 8 + col
                border[tile, pl.ds(spot, ROWS, stride=32), :] = strip
                for end in range(2):
                    has_both = jnp.logical_and((has_up, has_down)[end], has_col)
                    strip = hcor[end * 2 + side, col, :, lanes].astype(f32)
                    strip = jnp.where(has_both, strip, 0.0)
                    strip = strip[5:8] if end == 0 else strip[0:3]
                    image[tile, pl.ds(19 * end * PITCH + at, 3, stride=PITCH), :] = strip

        def load_rows(start, rows):
            return {
                row: cgrad[tile, pl.ds(pl.multiple_of(start + row * COLS, 8), 8), :] for row in rows
            }

        def store_rows(start, acc):
            for row, value in acc.items():
                cgrad[tile, pl.ds(pl.multiple_of(start + row * COLS, 8), 8), :] = value

        def group(jg, inner):
            acc = load_rows(jg * 8, (0, 1, 2, 13, 14, 15))
            for b in range(KERNEL):
                taps = taps_of(lanes, b)
                for row in (0, 1, 2, 19, 20, 21):
                    x = image[tile, pl.ds(jg * 8 + (row * PITCH + BLOCK0 - 3 + b), 8), :]
                    accumulate(acc, x, row, taps)
            store_rows(jg * 8, acc)
            return inner

        lax.fori_loop(0, COLS // 8, group, 0)
        for side in range(2):
            acc = load_rows(side * (COLS - 8), range(ROWS))
            for b in (range(3), range(4, 7))[side]:
                taps = taps_of(lanes, b)
                for row in range(ROWS):
                    spot = row * 32 + (21 + b if side == 0 else b - 3)
                    accumulate(acc, border[tile, spot : spot + 8, :], row + 3, taps)
            store_rows(side * (COLS - 8), acc)
        conv[:, lanes] = cgrad[tile].astype(bf16)
        return carry

    for copy in halo[:6]:
        copy.wait_recv()
    for part in range(3):
        for copy in halo[6 + 2 * part : 8 + 2 * part]:
            copy.wait_recv()
        lax.fori_loop(2 * part, 2 * part + 2, edges, 0)
    for copy in halo:
        copy.wait_send()

    colsum[...] = jnp.zeros_like(colsum)
    loads[3].wait()
    loads[4].wait()
    for part in range(4):
        rows = pl.ds(part * 256, 256)
        value = jnp.dot(conv[rows, :], rw_ref[...], preferred_element_type=f32) + rb_ref[...].reshape(1, REDUCED)
        before[rows, :] = value
        active = (value / (1.0 + jnp.exp(-value))).astype(bf16)
        feat[rows, :] = active
        colsum[...] += jnp.sum(active.astype(f32), axis=0, keepdims=True)
    total = lax.dot_general(
        feat[...], feat[...], (((0,), (0,)), ((), ())), preferred_element_type=f32
    )
    gram[...] = total.reshape(16, 16, REDUCED)
    crecv[me] = colsum[...]

    copies = []
    for offset in range(1, 16):
        device, index = plane(offset)
        copies.append(send(gram.at[index], grecv.at[offset], g_send.at[offset], g_recv.at[offset], device))
        copies.append(send(colsum, crecv.at[me], c_send.at[offset], c_recv.at[offset], device))
    for copy in copies:
        copy.start()
    for offset in range(1, 16):
        _, source = plane(offset, -1)
        send(gram.at[0], grecv.at[offset], g_send.at[offset], g_recv.at[offset], plane(offset)[0]).wait_recv()
        send(colsum, crecv.at[source], c_send.at[offset], c_recv.at[offset], plane(offset)[0]).wait_recv()
    mine = gram[me]
    for offset in range(1, 16):
        mine = mine + grecv[offset]
    mean = crecv[0]
    for index in range(1, 16):
        mean = mean + crecv[index]
    mean = mean * (1.0 / count)
    wide = jnp.broadcast_to(mean, (REDUCED, REDUCED))
    square[...] = (wide.T * wide).reshape(16, 16, REDUCED)
    gfull[me] = (mine * (1.0 / count) - square[me]).astype(bf16)
    gathers = []
    for offset in range(1, 16):
        device, _ = plane(offset)
        gathers.append(send(gfull.at[me], gfull.at[me], a_send.at[offset], a_recv.at[offset], device))
    for copy in gathers:
        copy.start()
    for copy in copies:
        copy.wait_send()
    for offset in range(1, 16):
        _, source = plane(offset, -1)
        send(gfull.at[source], gfull.at[source], a_send.at[offset], a_recv.at[offset], plane(offset)[0]).wait_recv()
    for copy in gathers:
        copy.wait_send()

    sigma = gfull[...].reshape(REDUCED, REDUCED).astype(f32)
    row_id = lax.broadcasted_iota(jnp.int32, (REDUCED, REDUCED), 0)
    col_id = lax.broadcasted_iota(jnp.int32, (REDUCED, REDUCED), 1)
    diagonal = row_id == col_id
    identity15 = jnp.where(diagonal, 1.5, 0.0)
    trace = jnp.sum(
        jnp.sum(jnp.where(diagonal, sigma, 0.0), axis=0, keepdims=True), axis=1, keepdims=True
    ) + epsilon
    start = sigma / trace

    def keep(ref, step, value):
        high, low = split(value)
        ref[step, 0] = high
        ref[step, 1] = low

    def kept(ref, step):
        return ref[step, 0], ref[step, 1]

    keep(ys, 0, start)
    keep(ts, 0, identity15 - 0.5 * start)
    keep(ys, 1, products((kept(ys, 0), kept(ts, 0))))
    for step in range(1, NEWTON_STEPS):
        inverse = kept(ts, 0) if step == 1 else kept(zs, step)
        factor = identity15 - 0.5 * products((inverse, kept(ys, step)))
        keep(ts, step, factor)
        if step < NEWTON_STEPS - 1:
            keep(zs, step + 1, products((kept(ts, step), inverse)))
            keep(ys, step + 1, products((kept(ys, step), kept(ts, step))))
    last = products((kept(ys, NEWTON_STEPS - 1), kept(ts, NEWTON_STEPS - 1)))
    root_scale = jnp.sqrt(trace)
    root = root_scale * last
    root_out[idp] = root.astype(bf16)

    loads[5].wait()
    loads[6].wait()
    class_id = lax.broadcasted_iota(jnp.int32, (1, CLASSES), 1)
    logits = cb_ref[...].reshape(1, CLASSES)
    for k in range(CLASSES):
        weighted = jnp.sum(cw_ref[k].astype(f32) * root, axis=0, keepdims=True)
        logits = logits + jnp.where(class_id == k, jnp.sum(weighted, axis=1, keepdims=True), 0.0)
    onehot = jnp.where(class_id == lab_ref[0], 1.0, 0.0)
    softplus = jnp.maximum(logits, 0.0) + jnp.log(1.0 + jnp.exp(-jnp.abs(logits)))
    loss = jnp.sum(softplus - onehot * logits, axis=1, keepdims=True)
    logit_grad = (loss_scale / images) * (1.0 / (1.0 + jnp.exp(-logits)) - onehot)
    small_out[idp] = jnp.zeros((8, 128), f32)
    small_out[idp, 0:1, 0:CLASSES] = logit_grad
    small_out[idp, 1:2, :] = jnp.broadcast_to(loss, (1, 128))
    roots, smalls = [], []
    for offset in range(1, 8):
        device, _ = line(offset)
        roots.append(send(root_out.at[idp], root_out.at[idp], x_send.at[offset], x_recv.at[offset], device))
        smalls.append(send(small_out.at[idp], small_out.at[idp], s_send.at[offset], s_recv.at[offset], device))
    for copy in smalls + roots:
        copy.start()

    root_grad = jnp.zeros((REDUCED, REDUCED), f32)
    for k in range(CLASSES):
        root_grad = root_grad + logit_grad[:, k : k + 1] * cw_ref[k].astype(f32)
    root_grad = 0.5 * (root_grad + root_grad.T)
    trace_grad = jnp.sum(jnp.sum(root_grad * last, axis=0, keepdims=True), axis=1, keepdims=True)
    trace_grad = trace_grad * 0.5 / root_scale
    seed = root_scale * root_grad
    d_y = split(seed)
    d_t = split(-0.5 * seed)
    d_z = d_t
    d_y = split(products((d_y, kept(ts, 0)), (kept(ys, 0), d_t)))
    for step in range(1, NEWTON_STEPS):
        inverse = kept(ts, 0) if step == 1 else kept(zs, step)
        d_t = split(-0.5 * products((d_z, kept(ys, step)), (inverse, d_y)))
        if step < NEWTON_STEPS - 1:
            d_z = split(products((d_t, inverse), (kept(ts, step), d_z)))
            d_y = split(products((d_y, kept(ts, step)), (kept(ys, step), d_t)))
    start_grad = products((d_y, kept(ts, NEWTON_STEPS - 1)), (kept(ys, NEWTON_STEPS - 1), d_t))
    start_grad = 0.5 * (start_grad + start_grad.T)
    start_value = ys[0, 0].astype(f32) + ys[0, 1].astype(f32)
    inner = jnp.sum(jnp.sum(start_grad * start_value, axis=0, keepdims=True), axis=1, keepdims=True)
    trace_grad = trace_grad - inner / trace
    sigma_grad = start_grad / trace + jnp.where(diagonal, trace_grad, 0.0)
    symmetric = (sigma_grad * (2.0 / count)).astype(bf16)
    sym[...] = symmetric
    mean_high, mean_low = split(jnp.broadcast_to(mean, (8, REDUCED)))
    mean_term[...] = jnp.dot(mean_high, symmetric, preferred_element_type=f32) + jnp.dot(
        mean_low, symmetric, preferred_element_type=f32
    )

    depth[...] = jnp.zeros_like(depth)
    bias_grad = jnp.zeros((1, REDUCED), f32)
    for part in range(4):
        rows = pl.ds(part * 256, 256)
        feat_grad = jnp.dot(feat[rows, :], sym[...], preferred_element_type=f32) - mean_term[0:1, :]
        value = before[rows, :]
        gate = 1.0 / (1.0 + jnp.exp(-value))
        pre_grad = (feat_grad * gate * (1.0 + value * (1.0 - gate))).astype(bf16)
        pre[rows, :] = pre_grad
        bias_grad = bias_grad + jnp.sum(pre_grad.astype(f32), axis=0, keepdims=True)
        conv_grad = lax.dot_general(
            pre_grad, rw_ref[...], (((1,), (1,)), ((), ())), preferred_element_type=f32
        ).astype(bf16).astype(f32)
        for tile in range(TILES):
            cgrad[tile, rows, :] = conv_grad[:, tile * 128 : tile * 128 + 128]
    weight_grad = lax.dot_general(
        conv[...], pre[...], (((0,), (0,)), ((), ())), preferred_element_type=f32
    )
    wsend[...] = weight_grad.astype(bf16).reshape(16, 48, REDUCED)
    depth[0, 15:16, :] = bias_grad[:, 0:128]
    depth[1, 15:16, :] = bias_grad[:, 128:256]

    w_copies = []
    for offset in range(1, 16):
        device, index = plane(offset)
        w_copies.append(send(wsend.at[index], wrecv.at[offset], w_send.at[offset], w_recv.at[offset], device))
    for copy in w_copies:
        copy.start()

    def depth_tile(tile, carry):
        for b in range(KERNEL):

            def group(jg, acc):
                acc = list(acc)
                grads = [
                    cgrad[tile, pl.ds(pl.multiple_of(jg * 8 + row * COLS, 8), 8), :]
                    for row in range(ROWS)
                ]
                for row in range(ROWS + 6):
                    x = image[tile, pl.ds(jg * 8 + (row * PITCH + BLOCK0 - 3 + b), 8), :]
                    for a in range(KERNEL):
                        if 0 <= row - a < ROWS:
                            acc[a] = acc[a] + x * grads[row - a]
                if b == 0:
                    partial = grads[0]
                    for row in range(1, ROWS):
                        partial = partial + grads[row]
                    acc[KERNEL] = acc[KERNEL] + partial
                return tuple(acc)

            zero = jnp.zeros((8, 128), f32)
            sums = lax.fori_loop(0, COLS // 8, group, (zero,) * (KERNEL + (b == 0)))
            for a in range(KERNEL):
                depth[tile, a * 8 + b : a * 8 + b + 1, :] = jnp.sum(sums[a], axis=0, keepdims=True)
            if b == 0:
                depth[tile, 7:8, :] = jnp.sum(sums[KERNEL], axis=0, keepdims=True)
        return carry

    lax.fori_loop(0, 3, depth_tile, 0)

    for copy in w_copies:
        copy.wait()
    w_sum = wsend[me].astype(f32)
    for offset in range(1, 16):
        w_sum = w_sum + wrecv[offset].astype(f32)
    wx[idp] = w_sum.astype(bf16)
    wx_copies = []
    for offset in range(1, 8):
        device, _ = line(offset)
        wx_copies.append(send(wx.at[idp], wx.at[idp], wx_send.at[offset], wx_recv.at[offset], device))
    for copy in wx_copies:
        copy.start()
    lax.fori_loop(3, TILES, depth_tile, 0)

    for group8 in range(8):
        for half in range(2):
            for third in range(3):
                dsend[group8 * 2 + half, :, third * 128 : third * 128 + 128] = depth[
                    half * 3 + third, group8 * 8 : group8 * 8 + 8, :
                ].astype(bf16)
    d_copies = []
    for offset in range(1, 16):
        device, index = plane(offset)
        d_copies.append(send(dsend.at[index], drecv.at[offset], d_send.at[offset], d_recv.at[offset], device))
    for copy in d_copies:
        copy.start()

    for offset in range(1, 8):
        _, source = line(offset, -1)
        send(wx.at[source], wx.at[source], wx_send.at[offset], wx_recv.at[offset], line(offset)[0]).wait_recv()
    for copy in wx_copies:
        copy.wait_send()
    w_sum = wx[0].astype(f32)
    for index in range(1, 8):
        w_sum = w_sum + wx[index].astype(f32)
    wg_out[me] = w_sum.astype(bf16)
    wa_copies = []
    for offset in range(1, 16):
        device, _ = plane(offset)
        wa_copies.append(send(wg_out.at[me], wg_out.at[me], wa_send.at[offset], wa_recv.at[offset], device))
    for copy in wa_copies:
        copy.start()

    for offset in range(1, 8):
        _, source = line(offset, -1)
        device = line(offset)[0]
        send(root_out.at[source], root_out.at[source], x_send.at[offset], x_recv.at[offset], device).wait_recv()
        send(small_out.at[source], small_out.at[source], s_send.at[offset], s_recv.at[offset], device).wait_recv()
    for index in range(8):
        for k in range(CLASSES):
            factors[index * CLASSES + k] = jnp.broadcast_to(small_out[index, 0:1, k : k + 1], (8, 128))

    def class_rows(block, carry):
        rows = pl.ds(pl.multiple_of(block * 16, 16), 16)
        for half in range(2):
            lanes = slice(half * 128, half * 128 + 128)
            blocks = [root_out[index, rows, lanes].astype(f32).reshape(2, 8, 128) for index in range(8)]
            for k in range(CLASSES):
                total = blocks[0] * factors[k]
                for index in range(1, 8):
                    total = total + blocks[index] * factors[index * CLASSES + k]
                class_out[k, rows, lanes] = total.reshape(16, 128)
        return carry

    lax.fori_loop(0, 16, class_rows, 0)
    store = pltpu.make_async_copy(class_out, class_hbm, out_sem)
    store.start()
    for copy in d_copies:
        copy.wait()
    d_sum = dsend[me].astype(f32)
    for offset in range(1, 16):
        d_sum = d_sum + drecv[offset].astype(f32)
    dx[idp] = d_sum.astype(bf16)
    dx_copies = []
    for offset in range(1, 8):
        device, _ = line(offset)
        dx_copies.append(send(dx.at[idp], dx.at[idp], dx_send.at[offset], dx_recv.at[offset], device))
    for copy in dx_copies:
        copy.start()
    for offset in range(1, 8):
        _, source = line(offset, -1)
        send(dx.at[source], dx.at[source], dx_send.at[offset], dx_recv.at[offset], line(offset)[0]).wait_recv()
    for copy in dx_copies:
        copy.wait_send()
    d_sum = dx[0].astype(f32)
    for index in range(1, 8):
        d_sum = d_sum + dx[index].astype(f32)
    dg_out[me] = d_sum.astype(bf16)
    da_copies = []
    for offset in range(1, 16):
        device, _ = plane(offset)
        da_copies.append(send(dg_out.at[me], dg_out.at[me], da_send.at[offset], da_recv.at[offset], device))
    for copy in da_copies:
        copy.start()
    for offset in range(1, 16):
        _, source = plane(offset, -1)
        device = plane(offset)[0]
        send(wg_out.at[source], wg_out.at[source], wa_send.at[offset], wa_recv.at[offset], device).wait_recv()
        send(dg_out.at[source], dg_out.at[source], da_send.at[offset], da_recv.at[offset], device).wait_recv()
    for copy in wa_copies + da_copies + roots + smalls:
        copy.wait_send()
    store.wait()


def finish_kernel(
    wg_hbm, dg_hbm, smalls_hbm, grads,
    loss_hbm, depth_hbm, depth_bias_hbm, weight_hbm, bias_hbm, class_weight, class_bias_hbm,
    wg, dg, smalls, buffer, loss, depth_grad, depth_bias, weight, bias, class_bias,
    load_sem, store_sem, class_in, class_out,
):
    loads = [
        pltpu.make_async_copy(src, dst, load_sem.at[i])
        for i, (src, dst) in enumerate([(wg_hbm, wg), (dg_hbm, dg), (smalls_hbm, smalls)])
    ]
    fetches = [pltpu.make_async_copy(grads.at[k], buffer.at[k], class_in.at[k]) for k in range(CLASSES)]
    stores = [pltpu.make_async_copy(buffer.at[k], class_weight.at[k], class_out.at[k]) for k in range(CLASSES)]
    results = [
        pltpu.make_async_copy(src, dst, store_sem.at[i])
        for i, (src, dst) in enumerate([
            (weight, weight_hbm), (depth_grad, depth_hbm), (depth_bias, depth_bias_hbm),
            (bias, bias_hbm), (class_bias, class_bias_hbm), (loss, loss_hbm),
        ])
    ]
    for load in loads + fetches:
        load.start()
    for load in loads:
        load.wait()
    weight[...] = wg[...].astype(f32).reshape(CHANNELS, REDUCED)
    results[0].start()
    for half in range(2):
        lanes = slice(half * 384, half * 384 + 384)
        for a in range(KERNEL):
            depth_grad[a, :, lanes] = dg[a * 2 + half, 0:7, :].astype(f32)
        depth_bias[lanes] = dg[half, 7:8, :].astype(f32).reshape(384)
    bias[...] = dg[2, 7:8, 0:REDUCED].astype(f32).reshape(REDUCED)
    small = smalls[0]
    for image in range(1, 8):
        small = small + smalls[image]
    class_bias[...] = small[0:1, 0:CLASSES].reshape(CLASSES)
    loss[...] = small[1:2, 0:1] * (1.0 / 8)
    for result in results[1:]:
        result.start()
    for fetch, store in zip(fetches, stores):
        fetch.wait()
        store.start()
    for copy in results + stores:
        copy.wait()


def body(
    features, depth_weight, depth_bias, reduce_weight, reduce_bias, class_weight, class_bias, labels
):
    vmem = pl.BlockSpec(memory_space=pltpu.VMEM)
    smem = pl.BlockSpec(memory_space=pltpu.SMEM)
    dma = pltpu.SemaphoreType.DMA
    hbm = pl.BlockSpec(memory_space=pltpu.HBM)
    scratch = [
        pltpu.VMEM((CLASSES, REDUCED, REDUCED), f32),
        pltpu.VMEM((ROWS, COLS, CHANNELS), bf16),
        pltpu.VMEM((KERNEL, KERNEL, CHANNELS), f32),
        pltpu.VMEM((CHANNELS,), f32),
        pltpu.VMEM((CHANNELS, REDUCED), bf16),
        pltpu.VMEM((REDUCED,), f32),
        pltpu.VMEM((CLASSES, REDUCED, REDUCED), bf16),
        pltpu.VMEM((CLASSES,), f32),
        pltpu.VMEM((8, REDUCED, REDUCED), bf16),
        pltpu.VMEM((8 * CLASSES, 8, 128), f32),
        pltpu.VMEM((TILES, (ROWS + 6) * PITCH, 128), f32),
        pltpu.VMEM((TILES, ROWS * 32, 128), f32),
        pltpu.VMEM((ROWS * COLS, CHANNELS), bf16),
        pltpu.VMEM((ROWS * COLS, REDUCED), f32),
        pltpu.VMEM((ROWS * COLS, REDUCED), bf16),
        pltpu.VMEM((ROWS * COLS, REDUCED), bf16),
        pltpu.VMEM((TILES, ROWS * COLS, 128), f32),
        pltpu.VMEM((2, 3, 16, CHANNELS), bf16),
        pltpu.VMEM((4, 3, 8, CHANNELS), bf16),
        pltpu.VMEM((2, 3, COLS, CHANNELS), bf16),
        pltpu.VMEM((2, 3, 16, CHANNELS), bf16),
        pltpu.VMEM((4, 3, 8, CHANNELS), bf16),
        pltpu.VMEM((16, 16, REDUCED), f32),
        pltpu.VMEM((16, 16, REDUCED), f32),
        pltpu.VMEM((16, 16, REDUCED), f32),
        pltpu.VMEM((16, 16, REDUCED), bf16),
        pltpu.VMEM((1, REDUCED), f32),
        pltpu.VMEM((16, 1, REDUCED), f32),
        pltpu.VMEM((NEWTON_STEPS, 2, REDUCED, REDUCED), bf16),
        pltpu.VMEM((NEWTON_STEPS, 2, REDUCED, REDUCED), bf16),
        pltpu.VMEM((NEWTON_STEPS, 2, REDUCED, REDUCED), bf16),
        pltpu.VMEM((REDUCED, REDUCED), bf16),
        pltpu.VMEM((8, REDUCED), f32),
        pltpu.VMEM((16, 48, REDUCED), bf16),
        pltpu.VMEM((16, 48, REDUCED), bf16),
        pltpu.VMEM((8, 48, REDUCED), bf16),
        pltpu.VMEM((TILES, 64, 128), f32),
        pltpu.VMEM((16, 8, 384), bf16),
        pltpu.VMEM((16, 8, 384), bf16),
        pltpu.VMEM((8, 8, 384), bf16),
        dma((7,)), dma, dma((12,)), dma((12,)),
        dma((16,)), dma((16,)), dma((16,)), dma((16,)), dma((16,)), dma((16,)),
        dma((8,)), dma((8,)), dma((8,)), dma((8,)),
        dma((16,)), dma((16,)), dma((8,)), dma((8,)), dma((16,)), dma((16,)),
        dma((16,)), dma((16,)), dma((8,)), dma((8,)), dma((16,)), dma((16,)),
    ]
    partial = pl.pallas_call(
        main_kernel,
        out_shape=(
            jax.ShapeDtypeStruct((16, 48, REDUCED), bf16),
            jax.ShapeDtypeStruct((16, 8, 384), bf16),
            jax.ShapeDtypeStruct((8, 8, 128), f32),
            jax.ShapeDtypeStruct((CLASSES, REDUCED, REDUCED), f32),
        ),
        in_specs=[hbm] * 7 + [smem],
        out_specs=(vmem,) * 3 + (hbm,),
        scratch_shapes=scratch,
        compiler_params=pltpu.CompilerParams(
            collective_id=0, has_side_effects=True, vmem_limit_bytes=63 << 20
        ),
        name="pooling_step",
    )(
        features, depth_weight, depth_bias, reduce_weight, reduce_bias, class_weight, class_bias, labels
    )
    loss, *grads = pl.pallas_call(
        finish_kernel,
        out_shape=(
            jax.ShapeDtypeStruct((1, 1), f32),
            jax.ShapeDtypeStruct((KERNEL, KERNEL, CHANNELS), f32),
            jax.ShapeDtypeStruct((CHANNELS,), f32),
            jax.ShapeDtypeStruct((CHANNELS, REDUCED), f32),
            jax.ShapeDtypeStruct((REDUCED,), f32),
            jax.ShapeDtypeStruct((CLASSES, REDUCED, REDUCED), f32),
            jax.ShapeDtypeStruct((CLASSES,), f32),
        ),
        in_specs=[hbm] * 4,
        out_specs=(hbm,) * 7,
        scratch_shapes=[
            pltpu.VMEM((16, 48, REDUCED), bf16), pltpu.VMEM((16, 8, 384), bf16), pltpu.VMEM((8, 8, 128), f32),
            pltpu.VMEM((CLASSES, REDUCED, REDUCED), f32), pltpu.VMEM((1, 1), f32),
            pltpu.VMEM((KERNEL, KERNEL, CHANNELS), f32), pltpu.VMEM((CHANNELS,), f32),
            pltpu.VMEM((CHANNELS, REDUCED), f32), pltpu.VMEM((REDUCED,), f32), pltpu.VMEM((CLASSES,), f32),
            dma((3,)), dma((6,)), dma((CLASSES,)), dma((CLASSES,)),
        ],
        compiler_params=pltpu.CompilerParams(vmem_limit_bytes=63 << 20),
        name="outputs",
    )(*partial)
    return (loss.reshape(()), *grads)


def solution(mesh):
    placed = (P("dp", "sy", "sx", None), P(), P(), P(), P(), P(), P(), P("dp"))
    return jax.shard_map(
        body,
        mesh=mesh,
        in_specs=placed,
        out_specs=(P(), P(), P(), P(), P(), P(), P()),
        check_vma=False,
    )
```

```python
import functools

import jax
import jax.numpy as jnp
from jax import lax
from jax.experimental import pallas as pl
from jax.experimental.pallas import tpu as pltpu
from jax.sharding import PartitionSpec as P

MESH = pl.DeviceIdType.MESH
KERNEL = 7
NEWTON_STEPS = 5
ROWS = 16
COLS = 64
TILES = 6
CHANNELS = 768
REDUCED = 256
CLASSES = 10
PITCH = 80
BLOCK0 = 8
epsilon = 1e-05
loss_scale = 64.0
f32 = jnp.float32
bf16 = jnp.bfloat16


def lanes_of(tile):
    return pl.ds(pl.multiple_of(tile * 128, 128), 128)


def split(value):
    high = value.astype(bf16)
    return high, (value - high.astype(f32)).astype(bf16)


def plus(a, b):
    return b if a is None else a if b is None else a + b


def minus(a, b):
    return a if b is None else 0.0 - b if a is None else a - b


def part_rows(rows):
    even, odd = rows[0::2], rows[1::2]
    return [
        odd,
        [minus(a, b) for a, b in zip(even, odd)],
        [minus(a, b) for a, b in zip(even[1:], odd)],
    ]


def part_taps(taps):
    even, odd = taps[0::2], taps[1::2]
    both = [plus(a, b) for a, b in zip(even, odd + [None] * (len(even) - len(odd)))]
    return [both, even, odd]


def part_outs(count):
    return [(count + 1) // 2, (count + 1) // 2, count // 2]


def join(parts, count):
    shared, first, second = parts
    return [plus(shared[i // 2], (first, second)[i % 2][i // 2]) for i in range(count)]


def twice(part, value):
    return [leaf for half in part(value) for leaf in part(half)]


def join_twice(leaves, count):
    halves = part_outs(count)
    return join([join(leaves[3 * i : 3 * i + 3], halves[i]) for i in range(3)], count)


LEAF_ROWS = 5
LEAVES = 9


def products(*pairs):
    left, right = [], []
    for (a_high, a_low), (b_high, b_low) in pairs:
        left += [a_low, a_high, a_high]
        right += [b_high, b_low, b_high]
    return jnp.dot(
        jnp.concatenate(left, axis=1), jnp.concatenate(right, axis=0), preferred_element_type=f32
    )


def main_kernel(
    x_hbm, w_hbm, db_hbm, rw_hbm, rb_hbm, cw_hbm, cb_hbm, lab_ref,
    wg_out, dg_out, small_out, class_hbm,
    class_out,
    x_ref, w_ref, db_ref, rw_ref, rb_ref, cw_ref, cb_ref, root_out, factors,
    leaf_rows, leaf_values, leaf_taps, leaf_sums, image, border, conv, before, feat, pre, cgrad,
    csend, ksend, hrow, hcol, hcor,
    gram, grecv, square, gfull, colsum, crecv,
    ys, zs, ts, sym, mean_term,
    wsend, wrecv, wx, depth, dsend, drecv, dx,
    in_sem, out_sem, halo_send, halo_recv, g_send, g_recv, c_send, c_recv, a_send, a_recv,
    x_send, x_recv, s_send, s_recv, w_send, w_recv, wx_send, wx_recv, wa_send, wa_recv,
    d_send, d_recv, dx_send, dx_recv, da_send, da_recv,
):
    idp, iz, iy = lax.axis_index("dp"), lax.axis_index("sy"), lax.axis_index("sx")
    images = 8
    count = ROWS * COLS * 16
    me = iz * 4 + iy

    def plane(offset, sign=1):
        dz, dy = divmod(offset, 4)
        pz, py = lax.rem(iz + 4 + sign * dz, 4), lax.rem(iy + 4 + sign * dy, 4)
        return (idp, pz, py), pz * 4 + py

    def line(offset, sign=1):
        other = lax.rem(idp + 8 + sign * offset, 8)
        return (other, iz, iy), other

    def send(src, dst, send_sem, recv_sem, device):
        copy = pltpu.make_async_remote_copy(
            src_ref=src, dst_ref=dst, send_sem=send_sem, recv_sem=recv_sem,
            device_id=device, device_id_type=MESH,
        )
        return copy

    barrier = pltpu.get_barrier_semaphore()
    for offset in range(1, 16):
        pl.semaphore_signal(barrier, inc=1, device_id=plane(offset)[0], device_id_type=MESH)
    for offset in range(1, 8):
        pl.semaphore_signal(barrier, inc=1, device_id=line(offset)[0], device_id_type=MESH)

    loads = [
        pltpu.make_async_copy(src, dst, in_sem.at[i])
        for i, (src, dst) in enumerate([
            (x_hbm.at[0], x_ref), (w_hbm, w_ref), (db_hbm, db_ref), (rw_hbm, rw_ref),
            (rb_hbm, rb_ref), (cw_hbm, cw_ref), (cb_hbm, cb_ref),
        ])
    ]
    for load in loads:
        load.start()
    loads[0].wait()

    def fill(tile, carry):
        lanes = lanes_of(tile)
        blank = jnp.zeros((8, 128), f32)
        for row in range(ROWS):
            start = (row + 3) * PITCH + BLOCK0
            image[tile, start : start + COLS, :] = x_ref[row, :, lanes].astype(f32)
            image[tile, start - 8 : start, :] = blank
            image[tile, start + COLS : start + COLS + 8, :] = blank
            border[tile, row * 32 : row * 32 + 32, :] = jnp.zeros((32, 128), f32)
        for row in (0, 1, 2, 19, 20, 21):
            image[tile, row * PITCH : row * PITCH + 8, :] = blank
            image[tile, row * PITCH + PITCH - 8 : row * PITCH + PITCH, :] = blank
        for side in range(2):
            for col in range(3):
                at = BLOCK0 + col + (0 if side == 0 else COLS - 3)
                strip = image[tile, pl.ds(3 * PITCH + at, ROWS, stride=PITCH), :]
                csend[side, col, :, lanes] = strip.astype(bf16)
                for end in range(2):
                    ksend[end * 2 + side, col, :, lanes] = strip[8 * end : 8 * end + 8].astype(bf16)
        return carry

    def build_leaves(tile, group, present):
        rows = [
            image[tile, pl.ds(pl.multiple_of(group * 8 + row * PITCH, 8), 8), :] if row in present else None
            for row in range(ROWS + 6)
        ]
        for leaf, values in enumerate(twice(part_rows, rows)):
            for k, value in enumerate(values[:LEAF_ROWS]):
                if value is not None:
                    leaf_rows[tile, leaf, pl.ds(pl.multiple_of(group * 8 + k * PITCH, 8), 8), :] = value

    own_rows = range(3, ROWS + 3)
    own_leaves = twice(part_rows, [0.0 if row in own_rows else None for row in range(ROWS + 6)])

    def fill_leaves(tile, carry):
        for leaf, values in enumerate(own_leaves):
            for k, value in enumerate(values[:LEAF_ROWS]):
                if value is not None:
                    leaf_rows[tile, leaf, k * PITCH : k * PITCH + 8, :] = jnp.zeros((8, 128), f32)
                    leaf_rows[tile, leaf, k * PITCH + 72 : k * PITCH + 80, :] = jnp.zeros((8, 128), f32)

        def group_leaves(group, inner):
            build_leaves(tile, group, own_rows)
            return inner

        lax.fori_loop(1, 9, group_leaves, 0)
        return carry

    lax.fori_loop(0, TILES, fill, 0)
    loads[1].wait()
    loads[2].wait()

    def taps_of(lanes, b):
        return [jnp.broadcast_to(w_ref[a, pl.ds(b, 1), lanes], (8, 128)) for a in range(KERNEL)]

    def accumulate(acc, x, row, taps):
        for a in range(KERNEL):
            if 0 <= row - a < ROWS:
                acc[row - a] = acc[row - a] + x * taps[a]

    def conv_tile(tile, carry):
        lanes = lanes_of(tile)
        fill_leaves(tile, 0)
        taps = twice(part_taps, [w_ref[a, :, lanes] for a in range(KERNEL)])
        for leaf in range(LEAVES):
            for beta, tap in enumerate(taps[leaf]):
                leaf_taps[leaf, beta, 0:KERNEL, :] = tap
        outs = twice(part_outs, ROWS)
        filled = []
        for leaf in range(LEAVES):
            weights = [
                [jnp.broadcast_to(leaf_taps[leaf, beta, b : b + 1, :], (8, 128)) for b in range(KERNEL)]
                for beta in range(len(taps[leaf]))
            ]
            here = [k for k, v in enumerate(own_leaves[leaf][:LEAF_ROWS]) if v is not None]
            filled.append([
                True if any(i + beta in here for beta in range(len(taps[leaf]))) else None
                for i in range(outs[leaf])
            ])

            def pair(index, inner, leaf=leaf, weights=weights, here=here):
                for jg in (index * 2, index * 2 + 1):
                    acc = [None] * outs[leaf]
                    for b in range(KERNEL):
                        for k in here:
                            x = leaf_rows[tile, leaf, pl.ds(jg * 8 + (k * PITCH + BLOCK0 - 3 + b), 8), :]
                            for beta in range(len(weights)):
                                if 0 <= k - beta < outs[leaf]:
                                    acc[k - beta] = plus(acc[k - beta], x * weights[beta][b])
                    for i, value in enumerate(acc):
                        if value is not None:
                            leaf_values[leaf, pl.ds(pl.multiple_of(jg * 8 + i * COLS, 8), 8), :] = value
                return inner

            lax.fori_loop(0, COLS // 16, pair, 0)

        def combine(jg, inner):
            bias = jnp.broadcast_to(db_ref[lanes].reshape(1, 128), (8, 128))
            leaves = [
                [
                    leaf_values[leaf, pl.ds(pl.multiple_of(jg * 8 + i * COLS, 8), 8), :] if here else None
                    for i, here in enumerate(filled[leaf])
                ]
                for leaf in range(LEAVES)
            ]
            for row, value in enumerate(join_twice(leaves, ROWS)):
                cgrad[tile, pl.ds(pl.multiple_of(jg * 8 + row * COLS, 8), 8), :] = value + bias
            return inner

        lax.fori_loop(0, COLS // 8, combine, 0)
        return carry

    lax.fori_loop(0, 1, conv_tile, 0)
    pl.semaphore_wait(barrier, 22)

    up, down = lax.rem(iz + 3, 4), lax.rem(iz + 1, 4)
    left, right = lax.rem(iy + 3, 4), lax.rem(iy + 1, 4)
    strips = [
        (csend.at[1], hcol.at[0], (idp, iz, right)),
        (csend.at[0], hcol.at[1], (idp, iz, left)),
        (ksend.at[3], hcor.at[0], (idp, down, right)),
        (ksend.at[2], hcor.at[1], (idp, down, left)),
        (ksend.at[1], hcor.at[2], (idp, up, right)),
        (ksend.at[0], hcor.at[3], (idp, up, left)),
    ]
    for part in range(3):
        lanes = pl.ds(part * 256, 256)
        strips += [
            (x_ref.at[pl.ds(ROWS - 3, 3), :, lanes], hrow.at[0, :, :, lanes], (idp, down, iy)),
            (x_ref.at[pl.ds(0, 3), :, lanes], hrow.at[1, :, :, lanes], (idp, up, iy)),
        ]
    halo = [
        send(src, dst, halo_send.at[i], halo_recv.at[i], device)
        for i, (src, dst, device) in enumerate(strips)
    ]
    for copy in halo:
        copy.start()
    lax.fori_loop(1, TILES, conv_tile, 0)
    has_up, has_down, has_left, has_right = iz > 0, iz < 3, iy > 0, iy < 3

    def edges(tile, carry):
        lanes = lanes_of(tile)
        for end in range(2):
            has_row = (has_up, has_down)[end]
            for row in range(3):
                start = (row + 19 * end) * PITCH + BLOCK0
                strip = hrow[end, row, :, lanes].astype(f32)
                image[tile, start : start + COLS, :] = jnp.where(has_row, strip, 0.0)
        for side in range(2):
            has_col = (has_left, has_right)[side]
            for col in range(3):
                at = BLOCK0 - 3 + col + side * (COLS + 3)
                strip = hcol[side, col, :, lanes].astype(f32)
                strip = jnp.where(has_col, strip, 0.0)
                image[tile, pl.ds(3 * PITCH + at, ROWS, stride=PITCH), :] = strip
                spot = 21 + col if side == 0 else 8 + col
                border[tile, pl.ds(spot, ROWS, stride=32), :] = strip
                for end in range(2):
                    has_both = jnp.logical_and((has_up, has_down)[end], has_col)
                    strip = hcor[end * 2 + side, col, :, lanes].astype(f32)
                    strip = jnp.where(has_both, strip, 0.0)
                    strip = strip[5:8] if end == 0 else strip[0:3]
                    image[tile, pl.ds(19 * end * PITCH + at, 3, stride=PITCH), :] = strip

        def load_rows(start, rows):
            return {
                row: cgrad[tile, pl.ds(pl.multiple_of(start + row * COLS, 8), 8), :] for row in rows
            }

        def store_rows(start, acc):
            for row, value in acc.items():
                cgrad[tile, pl.ds(pl.multiple_of(start + row * COLS, 8), 8), :] = value

        def group(jg, inner):
            acc = load_rows(jg * 8, (0, 1, 2, 13, 14, 15))
            for b in range(KERNEL):
                taps = taps_of(lanes, b)
                for row in (0, 1, 2, 19, 20, 21):
                    x = image[tile, pl.ds(jg * 8 + (row * PITCH + BLOCK0 - 3 + b), 8), :]
                    accumulate(acc, x, row, taps)
            store_rows(jg * 8, acc)
            return inner

        lax.fori_loop(0, COLS // 8, group, 0)
        for side in range(2):
            acc = load_rows(side * (COLS - 8), range(ROWS))
            for b in (range(3), range(4, 7))[side]:
                taps = taps_of(lanes, b)
                for row in range(ROWS):
                    spot = row * 32 + (21 + b if side == 0 else b - 3)
                    accumulate(acc, border[tile, spot : spot + 8, :], row + 3, taps)
            store_rows(side * (COLS - 8), acc)
        conv[:, lanes] = cgrad[tile].astype(bf16)
        return carry

    for copy in halo[:6]:
        copy.wait_recv()
    for part in range(3):
        for copy in halo[6 + 2 * part : 8 + 2 * part]:
            copy.wait_recv()
        lax.fori_loop(2 * part, 2 * part + 2, edges, 0)
    for copy in halo:
        copy.wait_send()

    colsum[...] = jnp.zeros_like(colsum)
    loads[3].wait()
    loads[4].wait()
    for part in range(4):
        rows = pl.ds(part * 256, 256)
        value = jnp.dot(conv[rows, :], rw_ref[...], preferred_element_type=f32) + rb_ref[...].reshape(1, REDUCED)
        before[rows, :] = value
        active = (value / (1.0 + jnp.exp(-value))).astype(bf16)
        feat[rows, :] = active
        colsum[...] += jnp.sum(active.astype(f32), axis=0, keepdims=True)
    total = lax.dot_general(
        feat[...], feat[...], (((0,), (0,)), ((), ())), preferred_element_type=f32
    )
    gram[...] = total.reshape(16, 16, REDUCED)
    crecv[me] = colsum[...]

    copies = []
    for offset in range(1, 16):
        device, index = plane(offset)
        copies.append(send(gram.at[index], grecv.at[offset], g_send.at[offset], g_recv.at[offset], device))
        copies.append(send(colsum, crecv.at[me], c_send.at[offset], c_recv.at[offset], device))
    for copy in copies:
        copy.start()

    def all_leaves(tile, carry):
        def group_leaves(group, inner):
            build_leaves(tile, group, range(ROWS + 6))
            return inner

        return lax.fori_loop(0, PITCH // 8, group_leaves, carry)

    lax.fori_loop(0, TILES, all_leaves, 0)
    leaf_sums[...] = jnp.zeros_like(leaf_sums)
    for offset in range(1, 16):
        _, source = plane(offset, -1)
        send(gram.at[0], grecv.at[offset], g_send.at[offset], g_recv.at[offset], plane(offset)[0]).wait_recv()
        send(colsum, crecv.at[source], c_send.at[offset], c_recv.at[offset], plane(offset)[0]).wait_recv()
    mine = gram[me]
    for offset in range(1, 16):
        mine = mine + grecv[offset]
    mean = crecv[0]
    for index in range(1, 16):
        mean = mean + crecv[index]
    mean = mean * (1.0 / count)
    wide = jnp.broadcast_to(mean, (REDUCED, REDUCED))
    square[...] = (wide.T * wide).reshape(16, 16, REDUCED)
    gfull[me] = (mine * (1.0 / count) - square[me]).astype(bf16)
    gathers = []
    for offset in range(1, 16):
        device, _ = plane(offset)
        gathers.append(send(gfull.at[me], gfull.at[me], a_send.at[offset], a_recv.at[offset], device))
    for copy in gathers:
        copy.start()
    for copy in copies:
        copy.wait_send()
    for offset in range(1, 16):
        _, source = plane(offset, -1)
        send(gfull.at[source], gfull.at[source], a_send.at[offset], a_recv.at[offset], plane(offset)[0]).wait_recv()
    for copy in gathers:
        copy.wait_send()

    sigma = gfull[...].reshape(REDUCED, REDUCED).astype(f32)
    row_id = lax.broadcasted_iota(jnp.int32, (REDUCED, REDUCED), 0)
    col_id = lax.broadcasted_iota(jnp.int32, (REDUCED, REDUCED), 1)
    diagonal = row_id == col_id
    identity15 = jnp.where(diagonal, 1.5, 0.0)
    trace = jnp.sum(
        jnp.sum(jnp.where(diagonal, sigma, 0.0), axis=0, keepdims=True), axis=1, keepdims=True
    ) + epsilon
    start = sigma / trace

    def keep(ref, step, value):
        high, low = split(value)
        ref[step, 0] = high
        ref[step, 1] = low

    def kept(ref, step):
        return ref[step, 0], ref[step, 1]

    keep(ys, 0, start)
    keep(ts, 0, identity15 - 0.5 * start)
    keep(ys, 1, products((kept(ys, 0), kept(ts, 0))))
    for step in range(1, NEWTON_STEPS):
        inverse = kept(ts, 0) if step == 1 else kept(zs, step)
        factor = identity15 - 0.5 * products((inverse, kept(ys, step)))
        keep(ts, step, factor)
        if step < NEWTON_STEPS - 1:
            keep(zs, step + 1, products((kept(ts, step), inverse)))
            keep(ys, step + 1, products((kept(ys, step), kept(ts, step))))
    last = products((kept(ys, NEWTON_STEPS - 1), kept(ts, NEWTON_STEPS - 1)))
    root_scale = jnp.sqrt(trace)
    root = root_scale * last
    root_out[idp] = root.astype(bf16)

    loads[5].wait()
    loads[6].wait()
    class_id = lax.broadcasted_iota(jnp.int32, (1, CLASSES), 1)
    logits = cb_ref[...].reshape(1, CLASSES)
    for k in range(CLASSES):
        weighted = jnp.sum(cw_ref[k].astype(f32) * root, axis=0, keepdims=True)
        logits = logits + jnp.where(class_id == k, jnp.sum(weighted, axis=1, keepdims=True), 0.0)
    onehot = jnp.where(class_id == lab_ref[0], 1.0, 0.0)
    softplus = jnp.maximum(logits, 0.0) + jnp.log(1.0 + jnp.exp(-jnp.abs(logits)))
    loss = jnp.sum(softplus - onehot * logits, axis=1, keepdims=True)
    logit_grad = (loss_scale / images) * (1.0 / (1.0 + jnp.exp(-logits)) - onehot)
    small_out[idp] = jnp.zeros((8, 128), f32)
    small_out[idp, 0:1, 0:CLASSES] = logit_grad
    small_out[idp, 1:2, :] = jnp.broadcast_to(loss, (1, 128))
    roots, smalls = [], []
    for offset in range(1, 8):
        device, _ = line(offset)
        roots.append(send(root_out.at[idp], root_out.at[idp], x_send.at[offset], x_recv.at[offset], device))
        smalls.append(send(small_out.at[idp], small_out.at[idp], s_send.at[offset], s_recv.at[offset], device))
    for copy in smalls + roots:
        copy.start()

    root_grad = jnp.zeros((REDUCED, REDUCED), f32)
    for k in range(CLASSES):
        root_grad = root_grad + logit_grad[:, k : k + 1] * cw_ref[k].astype(f32)
    root_grad = 0.5 * (root_grad + root_grad.T)
    trace_grad = jnp.sum(jnp.sum(root_grad * last, axis=0, keepdims=True), axis=1, keepdims=True)
    trace_grad = trace_grad * 0.5 / root_scale
    seed = root_scale * root_grad
    d_y = split(seed)
    d_t = split(-0.5 * seed)
    d_z = d_t
    d_y = split(products((d_y, kept(ts, 0)), (kept(ys, 0), d_t)))
    for step in range(1, NEWTON_STEPS):
        inverse = kept(ts, 0) if step == 1 else kept(zs, step)
        d_t = split(-0.5 * products((d_z, kept(ys, step)), (inverse, d_y)))
        if step < NEWTON_STEPS - 1:
            d_z = split(products((d_t, inverse), (kept(ts, step), d_z)))
            d_y = split(products((d_y, kept(ts, step)), (kept(ys, step), d_t)))
    start_grad = products((d_y, kept(ts, NEWTON_STEPS - 1)), (kept(ys, NEWTON_STEPS - 1), d_t))
    start_grad = 0.5 * (start_grad + start_grad.T)
    start_value = ys[0, 0].astype(f32) + ys[0, 1].astype(f32)
    inner = jnp.sum(jnp.sum(start_grad * start_value, axis=0, keepdims=True), axis=1, keepdims=True)
    trace_grad = trace_grad - inner / trace
    sigma_grad = start_grad / trace + jnp.where(diagonal, trace_grad, 0.0)
    symmetric = (sigma_grad * (2.0 / count)).astype(bf16)
    sym[...] = symmetric
    mean_high, mean_low = split(jnp.broadcast_to(mean, (8, REDUCED)))
    mean_term[...] = jnp.dot(mean_high, symmetric, preferred_element_type=f32) + jnp.dot(
        mean_low, symmetric, preferred_element_type=f32
    )

    depth[...] = jnp.zeros_like(depth)
    bias_grad = jnp.zeros((1, REDUCED), f32)
    for part in range(4):
        rows = pl.ds(part * 256, 256)
        feat_grad = jnp.dot(feat[rows, :], sym[...], preferred_element_type=f32) - mean_term[0:1, :]
        value = before[rows, :]
        gate = 1.0 / (1.0 + jnp.exp(-value))
        pre_grad = (feat_grad * gate * (1.0 + value * (1.0 - gate))).astype(bf16)
        pre[rows, :] = pre_grad
        bias_grad = bias_grad + jnp.sum(pre_grad.astype(f32), axis=0, keepdims=True)
        conv_grad = lax.dot_general(
            pre_grad, rw_ref[...], (((1,), (1,)), ((), ())), preferred_element_type=f32
        ).astype(bf16).astype(f32)
        for tile in range(TILES):
            cgrad[tile, rows, :] = conv_grad[:, tile * 128 : tile * 128 + 128]
    weight_grad = lax.dot_general(
        conv[...], pre[...], (((0,), (0,)), ((), ())), preferred_element_type=f32
    )
    wsend[...] = weight_grad.astype(bf16).reshape(16, 48, REDUCED)
    depth[0, 15:16, :] = bias_grad[:, 0:128]
    depth[1, 15:16, :] = bias_grad[:, 128:256]

    w_copies = []
    for offset in range(1, 16):
        device, index = plane(offset)
        w_copies.append(send(wsend.at[index], wrecv.at[offset], w_send.at[offset], w_recv.at[offset], device))
    for copy in w_copies:
        copy.start()

    def depth_tile(tile, carry):
        def grads(jg, inner):
            rows = [
                cgrad[tile, pl.ds(pl.multiple_of(jg * 8 + row * COLS, 8), 8), :] for row in range(ROWS)
            ]
            for leaf, values in enumerate(twice(part_taps, rows)):
                for k, value in enumerate(values):
                    leaf_values[leaf, pl.ds(pl.multiple_of(jg * 8 + k * COLS, 8), 8), :] = value
            return inner

        lax.fori_loop(0, COLS // 8, grads, 0)
        outs = twice(part_outs, KERNEL)
        zero = jnp.zeros((8, 128), f32)
        for leaf in range(LEAVES):
            count_out = outs[leaf]

            def group(jg, acc, leaf=leaf, count_out=count_out):
                acc = list(acc)
                taps = [
                    leaf_values[leaf, pl.ds(pl.multiple_of(jg * 8 + k * COLS, 8), 8), :] for k in range(4)
                ]
                for b in range(KERNEL):
                    for k in range(count_out + 3):
                        x = leaf_rows[tile, leaf, pl.ds(jg * 8 + (k * PITCH + BLOCK0 - 3 + b), 8), :]
                        for i in range(count_out):
                            if 0 <= k - i < 4:
                                acc[b * count_out + i] = acc[b * count_out + i] + x * taps[k - i]
                if leaf == 0:
                    acc[-1] = acc[-1] + ((taps[0] + taps[1]) + (taps[2] + taps[3]))
                return tuple(acc)

            sums = lax.fori_loop(0, COLS // 8, group, (zero,) * (KERNEL * count_out + (leaf == 0)))
            for b in range(KERNEL):
                for i in range(count_out):
                    leaf_sums[leaf, i, b : b + 1, :] = jnp.sum(sums[b * count_out + i], axis=0, keepdims=True)
            if leaf == 0:
                total = jnp.sum(sums[-1], axis=0, keepdims=True)
        leaves = [[leaf_sums[leaf, i] for i in range(outs[leaf])] for leaf in range(LEAVES)]
        for a, value in enumerate(join_twice(leaves, KERNEL)):
            depth[tile, a * 8 : a * 8 + 7, :] = value[0:7]
        depth[tile, 7:8, :] = total
        return carry

    lax.fori_loop(0, 5, depth_tile, 0)

    for copy in w_copies:
        copy.wait()
    w_sum = wsend[me].astype(f32)
    for offset in range(1, 16):
        w_sum = w_sum + wrecv[offset].astype(f32)
    wx[idp] = w_sum.astype(bf16)
    wx_copies = []
    for offset in range(1, 8):
        device, _ = line(offset)
        wx_copies.append(send(wx.at[idp], wx.at[idp], wx_send.at[offset], wx_recv.at[offset], device))
    for copy in wx_copies:
        copy.start()
    lax.fori_loop(5, TILES, depth_tile, 0)

    for group8 in range(8):
        for half in range(2):
            for third in range(3):
                dsend[group8 * 2 + half, :, third * 128 : third * 128 + 128] = depth[
                    half * 3 + third, group8 * 8 : group8 * 8 + 8, :
                ].astype(bf16)
    d_copies = []
    for offset in range(1, 16):
        device, index = plane(offset)
        d_copies.append(send(dsend.at[index], drecv.at[offset], d_send.at[offset], d_recv.at[offset], device))
    for copy in d_copies:
        copy.start()

    for offset in range(1, 8):
        _, source = line(offset, -1)
        send(wx.at[source], wx.at[source], wx_send.at[offset], wx_recv.at[offset], line(offset)[0]).wait_recv()
    for copy in wx_copies:
        copy.wait_send()
    w_sum = wx[0].astype(f32)
    for index in range(1, 8):
        w_sum = w_sum + wx[index].astype(f32)
    wg_out[me] = w_sum.astype(bf16)
    wa_copies = []
    for offset in range(1, 16):
        device, _ = plane(offset)
        wa_copies.append(send(wg_out.at[me], wg_out.at[me], wa_send.at[offset], wa_recv.at[offset], device))
    for copy in wa_copies:
        copy.start()

    for offset in range(1, 8):
        _, source = line(offset, -1)
        device = line(offset)[0]
        send(root_out.at[source], root_out.at[source], x_send.at[offset], x_recv.at[offset], device).wait_recv()
        send(small_out.at[source], small_out.at[source], s_send.at[offset], s_recv.at[offset], device).wait_recv()
    for index in range(8):
        for k in range(CLASSES):
            factors[index * CLASSES + k] = jnp.broadcast_to(small_out[index, 0:1, k : k + 1], (8, 128))

    def class_rows(block, carry):
        rows = pl.ds(pl.multiple_of(block * 16, 16), 16)
        for half in range(2):
            lanes = slice(half * 128, half * 128 + 128)
            blocks = [root_out[index, rows, lanes].astype(f32).reshape(2, 8, 128) for index in range(8)]
            for k in range(CLASSES):
                total = blocks[0] * factors[k]
                for index in range(1, 8):
                    total = total + blocks[index] * factors[index * CLASSES + k]
                class_out[k, rows, lanes] = total.reshape(16, 128)
        return carry

    lax.fori_loop(0, 16, class_rows, 0)
    store = pltpu.make_async_copy(class_out, class_hbm, out_sem)
    store.start()
    for copy in d_copies:
        copy.wait()
    d_sum = dsend[me].astype(f32)
    for offset in range(1, 16):
        d_sum = d_sum + drecv[offset].astype(f32)
    dx[idp] = d_sum.astype(bf16)
    dx_copies = []
    for offset in range(1, 8):
        device, _ = line(offset)
        dx_copies.append(send(dx.at[idp], dx.at[idp], dx_send.at[offset], dx_recv.at[offset], device))
    for copy in dx_copies:
        copy.start()
    for offset in range(1, 8):
        _, source = line(offset, -1)
        send(dx.at[source], dx.at[source], dx_send.at[offset], dx_recv.at[offset], line(offset)[0]).wait_recv()
    for copy in dx_copies:
        copy.wait_send()
    d_sum = dx[0].astype(f32)
    for index in range(1, 8):
        d_sum = d_sum + dx[index].astype(f32)
    dg_out[me] = d_sum.astype(bf16)
    da_copies = []
    for offset in range(1, 16):
        device, _ = plane(offset)
        da_copies.append(send(dg_out.at[me], dg_out.at[me], da_send.at[offset], da_recv.at[offset], device))
    for copy in da_copies:
        copy.start()
    for offset in range(1, 16):
        _, source = plane(offset, -1)
        device = plane(offset)[0]
        send(wg_out.at[source], wg_out.at[source], wa_send.at[offset], wa_recv.at[offset], device).wait_recv()
        send(dg_out.at[source], dg_out.at[source], da_send.at[offset], da_recv.at[offset], device).wait_recv()
    for copy in wa_copies + da_copies + roots + smalls:
        copy.wait_send()
    store.wait()


def finish_kernel(
    wg_hbm, dg_hbm, smalls_hbm, grads,
    loss_hbm, depth_hbm, depth_bias_hbm, weight_hbm, bias_hbm, class_weight, class_bias_hbm,
    wg, dg, smalls, buffer, loss, depth_grad, depth_bias, weight, bias, class_bias,
    load_sem, store_sem, class_in, class_out,
):
    loads = [
        pltpu.make_async_copy(src, dst, load_sem.at[i])
        for i, (src, dst) in enumerate([(wg_hbm, wg), (dg_hbm, dg), (smalls_hbm, smalls)])
    ]
    fetches = [pltpu.make_async_copy(grads.at[k], buffer.at[k], class_in.at[k]) for k in range(CLASSES)]
    stores = [pltpu.make_async_copy(buffer.at[k], class_weight.at[k], class_out.at[k]) for k in range(CLASSES)]
    results = [
        pltpu.make_async_copy(src, dst, store_sem.at[i])
        for i, (src, dst) in enumerate([
            (weight, weight_hbm), (depth_grad, depth_hbm), (depth_bias, depth_bias_hbm),
            (bias, bias_hbm), (class_bias, class_bias_hbm), (loss, loss_hbm),
        ])
    ]
    for load in loads + fetches:
        load.start()
    for load in loads:
        load.wait()
    weight[...] = wg[...].astype(f32).reshape(CHANNELS, REDUCED)
    results[0].start()
    for half in range(2):
        lanes = slice(half * 384, half * 384 + 384)
        for a in range(KERNEL):
            depth_grad[a, :, lanes] = dg[a * 2 + half, 0:7, :].astype(f32)
        depth_bias[lanes] = dg[half, 7:8, :].astype(f32).reshape(384)
    bias[...] = dg[2, 7:8, 0:REDUCED].astype(f32).reshape(REDUCED)
    small = smalls[0]
    for image in range(1, 8):
        small = small + smalls[image]
    class_bias[...] = small[0:1, 0:CLASSES].reshape(CLASSES)
    loss[...] = small[1:2, 0:1] * (1.0 / 8)
    for result in results[1:]:
        result.start()
    for fetch, store in zip(fetches, stores):
        fetch.wait()
        store.start()
    for copy in results + stores:
        copy.wait()


def body(
    features, depth_weight, depth_bias, reduce_weight, reduce_bias, class_weight, class_bias, labels
):
    vmem = pl.BlockSpec(memory_space=pltpu.VMEM)
    smem = pl.BlockSpec(memory_space=pltpu.SMEM)
    dma = pltpu.SemaphoreType.DMA
    hbm = pl.BlockSpec(memory_space=pltpu.HBM)
    scratch = [
        pltpu.VMEM((CLASSES, REDUCED, REDUCED), f32),
        pltpu.VMEM((ROWS, COLS, CHANNELS), bf16),
        pltpu.VMEM((KERNEL, KERNEL, CHANNELS), f32),
        pltpu.VMEM((CHANNELS,), f32),
        pltpu.VMEM((CHANNELS, REDUCED), bf16),
        pltpu.VMEM((REDUCED,), f32),
        pltpu.VMEM((CLASSES, REDUCED, REDUCED), bf16),
        pltpu.VMEM((CLASSES,), f32),
        pltpu.VMEM((8, REDUCED, REDUCED), bf16),
        pltpu.VMEM((8 * CLASSES, 8, 128), f32),
        pltpu.VMEM((TILES, LEAVES, LEAF_ROWS * PITCH, 128), f32),
        pltpu.VMEM((LEAVES, 4 * COLS, 128), f32),
        pltpu.VMEM((LEAVES, 2, 8, 128), f32),
        pltpu.VMEM((LEAVES, 2, 8, 128), f32),
        pltpu.VMEM((TILES, (ROWS + 6) * PITCH, 128), f32),
        pltpu.VMEM((TILES, ROWS * 32, 128), f32),
        pltpu.VMEM((ROWS * COLS, CHANNELS), bf16),
        pltpu.VMEM((ROWS * COLS, REDUCED), f32),
        pltpu.VMEM((ROWS * COLS, REDUCED), bf16),
        pltpu.VMEM((ROWS * COLS, REDUCED), bf16),
        pltpu.VMEM((TILES, ROWS * COLS, 128), f32),
        pltpu.VMEM((2, 3, 16, CHANNELS), bf16),
        pltpu.VMEM((4, 3, 8, CHANNELS), bf16),
        pltpu.VMEM((2, 3, COLS, CHANNELS), bf16),
        pltpu.VMEM((2, 3, 16, CHANNELS), bf16),
        pltpu.VMEM((4, 3, 8, CHANNELS), bf16),
        pltpu.VMEM((16, 16, REDUCED), f32),
        pltpu.VMEM((16, 16, REDUCED), f32),
        pltpu.VMEM((16, 16, REDUCED), f32),
        pltpu.VMEM((16, 16, REDUCED), bf16),
        pltpu.VMEM((1, REDUCED), f32),
        pltpu.VMEM((16, 1, REDUCED), f32),
        pltpu.VMEM((NEWTON_STEPS, 2, REDUCED, REDUCED), bf16),
        pltpu.VMEM((NEWTON_STEPS, 2, REDUCED, REDUCED), bf16),
        pltpu.VMEM((NEWTON_STEPS, 2, REDUCED, REDUCED), bf16),
        pltpu.VMEM((REDUCED, REDUCED), bf16),
        pltpu.VMEM((8, REDUCED), f32),
        pltpu.VMEM((16, 48, REDUCED), bf16),
        pltpu.VMEM((16, 48, REDUCED), bf16),
        pltpu.VMEM((8, 48, REDUCED), bf16),
        pltpu.VMEM((TILES, 64, 128), f32),
        pltpu.VMEM((16, 8, 384), bf16),
        pltpu.VMEM((16, 8, 384), bf16),
        pltpu.VMEM((8, 8, 384), bf16),
        dma((7,)), dma, dma((12,)), dma((12,)),
        dma((16,)), dma((16,)), dma((16,)), dma((16,)), dma((16,)), dma((16,)),
        dma((8,)), dma((8,)), dma((8,)), dma((8,)),
        dma((16,)), dma((16,)), dma((8,)), dma((8,)), dma((16,)), dma((16,)),
        dma((16,)), dma((16,)), dma((8,)), dma((8,)), dma((16,)), dma((16,)),
    ]
    partial = pl.pallas_call(
        main_kernel,
        out_shape=(
            jax.ShapeDtypeStruct((16, 48, REDUCED), bf16),
            jax.ShapeDtypeStruct((16, 8, 384), bf16),
            jax.ShapeDtypeStruct((8, 8, 128), f32),
            jax.ShapeDtypeStruct((CLASSES, REDUCED, REDUCED), f32),
        ),
        in_specs=[hbm] * 7 + [smem],
        out_specs=(vmem,) * 3 + (hbm,),
        scratch_shapes=scratch,
        compiler_params=pltpu.CompilerParams(
            collective_id=0, has_side_effects=True, vmem_limit_bytes=63 << 20
        ),
        name="pooling_step",
    )(
        features, depth_weight, depth_bias, reduce_weight, reduce_bias, class_weight, class_bias, labels
    )
    loss, *grads = pl.pallas_call(
        finish_kernel,
        out_shape=(
            jax.ShapeDtypeStruct((1, 1), f32),
            jax.ShapeDtypeStruct((KERNEL, KERNEL, CHANNELS), f32),
            jax.ShapeDtypeStruct((CHANNELS,), f32),
            jax.ShapeDtypeStruct((CHANNELS, REDUCED), f32),
            jax.ShapeDtypeStruct((REDUCED,), f32),
            jax.ShapeDtypeStruct((CLASSES, REDUCED, REDUCED), f32),
            jax.ShapeDtypeStruct((CLASSES,), f32),
        ),
        in_specs=[hbm] * 4,
        out_specs=(hbm,) * 7,
        scratch_shapes=[
            pltpu.VMEM((16, 48, REDUCED), bf16), pltpu.VMEM((16, 8, 384), bf16), pltpu.VMEM((8, 8, 128), f32),
            pltpu.VMEM((CLASSES, REDUCED, REDUCED), f32), pltpu.VMEM((1, 1), f32),
            pltpu.VMEM((KERNEL, KERNEL, CHANNELS), f32), pltpu.VMEM((CHANNELS,), f32),
            pltpu.VMEM((CHANNELS, REDUCED), f32), pltpu.VMEM((REDUCED,), f32), pltpu.VMEM((CLASSES,), f32),
            dma((3,)), dma((6,)), dma((CLASSES,)), dma((CLASSES,)),
        ],
        compiler_params=pltpu.CompilerParams(vmem_limit_bytes=63 << 20),
        name="outputs",
    )(*partial)
    return (loss.reshape(()), *grads)


def solution(mesh):
    placed = (P("dp", "sy", "sx", None), P(), P(), P(), P(), P(), P(), P("dp"))
    return jax.shard_map(
        body,
        mesh=mesh,
        in_specs=placed,
        out_specs=(P(), P(), P(), P(), P(), P(), P()),
        check_vma=False,
    )
```

```python
import functools

import jax
import jax.numpy as jnp
from jax import lax
from jax.experimental import pallas as pl
from jax.experimental.pallas import tpu as pltpu
from jax.sharding import PartitionSpec as P

MESH = pl.DeviceIdType.MESH
KERNEL = 7
NEWTON_STEPS = 5
ROWS = 16
COLS = 64
TILES = 6
CHANNELS = 768
REDUCED = 256
CLASSES = 10
PITCH = 80
BLOCK0 = 8
epsilon = 1e-05
loss_scale = 64.0
f32 = jnp.float32
bf16 = jnp.bfloat16


def lanes_of(tile):
    return pl.ds(pl.multiple_of(tile * 128, 128), 128)


def split(value):
    high = value.astype(bf16)
    return high, (value - high.astype(f32)).astype(bf16)


def plus(a, b):
    return b if a is None else a if b is None else a + b


def minus(a, b):
    return a if b is None else 0.0 - b if a is None else a - b


def part_rows(rows):
    even, odd = rows[0::2], rows[1::2]
    return [
        odd,
        [minus(a, b) for a, b in zip(even, odd)],
        [minus(a, b) for a, b in zip(even[1:], odd)],
    ]


def part_taps(taps):
    even, odd = taps[0::2], taps[1::2]
    both = [plus(a, b) for a, b in zip(even, odd + [None] * (len(even) - len(odd)))]
    return [both, even, odd]


def part_outs(count):
    return [(count + 1) // 2, (count + 1) // 2, count // 2]


def join(parts, count):
    shared, first, second = parts
    return [plus(shared[i // 2], (first, second)[i % 2][i // 2]) for i in range(count)]


def twice(part, value):
    return [leaf for half in part(value) for leaf in part(half)]


def join_twice(leaves, count):
    halves = part_outs(count)
    return join([join(leaves[3 * i : 3 * i + 3], halves[i]) for i in range(3)], count)


LEAF_ROWS = 5
LEAVES = 9


def products(*pairs):
    left, right = [], []
    for (a_high, a_low), (b_high, b_low) in pairs:
        left += [a_low, a_high, a_high]
        right += [b_high, b_low, b_high]
    return jnp.dot(
        jnp.concatenate(left, axis=1), jnp.concatenate(right, axis=0), preferred_element_type=f32
    )


def main_kernel(
    x_hbm, w_hbm, db_hbm, rw_hbm, rb_hbm, cw_hbm, cb_hbm, lab_ref,
    wg_out, dg_out, small_out, class_hbm,
    class_out,
    x_ref, w_ref, db_ref, rw_ref, rb_ref, cw_ref, cb_ref, root_out, factors,
    leaf_rows, leaf_values, leaf_taps, leaf_sums, image, border, conv, before, feat, pre, cgrad,
    csend, ksend, hrow, hcol, hcor,
    gram, grecv, square, gfull, colsum, crecv,
    ys, zs, ts, sym, mean_term,
    wsend, wrecv, wx, depth, dsend, drecv, dx,
    in_sem, out_sem, halo_send, halo_recv, g_send, g_recv, c_send, c_recv, a_send, a_recv,
    x_send, x_recv, s_send, s_recv, w_send, w_recv, wx_send, wx_recv, wa_send, wa_recv,
    d_send, d_recv, dx_send, dx_recv, da_send, da_recv,
):
    idp, iz, iy = lax.axis_index("dp"), lax.axis_index("sy"), lax.axis_index("sx")
    images = 8
    count = ROWS * COLS * 16
    me = iz * 4 + iy

    def plane(offset, sign=1):
        dz, dy = divmod(offset, 4)
        pz, py = lax.rem(iz + 4 + sign * dz, 4), lax.rem(iy + 4 + sign * dy, 4)
        return (idp, pz, py), pz * 4 + py

    def line(offset, sign=1):
        other = lax.rem(idp + 8 + sign * offset, 8)
        return (other, iz, iy), other

    def send(src, dst, send_sem, recv_sem, device):
        copy = pltpu.make_async_remote_copy(
            src_ref=src, dst_ref=dst, send_sem=send_sem, recv_sem=recv_sem,
            device_id=device, device_id_type=MESH,
        )
        return copy

    barrier = pltpu.get_barrier_semaphore()
    for offset in range(1, 16):
        pl.semaphore_signal(barrier, inc=1, device_id=plane(offset)[0], device_id_type=MESH)
    for offset in range(1, 8):
        pl.semaphore_signal(barrier, inc=1, device_id=line(offset)[0], device_id_type=MESH)

    loads = [
        pltpu.make_async_copy(src, dst, in_sem.at[i])
        for i, (src, dst) in enumerate([
            (x_hbm.at[0], x_ref), (w_hbm, w_ref), (db_hbm, db_ref), (rw_hbm, rw_ref),
            (rb_hbm, rb_ref), (cw_hbm, cw_ref), (cb_hbm, cb_ref),
        ])
    ]
    for load in loads:
        load.start()
    loads[0].wait()

    def fill(tile, carry):
        lanes = lanes_of(tile)
        blank = jnp.zeros((8, 128), f32)
        for row in range(ROWS):
            start = (row + 3) * PITCH + BLOCK0
            image[tile, start : start + COLS, :] = x_ref[row, :, lanes].astype(f32)
            image[tile, start - 8 : start, :] = blank
            image[tile, start + COLS : start + COLS + 8, :] = blank
            border[tile, row * 32 : row * 32 + 32, :] = jnp.zeros((32, 128), f32)
        for row in (0, 1, 2, 19, 20, 21):
            image[tile, row * PITCH : row * PITCH + 8, :] = blank
            image[tile, row * PITCH + PITCH - 8 : row * PITCH + PITCH, :] = blank
        for side in range(2):
            for col in range(3):
                at = BLOCK0 + col + (0 if side == 0 else COLS - 3)
                strip = image[tile, pl.ds(3 * PITCH + at, ROWS, stride=PITCH), :]
                csend[side, col, :, lanes] = strip.astype(bf16)
                for end in range(2):
                    ksend[end * 2 + side, col, :, lanes] = strip[8 * end : 8 * end + 8].astype(bf16)
        return carry

    def build_leaves(tile, group, present):
        rows = [
            image[tile, pl.ds(pl.multiple_of(group * 8 + row * PITCH, 8), 8), :] if row in present else None
            for row in range(ROWS + 6)
        ]
        for leaf, values in enumerate(twice(part_rows, rows)):
            for k, value in enumerate(values[:LEAF_ROWS]):
                if value is not None:
                    leaf_rows[tile, leaf, pl.ds(pl.multiple_of(group * 8 + k * PITCH, 8), 8), :] = value

    own_rows = range(3, ROWS + 3)
    own_leaves = twice(part_rows, [0.0 if row in own_rows else None for row in range(ROWS + 6)])

    def fill_leaves(tile, carry):
        for leaf, values in enumerate(own_leaves):
            for k, value in enumerate(values[:LEAF_ROWS]):
                if value is not None:
                    leaf_rows[tile, leaf, k * PITCH : k * PITCH + 8, :] = jnp.zeros((8, 128), f32)
                    leaf_rows[tile, leaf, k * PITCH + 72 : k * PITCH + 80, :] = jnp.zeros((8, 128), f32)

        def group_leaves(group, inner):
            build_leaves(tile, group, own_rows)
            return inner

        lax.fori_loop(1, 9, group_leaves, 0)
        return carry

    lax.fori_loop(0, TILES, fill, 0)
    loads[1].wait()
    loads[2].wait()

    def taps_of(lanes, b):
        return [jnp.broadcast_to(w_ref[a, pl.ds(b, 1), lanes], (8, 128)) for a in range(KERNEL)]

    def accumulate(acc, x, row, taps):
        for a in range(KERNEL):
            if 0 <= row - a < ROWS:
                acc[row - a] = acc[row - a] + x * taps[a]

    def conv_tile(tile, carry):
        lanes = lanes_of(tile)
        fill_leaves(tile, 0)
        taps = twice(part_taps, [w_ref[a, :, lanes] for a in range(KERNEL)])
        for leaf in range(LEAVES):
            for beta, tap in enumerate(taps[leaf]):
                leaf_taps[leaf, beta, 0:KERNEL, :] = tap
        outs = twice(part_outs, ROWS)
        filled = []
        for leaf in range(LEAVES):
            weights = [
                [jnp.broadcast_to(leaf_taps[leaf, beta, b : b + 1, :], (8, 128)) for b in range(KERNEL)]
                for beta in range(len(taps[leaf]))
            ]
            here = [k for k, v in enumerate(own_leaves[leaf][:LEAF_ROWS]) if v is not None]
            filled.append([
                True if any(i + beta in here for beta in range(len(taps[leaf]))) else None
                for i in range(outs[leaf])
            ])

            def pair(index, inner, leaf=leaf, weights=weights, here=here):
                for jg in (index * 2, index * 2 + 1):
                    acc = [None] * outs[leaf]
                    for b in range(KERNEL):
                        for k in here:
                            x = leaf_rows[tile, leaf, pl.ds(jg * 8 + (k * PITCH + BLOCK0 - 3 + b), 8), :]
                            for beta in range(len(weights)):
                                if 0 <= k - beta < outs[leaf]:
                                    acc[k - beta] = plus(acc[k - beta], x * weights[beta][b])
                    for i, value in enumerate(acc):
                        if value is not None:
                            leaf_values[leaf, pl.ds(pl.multiple_of(jg * 8 + i * COLS, 8), 8), :] = value
                return inner

            lax.fori_loop(0, COLS // 16, pair, 0)

        def combine(jg, inner):
            bias = jnp.broadcast_to(db_ref[lanes].reshape(1, 128), (8, 128))
            leaves = [
                [
                    leaf_values[leaf, pl.ds(pl.multiple_of(jg * 8 + i * COLS, 8), 8), :] if here else None
                    for i, here in enumerate(filled[leaf])
                ]
                for leaf in range(LEAVES)
            ]
            for row, value in enumerate(join_twice(leaves, ROWS)):
                cgrad[tile, pl.ds(pl.multiple_of(jg * 8 + row * COLS, 8), 8), :] = value + bias
            return inner

        lax.fori_loop(0, COLS // 8, combine, 0)
        return carry

    lax.fori_loop(0, 1, conv_tile, 0)
    pl.semaphore_wait(barrier, 22)

    up, down = lax.rem(iz + 3, 4), lax.rem(iz + 1, 4)
    left, right = lax.rem(iy + 3, 4), lax.rem(iy + 1, 4)
    strips = [
        (csend.at[1], hcol.at[0], (idp, iz, right)),
        (csend.at[0], hcol.at[1], (idp, iz, left)),
        (ksend.at[3], hcor.at[0], (idp, down, right)),
        (ksend.at[2], hcor.at[1], (idp, down, left)),
        (ksend.at[1], hcor.at[2], (idp, up, right)),
        (ksend.at[0], hcor.at[3], (idp, up, left)),
    ]
    for part in range(3):
        lanes = pl.ds(part * 256, 256)
        strips += [
            (x_ref.at[pl.ds(ROWS - 3, 3), :, lanes], hrow.at[0, :, :, lanes], (idp, down, iy)),
            (x_ref.at[pl.ds(0, 3), :, lanes], hrow.at[1, :, :, lanes], (idp, up, iy)),
        ]
    halo = [
        send(src, dst, halo_send.at[i], halo_recv.at[i], device)
        for i, (src, dst, device) in enumerate(strips)
    ]
    for copy in halo:
        copy.start()
    lax.fori_loop(1, TILES, conv_tile, 0)
    has_up, has_down, has_left, has_right = iz > 0, iz < 3, iy > 0, iy < 3

    def edges(tile, carry):
        lanes = lanes_of(tile)
        for end in range(2):
            has_row = (has_up, has_down)[end]
            for row in range(3):
                start = (row + 19 * end) * PITCH + BLOCK0
                strip = hrow[end, row, :, lanes].astype(f32)
                image[tile, start : start + COLS, :] = jnp.where(has_row, strip, 0.0)
        for side in range(2):
            has_col = (has_left, has_right)[side]
            for col in range(3):
                at = BLOCK0 - 3 + col + side * (COLS + 3)
                strip = hcol[side, col, :, lanes].astype(f32)
                strip = jnp.where(has_col, strip, 0.0)
                image[tile, pl.ds(3 * PITCH + at, ROWS, stride=PITCH), :] = strip
                spot = 21 + col if side == 0 else 8 + col
                border[tile, pl.ds(spot, ROWS, stride=32), :] = strip
                for end in range(2):
                    has_both = jnp.logical_and((has_up, has_down)[end], has_col)
                    strip = hcor[end * 2 + side, col, :, lanes].astype(f32)
                    strip = jnp.where(has_both, strip, 0.0)
                    strip = strip[5:8] if end == 0 else strip[0:3]
                    image[tile, pl.ds(19 * end * PITCH + at, 3, stride=PITCH), :] = strip

        def load_rows(start, rows):
            return {
                row: cgrad[tile, pl.ds(pl.multiple_of(start + row * COLS, 8), 8), :] for row in rows
            }

        def store_rows(start, acc):
            for row, value in acc.items():
                cgrad[tile, pl.ds(pl.multiple_of(start + row * COLS, 8), 8), :] = value

        def group(jg, inner):
            acc = load_rows(jg * 8, (0, 1, 2, 13, 14, 15))
            for b in range(KERNEL):
                taps = taps_of(lanes, b)
                for row in (0, 1, 2, 19, 20, 21):
                    x = image[tile, pl.ds(jg * 8 + (row * PITCH + BLOCK0 - 3 + b), 8), :]
                    accumulate(acc, x, row, taps)
            store_rows(jg * 8, acc)
            return inner

        lax.fori_loop(0, COLS // 8, group, 0)
        for side in range(2):
            acc = load_rows(side * (COLS - 8), range(ROWS))
            for b in (range(3), range(4, 7))[side]:
                taps = taps_of(lanes, b)
                for row in range(ROWS):
                    spot = row * 32 + (21 + b if side == 0 else b - 3)
                    accumulate(acc, border[tile, spot : spot + 8, :], row + 3, taps)
            store_rows(side * (COLS - 8), acc)
        conv[:, lanes] = cgrad[tile].astype(bf16)
        return carry

    for copy in halo[:6]:
        copy.wait_recv()
    for part in range(3):
        for copy in halo[6 + 2 * part : 8 + 2 * part]:
            copy.wait_recv()
        lax.fori_loop(2 * part, 2 * part + 2, edges, 0)
    for copy in halo:
        copy.wait_send()

    colsum[...] = jnp.zeros_like(colsum)
    loads[3].wait()
    loads[4].wait()
    for part in range(4):
        rows = pl.ds(part * 256, 256)
        value = jnp.dot(conv[rows, :], rw_ref[...], preferred_element_type=f32) + rb_ref[...].reshape(1, REDUCED)
        before[rows, :] = value
        active = (value / (1.0 + jnp.exp(-value))).astype(bf16)
        feat[rows, :] = active
        colsum[...] += jnp.sum(active.astype(f32), axis=0, keepdims=True)
    total = lax.dot_general(
        feat[...], feat[...], (((0,), (0,)), ((), ())), preferred_element_type=f32
    )
    own_mean = colsum[...] * (1.0 / (ROWS * COLS))
    wide = jnp.broadcast_to(own_mean, (REDUCED, REDUCED))
    centred = total * (1.0 / (ROWS * COLS)) - wide.T * wide
    gram[...] = centred.astype(bf16).reshape(16, 16, REDUCED)
    colsum[...] = own_mean
    crecv[me] = own_mean

    copies = []
    for offset in range(1, 16):
        device, index = plane(offset)
        copies.append(send(gram.at[index], grecv.at[offset], g_send.at[offset], g_recv.at[offset], device))
        copies.append(send(colsum, crecv.at[me], c_send.at[offset], c_recv.at[offset], device))
    for copy in copies:
        copy.start()

    def all_leaves(tile, carry):
        def group_leaves(group, inner):
            build_leaves(tile, group, range(ROWS + 6))
            return inner

        return lax.fori_loop(0, PITCH // 8, group_leaves, carry)

    lax.fori_loop(0, TILES, all_leaves, 0)
    leaf_sums[...] = jnp.zeros_like(leaf_sums)
    for offset in range(1, 16):
        _, source = plane(offset, -1)
        send(gram.at[0], grecv.at[offset], g_send.at[offset], g_recv.at[offset], plane(offset)[0]).wait_recv()
        send(colsum, crecv.at[source], c_send.at[offset], c_recv.at[offset], plane(offset)[0]).wait_recv()
    mean = crecv[0]
    for index in range(1, 16):
        mean = mean + crecv[index]
    mean = mean * (1.0 / 16)
    between = split(crecv[...].reshape(16, REDUCED) - mean)
    square[...] = sum(
        lax.dot_general(a, b, (((0,), (0,)), ((), ())), preferred_element_type=f32)
        for a, b in ((between[0], between[0]), (between[0], between[1]), (between[1], between[0]))
    ).reshape(16, 16, REDUCED)
    mine = gram[me].astype(f32) + square[me]
    for offset in range(1, 16):
        mine = mine + grecv[offset].astype(f32)
    gfull[me] = (mine * (1.0 / 16)).astype(bf16)
    gathers = []
    for offset in range(1, 16):
        device, _ = plane(offset)
        gathers.append(send(gfull.at[me], gfull.at[me], a_send.at[offset], a_recv.at[offset], device))
    for copy in gathers:
        copy.start()
    for copy in copies:
        copy.wait_send()
    for offset in range(1, 16):
        _, source = plane(offset, -1)
        send(gfull.at[source], gfull.at[source], a_send.at[offset], a_recv.at[offset], plane(offset)[0]).wait_recv()
    for copy in gathers:
        copy.wait_send()

    sigma = gfull[...].reshape(REDUCED, REDUCED).astype(f32)
    row_id = lax.broadcasted_iota(jnp.int32, (REDUCED, REDUCED), 0)
    col_id = lax.broadcasted_iota(jnp.int32, (REDUCED, REDUCED), 1)
    diagonal = row_id == col_id
    identity15 = jnp.where(diagonal, 1.5, 0.0)
    trace = jnp.sum(
        jnp.sum(jnp.where(diagonal, sigma, 0.0), axis=0, keepdims=True), axis=1, keepdims=True
    ) + epsilon
    start = sigma / trace

    def keep(ref, step, value):
        high, low = split(value)
        ref[step, 0] = high
        ref[step, 1] = low

    def kept(ref, step):
        return ref[step, 0], ref[step, 1]

    keep(ys, 0, start)
    keep(ts, 0, identity15 - 0.5 * start)
    keep(ys, 1, products((kept(ys, 0), kept(ts, 0))))
    for step in range(1, NEWTON_STEPS):
        inverse = kept(ts, 0) if step == 1 else kept(zs, step)
        factor = identity15 - 0.5 * products((inverse, kept(ys, step)))
        keep(ts, step, factor)
        if step < NEWTON_STEPS - 1:
            keep(zs, step + 1, products((kept(ts, step), inverse)))
            keep(ys, step + 1, products((kept(ys, step), kept(ts, step))))
    last = products((kept(ys, NEWTON_STEPS - 1), kept(ts, NEWTON_STEPS - 1)))
    root_scale = jnp.sqrt(trace)
    root = root_scale * last
    root_out[idp] = root.astype(bf16)

    loads[5].wait()
    loads[6].wait()
    class_id = lax.broadcasted_iota(jnp.int32, (1, CLASSES), 1)
    logits = cb_ref[...].reshape(1, CLASSES)
    for k in range(CLASSES):
        weighted = jnp.sum(cw_ref[k].astype(f32) * root, axis=0, keepdims=True)
        logits = logits + jnp.where(class_id == k, jnp.sum(weighted, axis=1, keepdims=True), 0.0)
    onehot = jnp.where(class_id == lab_ref[0], 1.0, 0.0)
    softplus = jnp.maximum(logits, 0.0) + jnp.log(1.0 + jnp.exp(-jnp.abs(logits)))
    loss = jnp.sum(softplus - onehot * logits, axis=1, keepdims=True)
    logit_grad = (loss_scale / images) * (1.0 / (1.0 + jnp.exp(-logits)) - onehot)
    small_out[idp] = jnp.zeros((8, 128), f32)
    small_out[idp, 0:1, 0:CLASSES] = logit_grad
    small_out[idp, 1:2, :] = jnp.broadcast_to(loss, (1, 128))
    roots, smalls = [], []
    for offset in range(1, 8):
        device, _ = line(offset)
        roots.append(send(root_out.at[idp], root_out.at[idp], x_send.at[offset], x_recv.at[offset], device))
        smalls.append(send(small_out.at[idp], small_out.at[idp], s_send.at[offset], s_recv.at[offset], device))
    for copy in smalls + roots:
        copy.start()

    root_grad = jnp.zeros((REDUCED, REDUCED), f32)
    for k in range(CLASSES):
        root_grad = root_grad + logit_grad[:, k : k + 1] * cw_ref[k].astype(f32)
    root_grad = 0.5 * (root_grad + root_grad.T)
    trace_grad = jnp.sum(jnp.sum(root_grad * last, axis=0, keepdims=True), axis=1, keepdims=True)
    trace_grad = trace_grad * 0.5 / root_scale
    seed = root_scale * root_grad
    d_y = split(seed)
    d_t = split(-0.5 * seed)
    d_z = d_t
    d_y = split(products((d_y, kept(ts, 0)), (kept(ys, 0), d_t)))
    for step in range(1, NEWTON_STEPS):
        inverse = kept(ts, 0) if step == 1 else kept(zs, step)
        d_t = split(-0.5 * products((d_z, kept(ys, step)), (inverse, d_y)))
        if step < NEWTON_STEPS - 1:
            d_z = split(products((d_t, inverse), (kept(ts, step), d_z)))
            d_y = split(products((d_y, kept(ts, step)), (kept(ys, step), d_t)))
    start_grad = products((d_y, kept(ts, NEWTON_STEPS - 1)), (kept(ys, NEWTON_STEPS - 1), d_t))
    start_grad = 0.5 * (start_grad + start_grad.T)
    start_value = ys[0, 0].astype(f32) + ys[0, 1].astype(f32)
    inner = jnp.sum(jnp.sum(start_grad * start_value, axis=0, keepdims=True), axis=1, keepdims=True)
    trace_grad = trace_grad - inner / trace
    sigma_grad = start_grad / trace + jnp.where(diagonal, trace_grad, 0.0)
    symmetric = (sigma_grad * (2.0 / count)).astype(bf16)
    sym[...] = symmetric
    mean_high, mean_low = split(jnp.broadcast_to(mean, (8, REDUCED)))
    mean_term[...] = jnp.dot(mean_high, symmetric, preferred_element_type=f32) + jnp.dot(
        mean_low, symmetric, preferred_element_type=f32
    )

    depth[...] = jnp.zeros_like(depth)
    bias_grad = jnp.zeros((1, REDUCED), f32)
    for part in range(4):
        rows = pl.ds(part * 256, 256)
        feat_grad = jnp.dot(feat[rows, :], sym[...], preferred_element_type=f32) - mean_term[0:1, :]
        value = before[rows, :]
        gate = 1.0 / (1.0 + jnp.exp(-value))
        pre_grad = (feat_grad * gate * (1.0 + value * (1.0 - gate))).astype(bf16)
        pre[rows, :] = pre_grad
        bias_grad = bias_grad + jnp.sum(pre_grad.astype(f32), axis=0, keepdims=True)
        conv_grad = lax.dot_general(
            pre_grad, rw_ref[...], (((1,), (1,)), ((), ())), preferred_element_type=f32
        ).astype(bf16).astype(f32)
        for tile in range(TILES):
            cgrad[tile, rows, :] = conv_grad[:, tile * 128 : tile * 128 + 128]
    weight_grad = lax.dot_general(
        conv[...], pre[...], (((0,), (0,)), ((), ())), preferred_element_type=f32
    )
    wsend[...] = weight_grad.astype(bf16).reshape(16, 48, REDUCED)
    depth[0, 15:16, :] = bias_grad[:, 0:128]
    depth[1, 15:16, :] = bias_grad[:, 128:256]

    w_copies = []
    for offset in range(1, 16):
        device, index = plane(offset)
        w_copies.append(send(wsend.at[index], wrecv.at[offset], w_send.at[offset], w_recv.at[offset], device))
    for copy in w_copies:
        copy.start()

    def depth_tile(tile, carry):
        def grads(jg, inner):
            rows = [
                cgrad[tile, pl.ds(pl.multiple_of(jg * 8 + row * COLS, 8), 8), :] for row in range(ROWS)
            ]
            for leaf, values in enumerate(twice(part_taps, rows)):
                for k, value in enumerate(values):
                    leaf_values[leaf, pl.ds(pl.multiple_of(jg * 8 + k * COLS, 8), 8), :] = value
            return inner

        lax.fori_loop(0, COLS // 8, grads, 0)
        outs = twice(part_outs, KERNEL)
        zero = jnp.zeros((8, 128), f32)
        for leaf in range(LEAVES):
            count_out = outs[leaf]

            def group(jg, acc, leaf=leaf, count_out=count_out):
                acc = list(acc)
                taps = [
                    leaf_values[leaf, pl.ds(pl.multiple_of(jg * 8 + k * COLS, 8), 8), :] for k in range(4)
                ]
                for b in range(KERNEL):
                    for k in range(count_out + 3):
                        x = leaf_rows[tile, leaf, pl.ds(jg * 8 + (k * PITCH + BLOCK0 - 3 + b), 8), :]
                        for i in range(count_out):
                            if 0 <= k - i < 4:
                                acc[b * count_out + i] = acc[b * count_out + i] + x * taps[k - i]
                if leaf == 0:
                    acc[-1] = acc[-1] + ((taps[0] + taps[1]) + (taps[2] + taps[3]))
                return tuple(acc)

            sums = lax.fori_loop(0, COLS // 8, group, (zero,) * (KERNEL * count_out + (leaf == 0)))
            for b in range(KERNEL):
                for i in range(count_out):
                    leaf_sums[leaf, i, b : b + 1, :] = jnp.sum(sums[b * count_out + i], axis=0, keepdims=True)
            if leaf == 0:
                total = jnp.sum(sums[-1], axis=0, keepdims=True)
        leaves = [[leaf_sums[leaf, i] for i in range(outs[leaf])] for leaf in range(LEAVES)]
        for a, value in enumerate(join_twice(leaves, KERNEL)):
            depth[tile, a * 8 : a * 8 + 7, :] = value[0:7]
        depth[tile, 7:8, :] = total
        return carry

    lax.fori_loop(0, 5, depth_tile, 0)

    for copy in w_copies:
        copy.wait()
    w_sum = wsend[me].astype(f32)
    for offset in range(1, 16):
        w_sum = w_sum + wrecv[offset].astype(f32)
    wx[idp] = w_sum.astype(bf16)
    wx_copies = []
    for offset in range(1, 8):
        device, _ = line(offset)
        wx_copies.append(send(wx.at[idp], wx.at[idp], wx_send.at[offset], wx_recv.at[offset], device))
    for copy in wx_copies:
        copy.start()
    lax.fori_loop(5, TILES, depth_tile, 0)

    for group8 in range(8):
        for half in range(2):
            for third in range(3):
                dsend[group8 * 2 + half, :, third * 128 : third * 128 + 128] = depth[
                    half * 3 + third, group8 * 8 : group8 * 8 + 8, :
                ].astype(bf16)
    d_copies = []
    for offset in range(1, 16):
        device, index = plane(offset)
        d_copies.append(send(dsend.at[index], drecv.at[offset], d_send.at[offset], d_recv.at[offset], device))
    for copy in d_copies:
        copy.start()

    for offset in range(1, 8):
        _, source = line(offset, -1)
        send(wx.at[source], wx.at[source], wx_send.at[offset], wx_recv.at[offset], line(offset)[0]).wait_recv()
    for copy in wx_copies:
        copy.wait_send()
    w_sum = wx[0].astype(f32)
    for index in range(1, 8):
        w_sum = w_sum + wx[index].astype(f32)
    wg_out[me] = w_sum.astype(bf16)
    wa_copies = []
    for offset in range(1, 16):
        device, _ = plane(offset)
        wa_copies.append(send(wg_out.at[me], wg_out.at[me], wa_send.at[offset], wa_recv.at[offset], device))
    for copy in wa_copies:
        copy.start()

    for offset in range(1, 8):
        _, source = line(offset, -1)
        device = line(offset)[0]
        send(root_out.at[source], root_out.at[source], x_send.at[offset], x_recv.at[offset], device).wait_recv()
        send(small_out.at[source], small_out.at[source], s_send.at[offset], s_recv.at[offset], device).wait_recv()
    for index in range(8):
        for k in range(CLASSES):
            factors[index * CLASSES + k] = jnp.broadcast_to(small_out[index, 0:1, k : k + 1], (8, 128))

    def class_rows(block, carry):
        rows = pl.ds(pl.multiple_of(block * 16, 16), 16)
        for half in range(2):
            lanes = slice(half * 128, half * 128 + 128)
            blocks = [root_out[index, rows, lanes].astype(f32).reshape(2, 8, 128) for index in range(8)]
            for k in range(CLASSES):
                total = blocks[0] * factors[k]
                for index in range(1, 8):
                    total = total + blocks[index] * factors[index * CLASSES + k]
                class_out[k, rows, lanes] = total.reshape(16, 128)
        return carry

    lax.fori_loop(0, 16, class_rows, 0)
    store = pltpu.make_async_copy(class_out, class_hbm, out_sem)
    store.start()
    for copy in d_copies:
        copy.wait()
    d_sum = dsend[me].astype(f32)
    for offset in range(1, 16):
        d_sum = d_sum + drecv[offset].astype(f32)
    dx[idp] = d_sum.astype(bf16)
    dx_copies = []
    for offset in range(1, 8):
        device, _ = line(offset)
        dx_copies.append(send(dx.at[idp], dx.at[idp], dx_send.at[offset], dx_recv.at[offset], device))
    for copy in dx_copies:
        copy.start()
    for offset in range(1, 8):
        _, source = line(offset, -1)
        send(dx.at[source], dx.at[source], dx_send.at[offset], dx_recv.at[offset], line(offset)[0]).wait_recv()
    for copy in dx_copies:
        copy.wait_send()
    d_sum = dx[0].astype(f32)
    for index in range(1, 8):
        d_sum = d_sum + dx[index].astype(f32)
    dg_out[me] = d_sum.astype(bf16)
    da_copies = []
    for offset in range(1, 16):
        device, _ = plane(offset)
        da_copies.append(send(dg_out.at[me], dg_out.at[me], da_send.at[offset], da_recv.at[offset], device))
    for copy in da_copies:
        copy.start()
    for offset in range(1, 16):
        _, source = plane(offset, -1)
        device = plane(offset)[0]
        send(wg_out.at[source], wg_out.at[source], wa_send.at[offset], wa_recv.at[offset], device).wait_recv()
        send(dg_out.at[source], dg_out.at[source], da_send.at[offset], da_recv.at[offset], device).wait_recv()
    for copy in wa_copies + da_copies + roots + smalls:
        copy.wait_send()
    store.wait()


def finish_kernel(
    wg_hbm, dg_hbm, smalls_hbm, grads,
    loss_hbm, depth_hbm, depth_bias_hbm, weight_hbm, bias_hbm, class_weight, class_bias_hbm,
    wg, dg, smalls, buffer, loss, depth_grad, depth_bias, weight, bias, class_bias,
    load_sem, store_sem, class_in, class_out,
):
    loads = [
        pltpu.make_async_copy(src, dst, load_sem.at[i])
        for i, (src, dst) in enumerate([(wg_hbm, wg), (dg_hbm, dg), (smalls_hbm, smalls)])
    ]
    fetches = [pltpu.make_async_copy(grads.at[k], buffer.at[k], class_in.at[k]) for k in range(CLASSES)]
    stores = [pltpu.make_async_copy(buffer.at[k], class_weight.at[k], class_out.at[k]) for k in range(CLASSES)]
    results = [
        pltpu.make_async_copy(src, dst, store_sem.at[i])
        for i, (src, dst) in enumerate([
            (weight, weight_hbm), (depth_grad, depth_hbm), (depth_bias, depth_bias_hbm),
            (bias, bias_hbm), (class_bias, class_bias_hbm), (loss, loss_hbm),
        ])
    ]
    for load in loads + fetches:
        load.start()
    for load in loads:
        load.wait()
    weight[...] = wg[...].astype(f32).reshape(CHANNELS, REDUCED)
    results[0].start()
    for half in range(2):
        lanes = slice(half * 384, half * 384 + 384)
        for a in range(KERNEL):
            depth_grad[a, :, lanes] = dg[a * 2 + half, 0:7, :].astype(f32)
        depth_bias[lanes] = dg[half, 7:8, :].astype(f32).reshape(384)
    bias[...] = dg[2, 7:8, 0:REDUCED].astype(f32).reshape(REDUCED)
    small = smalls[0]
    for image in range(1, 8):
        small = small + smalls[image]
    class_bias[...] = small[0:1, 0:CLASSES].reshape(CLASSES)
    loss[...] = small[1:2, 0:1] * (1.0 / 8)
    for result in results[1:]:
        result.start()
    for fetch, store in zip(fetches, stores):
        fetch.wait()
        store.start()
    for copy in results + stores:
        copy.wait()


def body(
    features, depth_weight, depth_bias, reduce_weight, reduce_bias, class_weight, class_bias, labels
):
    vmem = pl.BlockSpec(memory_space=pltpu.VMEM)
    dma = pltpu.SemaphoreType.DMA
    hbm = pl.BlockSpec(memory_space=pltpu.HBM)
    smem = pl.BlockSpec(memory_space=pltpu.SMEM)
    scratch = [
        pltpu.VMEM((CLASSES, REDUCED, REDUCED), f32),
        pltpu.VMEM((ROWS, COLS, CHANNELS), bf16),
        pltpu.VMEM((KERNEL, KERNEL, CHANNELS), f32),
        pltpu.VMEM((CHANNELS,), f32),
        pltpu.VMEM((CHANNELS, REDUCED), bf16),
        pltpu.VMEM((REDUCED,), f32),
        pltpu.VMEM((CLASSES, REDUCED, REDUCED), bf16),
        pltpu.VMEM((CLASSES,), f32),
        pltpu.VMEM((8, REDUCED, REDUCED), bf16),
        pltpu.VMEM((8 * CLASSES, 8, 128), f32),
        pltpu.VMEM((TILES, LEAVES, LEAF_ROWS * PITCH, 128), f32),
        pltpu.VMEM((LEAVES, 4 * COLS, 128), f32),
        pltpu.VMEM((LEAVES, 2, 8, 128), f32),
        pltpu.VMEM((LEAVES, 2, 8, 128), f32),
        pltpu.VMEM((TILES, (ROWS + 6) * PITCH, 128), f32),
        pltpu.VMEM((TILES, ROWS * 32, 128), f32),
        pltpu.VMEM((ROWS * COLS, CHANNELS), bf16),
        pltpu.VMEM((ROWS * COLS, REDUCED), f32),
        pltpu.VMEM((ROWS * COLS, REDUCED), bf16),
        pltpu.VMEM((ROWS * COLS, REDUCED), bf16),
        pltpu.VMEM((TILES, ROWS * COLS, 128), f32),
        pltpu.VMEM((2, 3, 16, CHANNELS), bf16),
        pltpu.VMEM((4, 3, 8, CHANNELS), bf16),
        pltpu.VMEM((2, 3, COLS, CHANNELS), bf16),
        pltpu.VMEM((2, 3, 16, CHANNELS), bf16),
        pltpu.VMEM((4, 3, 8, CHANNELS), bf16),
        pltpu.VMEM((16, 16, REDUCED), bf16),
        pltpu.VMEM((16, 16, REDUCED), bf16),
        pltpu.VMEM((16, 16, REDUCED), f32),
        pltpu.VMEM((16, 16, REDUCED), bf16),
        pltpu.VMEM((1, REDUCED), f32),
        pltpu.VMEM((16, 1, REDUCED), f32),
        pltpu.VMEM((NEWTON_STEPS, 2, REDUCED, REDUCED), bf16),
        pltpu.VMEM((NEWTON_STEPS, 2, REDUCED, REDUCED), bf16),
        pltpu.VMEM((NEWTON_STEPS, 2, REDUCED, REDUCED), bf16),
        pltpu.VMEM((REDUCED, REDUCED), bf16),
        pltpu.VMEM((8, REDUCED), f32),
        pltpu.VMEM((16, 48, REDUCED), bf16),
        pltpu.VMEM((16, 48, REDUCED), bf16),
        pltpu.VMEM((8, 48, REDUCED), bf16),
        pltpu.VMEM((TILES, 64, 128), f32),
        pltpu.VMEM((16, 8, 384), bf16),
        pltpu.VMEM((16, 8, 384), bf16),
        pltpu.VMEM((8, 8, 384), bf16),
        dma((7,)), dma, dma((12,)), dma((12,)),
        dma((16,)), dma((16,)), dma((16,)), dma((16,)), dma((16,)), dma((16,)),
        dma((8,)), dma((8,)), dma((8,)), dma((8,)),
        dma((16,)), dma((16,)), dma((8,)), dma((8,)), dma((16,)), dma((16,)),
        dma((16,)), dma((16,)), dma((8,)), dma((8,)), dma((16,)), dma((16,)),
    ]
    partial = pl.pallas_call(
        main_kernel,
        out_shape=(
            jax.ShapeDtypeStruct((16, 48, REDUCED), bf16),
            jax.ShapeDtypeStruct((16, 8, 384), bf16),
            jax.ShapeDtypeStruct((8, 8, 128), f32),
            jax.ShapeDtypeStruct((CLASSES, REDUCED, REDUCED), f32),
        ),
        in_specs=[hbm] * 7 + [smem],
        out_specs=(vmem,) * 3 + (hbm,),
        scratch_shapes=scratch,
        compiler_params=pltpu.CompilerParams(
            collective_id=0, has_side_effects=True, vmem_limit_bytes=63 << 20
        ),
        name="pooling_step",
    )(
        features, depth_weight, depth_bias, reduce_weight, reduce_bias, class_weight, class_bias, labels
    )
    loss, *grads = pl.pallas_call(
        finish_kernel,
        out_shape=(
            jax.ShapeDtypeStruct((1, 1), f32),
            jax.ShapeDtypeStruct((KERNEL, KERNEL, CHANNELS), f32),
            jax.ShapeDtypeStruct((CHANNELS,), f32),
            jax.ShapeDtypeStruct((CHANNELS, REDUCED), f32),
            jax.ShapeDtypeStruct((REDUCED,), f32),
            jax.ShapeDtypeStruct((CLASSES, REDUCED, REDUCED), f32),
            jax.ShapeDtypeStruct((CLASSES,), f32),
        ),
        in_specs=[hbm] * 4,
        out_specs=(hbm,) * 7,
        scratch_shapes=[
            pltpu.VMEM((16, 48, REDUCED), bf16), pltpu.VMEM((16, 8, 384), bf16), pltpu.VMEM((8, 8, 128), f32),
            pltpu.VMEM((CLASSES, REDUCED, REDUCED), f32), pltpu.VMEM((1, 1), f32),
            pltpu.VMEM((KERNEL, KERNEL, CHANNELS), f32), pltpu.VMEM((CHANNELS,), f32),
            pltpu.VMEM((CHANNELS, REDUCED), f32), pltpu.VMEM((REDUCED,), f32), pltpu.VMEM((CLASSES,), f32),
            dma((3,)), dma((6,)), dma((CLASSES,)), dma((CLASSES,)),
        ],
        compiler_params=pltpu.CompilerParams(vmem_limit_bytes=63 << 20),
        name="outputs",
    )(*partial)
    return (loss.reshape(()), *grads)


def solution(mesh):
    placed = (P("dp", "sy", "sx", None), P(), P(), P(), P(), P(), P(), P("dp"))
    return jax.shard_map(
        body,
        mesh=mesh,
        in_specs=placed,
        out_specs=(P(), P(), P(), P(), P(), P(), P()),
        check_vma=False,
    )
```

```python
import functools

import jax
import jax.numpy as jnp
from jax import lax
from jax.experimental import pallas as pl
from jax.experimental.pallas import tpu as pltpu
from jax.sharding import PartitionSpec as P

MESH = pl.DeviceIdType.MESH
KERNEL = 7
NEWTON_STEPS = 5
ROWS = 16
COLS = 64
TILES = 6
CHANNELS = 768
REDUCED = 256
CLASSES = 10
PITCH = 80
BLOCK0 = 8
PLANE = sorted(range(1, 16), key=lambda o: -(min(o // 4, 4 - o // 4) + min(o % 4, 4 - o % 4)))
LINE = sorted(range(1, 8), key=lambda o: -min(o, 8 - o))
epsilon = 1e-05
loss_scale = 64.0
f32 = jnp.float32
bf16 = jnp.bfloat16


def lanes_of(tile):
    return pl.ds(pl.multiple_of(tile * 128, 128), 128)


def split(value):
    high = value.astype(bf16)
    return high, (value - high.astype(f32)).astype(bf16)


def plus(a, b):
    return b if a is None else a if b is None else a + b


def minus(a, b):
    return a if b is None else 0.0 - b if a is None else a - b


def part_rows(rows):
    even, odd = rows[0::2], rows[1::2]
    return [
        odd,
        [minus(a, b) for a, b in zip(even, odd)],
        [minus(a, b) for a, b in zip(even[1:], odd)],
    ]


def part_taps(taps):
    even, odd = taps[0::2], taps[1::2]
    both = [plus(a, b) for a, b in zip(even, odd + [None] * (len(even) - len(odd)))]
    return [both, even, odd]


def part_outs(count):
    return [(count + 1) // 2, (count + 1) // 2, count // 2]


def join(parts, count):
    shared, first, second = parts
    return [plus(shared[i // 2], (first, second)[i % 2][i // 2]) for i in range(count)]


def twice(part, value):
    return [leaf for half in part(value) for leaf in part(half)]


def join_twice(leaves, count):
    halves = part_outs(count)
    return join([join(leaves[3 * i : 3 * i + 3], halves[i]) for i in range(3)], count)


LEAF_ROWS = 5
LEAVES = 9


def products(*pairs):
    left, right = [], []
    for (a_high, a_low), (b_high, b_low) in pairs:
        left += [a_low, a_high, a_high]
        right += [b_high, b_low, b_high]
    return jnp.dot(
        jnp.concatenate(left, axis=1), jnp.concatenate(right, axis=0), preferred_element_type=f32
    )


def main_kernel(
    x_hbm, w_hbm, db_hbm, rw_hbm, rb_hbm, cw_hbm, cb_hbm, lab_ref,
    wg_out, dg_out, small_out, class_hbm,
    class_out,
    x_ref, w_ref, db_ref, rw_ref, rb_ref, cw_ref, cb_ref, root_out, factors,
    leaf_rows, leaf_values, leaf_taps, leaf_sums, image, border, conv, before, feat, pre, cgrad,
    csend, ksend, hrow, hcol, hcor,
    gram, grecv, square, gfull, colsum, crecv,
    ys, zs, ts, sym, mean_term,
    wsend, wrecv, wx, depth, dsend, drecv, dx,
    in_sem, out_sem, halo_send, halo_recv, g_send, g_recv, c_send, c_recv, a_send, a_recv,
    x_send, x_recv, s_send, s_recv, w_send, w_recv, wx_send, wx_recv, wa_send, wa_recv,
    d_send, d_recv, dx_send, dx_recv, da_send, da_recv,
):
    idp, iz, iy = lax.axis_index("dp"), lax.axis_index("sy"), lax.axis_index("sx")
    images = 8
    count = ROWS * COLS * 16
    me = iz * 4 + iy

    def plane(offset, sign=1):
        dz, dy = divmod(offset, 4)
        pz, py = lax.rem(iz + 4 + sign * dz, 4), lax.rem(iy + 4 + sign * dy, 4)
        return (idp, pz, py), pz * 4 + py

    def line(offset, sign=1):
        other = lax.rem(idp + 8 + sign * offset, 8)
        return (other, iz, iy), other

    def send(src, dst, send_sem, recv_sem, device):
        copy = pltpu.make_async_remote_copy(
            src_ref=src, dst_ref=dst, send_sem=send_sem, recv_sem=recv_sem,
            device_id=device, device_id_type=MESH,
        )
        return copy

    barrier = pltpu.get_barrier_semaphore()
    for offset in range(1, 16):
        pl.semaphore_signal(barrier, inc=1, device_id=plane(offset)[0], device_id_type=MESH)
    for offset in range(1, 8):
        pl.semaphore_signal(barrier, inc=1, device_id=line(offset)[0], device_id_type=MESH)

    loads = [
        pltpu.make_async_copy(src, dst, in_sem.at[i])
        for i, (src, dst) in enumerate([
            (x_hbm.at[0], x_ref), (w_hbm, w_ref), (db_hbm, db_ref), (rw_hbm, rw_ref),
            (rb_hbm, rb_ref), (cw_hbm, cw_ref), (cb_hbm, cb_ref),
        ])
    ]
    for load in loads:
        load.start()
    loads[0].wait()

    def fill(tile, carry):
        lanes = lanes_of(tile)
        blank = jnp.zeros((8, 128), f32)
        for row in range(ROWS):
            start = (row + 3) * PITCH + BLOCK0
            image[tile, start : start + COLS, :] = x_ref[row, :, lanes].astype(f32)
            image[tile, start - 8 : start, :] = blank
            image[tile, start + COLS : start + COLS + 8, :] = blank
            border[tile, row * 32 : row * 32 + 32, :] = jnp.zeros((32, 128), f32)
        for row in (0, 1, 2, 19, 20, 21):
            image[tile, row * PITCH : row * PITCH + 8, :] = blank
            image[tile, row * PITCH + PITCH - 8 : row * PITCH + PITCH, :] = blank
        for side in range(2):
            for col in range(3):
                at = BLOCK0 + col + (0 if side == 0 else COLS - 3)
                strip = image[tile, pl.ds(3 * PITCH + at, ROWS, stride=PITCH), :]
                csend[side, col, :, lanes] = strip.astype(bf16)
                for end in range(2):
                    ksend[end * 2 + side, col, :, lanes] = strip[8 * end : 8 * end + 8].astype(bf16)
        return carry

    def build_leaves(tile, group, present):
        rows = [
            image[tile, pl.ds(pl.multiple_of(group * 8 + row * PITCH, 8), 8), :] if row in present else None
            for row in range(ROWS + 6)
        ]
        for leaf, values in enumerate(twice(part_rows, rows)):
            for k, value in enumerate(values[:LEAF_ROWS]):
                if value is not None:
                    leaf_rows[tile, leaf, pl.ds(pl.multiple_of(group * 8 + k * PITCH, 8), 8), :] = value

    own_rows = range(3, ROWS + 3)
    own_leaves = twice(part_rows, [0.0 if row in own_rows else None for row in range(ROWS + 6)])

    def fill_leaves(tile, carry):
        for leaf, values in enumerate(own_leaves):
            for k, value in enumerate(values[:LEAF_ROWS]):
                if value is not None:
                    leaf_rows[tile, leaf, k * PITCH : k * PITCH + 8, :] = jnp.zeros((8, 128), f32)
                    leaf_rows[tile, leaf, k * PITCH + 72 : k * PITCH + 80, :] = jnp.zeros((8, 128), f32)

        def group_leaves(group, inner):
            build_leaves(tile, group, own_rows)
            return inner

        lax.fori_loop(1, 9, group_leaves, 0)
        return carry

    lax.fori_loop(0, TILES, fill, 0)
    loads[1].wait()
    loads[2].wait()

    def taps_of(lanes, b):
        return [jnp.broadcast_to(w_ref[a, pl.ds(b, 1), lanes], (8, 128)) for a in range(KERNEL)]

    def accumulate(acc, x, row, taps):
        for a in range(KERNEL):
            if 0 <= row - a < ROWS:
                acc[row - a] = acc[row - a] + x * taps[a]

    def conv_tile(tile, carry):
        lanes = lanes_of(tile)
        fill_leaves(tile, 0)
        taps = twice(part_taps, [w_ref[a, :, lanes] for a in range(KERNEL)])
        for leaf in range(LEAVES):
            for beta, tap in enumerate(taps[leaf]):
                leaf_taps[leaf, beta, 0:KERNEL, :] = tap
        outs = twice(part_outs, ROWS)
        filled = []
        for leaf in range(LEAVES):
            weights = [
                [jnp.broadcast_to(leaf_taps[leaf, beta, b : b + 1, :], (8, 128)) for b in range(KERNEL)]
                for beta in range(len(taps[leaf]))
            ]
            here = [k for k, v in enumerate(own_leaves[leaf][:LEAF_ROWS]) if v is not None]
            filled.append([
                True if any(i + beta in here for beta in range(len(taps[leaf]))) else None
                for i in range(outs[leaf])
            ])

            def pair(index, inner, leaf=leaf, weights=weights, here=here):
                for jg in (index * 2, index * 2 + 1):
                    acc = [None] * outs[leaf]
                    for b in range(KERNEL):
                        for k in here:
                            x = leaf_rows[tile, leaf, pl.ds(jg * 8 + (k * PITCH + BLOCK0 - 3 + b), 8), :]
                            for beta in range(len(weights)):
                                if 0 <= k - beta < outs[leaf]:
                                    acc[k - beta] = plus(acc[k - beta], x * weights[beta][b])
                    for i, value in enumerate(acc):
                        if value is not None:
                            leaf_values[leaf, pl.ds(pl.multiple_of(jg * 8 + i * COLS, 8), 8), :] = value
                return inner

            lax.fori_loop(0, COLS // 16, pair, 0)

        def combine(jg, inner):
            bias = jnp.broadcast_to(db_ref[lanes].reshape(1, 128), (8, 128))
            leaves = [
                [
                    leaf_values[leaf, pl.ds(pl.multiple_of(jg * 8 + i * COLS, 8), 8), :] if here else None
                    for i, here in enumerate(filled[leaf])
                ]
                for leaf in range(LEAVES)
            ]
            for row, value in enumerate(join_twice(leaves, ROWS)):
                cgrad[tile, pl.ds(pl.multiple_of(jg * 8 + row * COLS, 8), 8), :] = value + bias
            return inner

        lax.fori_loop(0, COLS // 8, combine, 0)
        return carry

    lax.fori_loop(0, 1, conv_tile, 0)
    pl.semaphore_wait(barrier, 22)

    up, down = lax.rem(iz + 3, 4), lax.rem(iz + 1, 4)
    left, right = lax.rem(iy + 3, 4), lax.rem(iy + 1, 4)
    strips = [
        (csend.at[1], hcol.at[0], (idp, iz, right)),
        (csend.at[0], hcol.at[1], (idp, iz, left)),
        (ksend.at[3], hcor.at[0], (idp, down, right)),
        (ksend.at[2], hcor.at[1], (idp, down, left)),
        (ksend.at[1], hcor.at[2], (idp, up, right)),
        (ksend.at[0], hcor.at[3], (idp, up, left)),
    ]
    for part in range(3):
        lanes = pl.ds(part * 256, 256)
        strips += [
            (x_ref.at[pl.ds(ROWS - 3, 3), :, lanes], hrow.at[0, :, :, lanes], (idp, down, iy)),
            (x_ref.at[pl.ds(0, 3), :, lanes], hrow.at[1, :, :, lanes], (idp, up, iy)),
        ]
    halo = [
        send(src, dst, halo_send.at[i], halo_recv.at[i], device)
        for i, (src, dst, device) in enumerate(strips)
    ]
    for copy in halo:
        copy.start()
    lax.fori_loop(1, TILES, conv_tile, 0)
    has_up, has_down, has_left, has_right = iz > 0, iz < 3, iy > 0, iy < 3

    def edges(tile, carry):
        lanes = lanes_of(tile)
        for end in range(2):
            has_row = (has_up, has_down)[end]
            for row in range(3):
                start = (row + 19 * end) * PITCH + BLOCK0
                strip = hrow[end, row, :, lanes].astype(f32)
                image[tile, start : start + COLS, :] = jnp.where(has_row, strip, 0.0)
        for side in range(2):
            has_col = (has_left, has_right)[side]
            for col in range(3):
                at = BLOCK0 - 3 + col + side * (COLS + 3)
                strip = hcol[side, col, :, lanes].astype(f32)
                strip = jnp.where(has_col, strip, 0.0)
                image[tile, pl.ds(3 * PITCH + at, ROWS, stride=PITCH), :] = strip
                spot = 21 + col if side == 0 else 8 + col
                border[tile, pl.ds(spot, ROWS, stride=32), :] = strip
                for end in range(2):
                    has_both = jnp.logical_and((has_up, has_down)[end], has_col)
                    strip = hcor[end * 2 + side, col, :, lanes].astype(f32)
                    strip = jnp.where(has_both, strip, 0.0)
                    strip = strip[5:8] if end == 0 else strip[0:3]
                    image[tile, pl.ds(19 * end * PITCH + at, 3, stride=PITCH), :] = strip

        def load_rows(start, rows):
            return {
                row: cgrad[tile, pl.ds(pl.multiple_of(start + row * COLS, 8), 8), :] for row in rows
            }

        def store_rows(start, acc):
            for row, value in acc.items():
                cgrad[tile, pl.ds(pl.multiple_of(start + row * COLS, 8), 8), :] = value

        def group(jg, inner):
            acc = load_rows(jg * 8, (0, 1, 2, 13, 14, 15))
            for b in range(KERNEL):
                taps = taps_of(lanes, b)
                for row in (0, 1, 2, 19, 20, 21):
                    x = image[tile, pl.ds(jg * 8 + (row * PITCH + BLOCK0 - 3 + b), 8), :]
                    accumulate(acc, x, row, taps)
            store_rows(jg * 8, acc)
            return inner

        lax.fori_loop(0, COLS // 8, group, 0)
        for side in range(2):
            acc = load_rows(side * (COLS - 8), range(ROWS))
            for b in (range(3), range(4, 7))[side]:
                taps = taps_of(lanes, b)
                for row in range(ROWS):
                    spot = row * 32 + (21 + b if side == 0 else b - 3)
                    accumulate(acc, border[tile, spot : spot + 8, :], row + 3, taps)
            store_rows(side * (COLS - 8), acc)
        conv[:, lanes] = cgrad[tile].astype(bf16)
        return carry

    for copy in halo[:6]:
        copy.wait_recv()
    for part in range(3):
        for copy in halo[6 + 2 * part : 8 + 2 * part]:
            copy.wait_recv()
        lax.fori_loop(2 * part, 2 * part + 2, edges, 0)
    for copy in halo:
        copy.wait_send()

    colsum[...] = jnp.zeros_like(colsum)
    loads[3].wait()
    loads[4].wait()
    for part in range(4):
        rows = pl.ds(part * 256, 256)
        value = jnp.dot(conv[rows, :], rw_ref[...], preferred_element_type=f32) + rb_ref[...].reshape(1, REDUCED)
        before[rows, :] = value
        active = (value / (1.0 + jnp.exp(-value))).astype(bf16)
        feat[rows, :] = active
        colsum[...] += jnp.sum(active.astype(f32), axis=0, keepdims=True)
    total = lax.dot_general(
        feat[...], feat[...], (((0,), (0,)), ((), ())), preferred_element_type=f32
    )
    own_mean = colsum[...] * (1.0 / (ROWS * COLS))
    wide = jnp.broadcast_to(own_mean, (REDUCED, REDUCED))
    centred = total * (1.0 / (ROWS * COLS)) - wide.T * wide
    gram[...] = centred.astype(bf16).reshape(16, 16, REDUCED)
    colsum[...] = own_mean
    crecv[me] = own_mean

    copies, means = [], []
    for offset in PLANE:
        device, index = plane(offset)
        copies.append(send(gram.at[index], grecv.at[offset], g_send.at[offset], g_recv.at[offset], device))
        means.append(send(colsum, crecv.at[me], c_send.at[offset], c_recv.at[offset], device))
    copies = means + copies
    for copy in copies:
        copy.start()

    def all_leaves(tile, carry):
        def group_leaves(group, inner):
            build_leaves(tile, group, range(ROWS + 6))
            return inner

        return lax.fori_loop(0, PITCH // 8, group_leaves, carry)

    lax.fori_loop(0, TILES, all_leaves, 0)
    leaf_sums[...] = jnp.zeros_like(leaf_sums)
    for offset in range(1, 16):
        _, source = plane(offset, -1)
        send(colsum, crecv.at[source], c_send.at[offset], c_recv.at[offset], plane(offset)[0]).wait_recv()
    mean = crecv[0]
    for index in range(1, 16):
        mean = mean + crecv[index]
    mean = mean * (1.0 / 16)
    between = split(crecv[...].reshape(16, REDUCED) - mean)
    square[...] = sum(
        lax.dot_general(a, b, (((0,), (0,)), ((), ())), preferred_element_type=f32)
        for a, b in ((between[0], between[0]), (between[0], between[1]), (between[1], between[0]))
    ).reshape(16, 16, REDUCED)
    for offset in PLANE:
        send(gram.at[0], grecv.at[offset], g_send.at[offset], g_recv.at[offset], plane(offset)[0]).wait_recv()
    mine = gram[me].astype(f32) + square[me]
    for offset in range(1, 16):
        mine = mine + grecv[offset].astype(f32)
    gfull[me] = (mine * (1.0 / 16)).astype(bf16)
    gathers = []
    for offset in PLANE:
        device, _ = plane(offset)
        gathers.append(send(gfull.at[me], gfull.at[me], a_send.at[offset], a_recv.at[offset], device))
    for copy in gathers:
        copy.start()
    for part in range(4):
        rows = pl.ds(part * 256, 256)
        value = before[rows, :]
        gate = 1.0 / (1.0 + jnp.exp(-value))
        before[rows, :] = gate * (1.0 + value * (1.0 - gate))
    for copy in copies:
        copy.wait_send()
    for offset in range(1, 16):
        _, source = plane(offset, -1)
        send(gfull.at[source], gfull.at[source], a_send.at[offset], a_recv.at[offset], plane(offset)[0]).wait_recv()
    for copy in gathers:
        copy.wait_send()

    sigma = gfull[...].reshape(REDUCED, REDUCED).astype(f32)
    row_id = lax.broadcasted_iota(jnp.int32, (REDUCED, REDUCED), 0)
    col_id = lax.broadcasted_iota(jnp.int32, (REDUCED, REDUCED), 1)
    diagonal = row_id == col_id
    identity15 = jnp.where(diagonal, 1.5, 0.0)
    trace = jnp.sum(
        jnp.sum(jnp.where(diagonal, sigma, 0.0), axis=0, keepdims=True), axis=1, keepdims=True
    ) + epsilon
    start = sigma / trace

    def keep(ref, step, value):
        high, low = split(value)
        ref[step, 0] = high
        ref[step, 1] = low

    def kept(ref, step):
        return ref[step, 0], ref[step, 1]

    keep(ys, 0, start)
    keep(ts, 0, identity15 - 0.5 * start)
    keep(ys, 1, products((kept(ys, 0), kept(ts, 0))))
    for step in range(1, NEWTON_STEPS):
        inverse = kept(ts, 0) if step == 1 else kept(zs, step)
        factor = identity15 - 0.5 * products((inverse, kept(ys, step)))
        keep(ts, step, factor)
        if step < NEWTON_STEPS - 1:
            keep(zs, step + 1, products((kept(ts, step), inverse)))
            keep(ys, step + 1, products((kept(ys, step), kept(ts, step))))
    last = products((kept(ys, NEWTON_STEPS - 1), kept(ts, NEWTON_STEPS - 1)))
    root_scale = jnp.sqrt(trace)
    root = root_scale * last
    root_out[idp] = root.astype(bf16)

    loads[5].wait()
    loads[6].wait()
    class_id = lax.broadcasted_iota(jnp.int32, (1, CLASSES), 1)
    logits = cb_ref[...].reshape(1, CLASSES)
    for k in range(CLASSES):
        weighted = jnp.sum(cw_ref[k].astype(f32) * root, axis=0, keepdims=True)
        logits = logits + jnp.where(class_id == k, jnp.sum(weighted, axis=1, keepdims=True), 0.0)
    onehot = jnp.where(class_id == lab_ref[0], 1.0, 0.0)
    softplus = jnp.maximum(logits, 0.0) + jnp.log(1.0 + jnp.exp(-jnp.abs(logits)))
    loss = jnp.sum(softplus - onehot * logits, axis=1, keepdims=True)
    logit_grad = (loss_scale / images) * (1.0 / (1.0 + jnp.exp(-logits)) - onehot)
    small_out[idp] = jnp.zeros((8, 128), f32)
    small_out[idp, 0:1, 0:CLASSES] = logit_grad
    small_out[idp, 1:2, :] = jnp.broadcast_to(loss, (1, 128))
    roots, smalls = [], []
    for offset in LINE:
        device, _ = line(offset)
        roots.append(send(root_out.at[idp], root_out.at[idp], x_send.at[offset], x_recv.at[offset], device))
        smalls.append(send(small_out.at[idp], small_out.at[idp], s_send.at[offset], s_recv.at[offset], device))
    for copy in smalls + roots:
        copy.start()

    root_grad = jnp.zeros((REDUCED, REDUCED), f32)
    for k in range(CLASSES):
        root_grad = root_grad + logit_grad[:, k : k + 1] * cw_ref[k].astype(f32)
    root_grad = 0.5 * (root_grad + root_grad.T)
    trace_grad = jnp.sum(jnp.sum(root_grad * last, axis=0, keepdims=True), axis=1, keepdims=True)
    trace_grad = trace_grad * 0.5 / root_scale
    seed = root_scale * root_grad
    d_y = split(seed)
    d_t = split(-0.5 * seed)
    d_z = d_t
    d_y = split(products((d_y, kept(ts, 0)), (kept(ys, 0), d_t)))
    for step in range(1, NEWTON_STEPS):
        inverse = kept(ts, 0) if step == 1 else kept(zs, step)
        d_t = split(-0.5 * products((d_z, kept(ys, step)), (inverse, d_y)))
        if step < NEWTON_STEPS - 1:
            d_z = split(products((d_t, inverse), (kept(ts, step), d_z)))
            d_y = split(products((d_y, kept(ts, step)), (kept(ys, step), d_t)))
    start_grad = products((d_y, kept(ts, NEWTON_STEPS - 1)), (kept(ys, NEWTON_STEPS - 1), d_t))
    start_grad = 0.5 * (start_grad + start_grad.T)
    start_value = ys[0, 0].astype(f32) + ys[0, 1].astype(f32)
    inner = jnp.sum(jnp.sum(start_grad * start_value, axis=0, keepdims=True), axis=1, keepdims=True)
    trace_grad = trace_grad - inner / trace
    sigma_grad = start_grad / trace + jnp.where(diagonal, trace_grad, 0.0)
    symmetric = (sigma_grad * (2.0 / count)).astype(bf16)
    sym[...] = symmetric
    mean_high, mean_low = split(jnp.broadcast_to(mean, (8, REDUCED)))
    mean_term[...] = jnp.dot(mean_high, symmetric, preferred_element_type=f32) + jnp.dot(
        mean_low, symmetric, preferred_element_type=f32
    )

    depth[...] = jnp.zeros_like(depth)
    bias_grad = jnp.zeros((1, REDUCED), f32)
    for part in range(4):
        rows = pl.ds(part * 256, 256)
        feat_grad = jnp.dot(feat[rows, :], sym[...], preferred_element_type=f32) - mean_term[0:1, :]
        pre_grad = (feat_grad * before[rows, :]).astype(bf16)
        pre[rows, :] = pre_grad
        bias_grad = bias_grad + jnp.sum(pre_grad.astype(f32), axis=0, keepdims=True)
        conv_grad = lax.dot_general(
            pre_grad, rw_ref[...], (((1,), (1,)), ((), ())), preferred_element_type=f32
        ).astype(bf16).astype(f32)
        for tile in range(TILES):
            cgrad[tile, rows, :] = conv_grad[:, tile * 128 : tile * 128 + 128]
    weight_grad = lax.dot_general(
        conv[...], pre[...], (((0,), (0,)), ((), ())), preferred_element_type=f32
    )
    wsend[...] = weight_grad.astype(bf16).reshape(16, 48, REDUCED)
    depth[0, 15:16, :] = bias_grad[:, 0:128]
    depth[1, 15:16, :] = bias_grad[:, 128:256]

    w_copies = []
    for offset in PLANE:
        device, index = plane(offset)
        w_copies.append(send(wsend.at[index], wrecv.at[offset], w_send.at[offset], w_recv.at[offset], device))
    for copy in w_copies:
        copy.start()

    def depth_tile(tile, carry):
        def grads(jg, inner):
            rows = [
                cgrad[tile, pl.ds(pl.multiple_of(jg * 8 + row * COLS, 8), 8), :] for row in range(ROWS)
            ]
            for leaf, values in enumerate(twice(part_taps, rows)):
                for k, value in enumerate(values):
                    leaf_values[leaf, pl.ds(pl.multiple_of(jg * 8 + k * COLS, 8), 8), :] = value
            return inner

        lax.fori_loop(0, COLS // 8, grads, 0)
        outs = twice(part_outs, KERNEL)
        zero = jnp.zeros((8, 128), f32)
        for leaf in range(LEAVES):
            count_out = outs[leaf]

            def group(jg, acc, leaf=leaf, count_out=count_out):
                acc = list(acc)
                taps = [
                    leaf_values[leaf, pl.ds(pl.multiple_of(jg * 8 + k * COLS, 8), 8), :] for k in range(4)
                ]
                for b in range(KERNEL):
                    for k in range(count_out + 3):
                        x = leaf_rows[tile, leaf, pl.ds(jg * 8 + (k * PITCH + BLOCK0 - 3 + b), 8), :]
                        for i in range(count_out):
                            if 0 <= k - i < 4:
                                acc[b * count_out + i] = acc[b * count_out + i] + x * taps[k - i]
                if leaf == 0:
                    acc[-1] = acc[-1] + ((taps[0] + taps[1]) + (taps[2] + taps[3]))
                return tuple(acc)

            sums = lax.fori_loop(0, COLS // 8, group, (zero,) * (KERNEL * count_out + (leaf == 0)))
            for b in range(KERNEL):
                for i in range(count_out):
                    leaf_sums[leaf, i, b : b + 1, :] = jnp.sum(sums[b * count_out + i], axis=0, keepdims=True)
            if leaf == 0:
                total = jnp.sum(sums[-1], axis=0, keepdims=True)
        leaves = [[leaf_sums[leaf, i] for i in range(outs[leaf])] for leaf in range(LEAVES)]
        for a, value in enumerate(join_twice(leaves, KERNEL)):
            depth[tile, a * 8 : a * 8 + 7, :] = value[0:7]
        depth[tile, 7:8, :] = total
        return carry

    lax.fori_loop(0, 5, depth_tile, 0)

    for copy in w_copies:
        copy.wait()
    w_sum = wsend[me].astype(f32)
    for offset in range(1, 16):
        w_sum = w_sum + wrecv[offset].astype(f32)
    wx[idp] = w_sum.astype(bf16)
    wx_copies = []
    for offset in LINE:
        device, _ = line(offset)
        wx_copies.append(send(wx.at[idp], wx.at[idp], wx_send.at[offset], wx_recv.at[offset], device))
    for copy in wx_copies:
        copy.start()
    lax.fori_loop(5, TILES, depth_tile, 0)

    for group8 in range(8):
        for half in range(2):
            for third in range(3):
                dsend[group8 * 2 + half, :, third * 128 : third * 128 + 128] = depth[
                    half * 3 + third, group8 * 8 : group8 * 8 + 8, :
                ].astype(bf16)
    d_copies = []
    for offset in PLANE:
        device, index = plane(offset)
        d_copies.append(send(dsend.at[index], drecv.at[offset], d_send.at[offset], d_recv.at[offset], device))
    for copy in d_copies:
        copy.start()

    for offset in range(1, 8):
        _, source = line(offset, -1)
        send(wx.at[source], wx.at[source], wx_send.at[offset], wx_recv.at[offset], line(offset)[0]).wait_recv()
    for copy in wx_copies:
        copy.wait_send()
    w_sum = wx[0].astype(f32)
    for index in range(1, 8):
        w_sum = w_sum + wx[index].astype(f32)
    wg_out[me] = w_sum.astype(bf16)
    wa_copies = []
    for offset in PLANE:
        device, _ = plane(offset)
        wa_copies.append(send(wg_out.at[me], wg_out.at[me], wa_send.at[offset], wa_recv.at[offset], device))
    for copy in wa_copies:
        copy.start()

    for offset in range(1, 8):
        _, source = line(offset, -1)
        device = line(offset)[0]
        send(root_out.at[source], root_out.at[source], x_send.at[offset], x_recv.at[offset], device).wait_recv()
        send(small_out.at[source], small_out.at[source], s_send.at[offset], s_recv.at[offset], device).wait_recv()
    for index in range(8):
        for k in range(CLASSES):
            factors[index * CLASSES + k] = jnp.broadcast_to(small_out[index, 0:1, k : k + 1], (8, 128))

    def class_rows(block, carry):
        rows = pl.ds(pl.multiple_of(block * 16, 16), 16)
        for half in range(2):
            lanes = slice(half * 128, half * 128 + 128)
            blocks = [root_out[index, rows, lanes].astype(f32).reshape(2, 8, 128) for index in range(8)]
            for k in range(CLASSES):
                total = blocks[0] * factors[k]
                for index in range(1, 8):
                    total = total + blocks[index] * factors[index * CLASSES + k]
                class_out[k, rows, lanes] = total.reshape(16, 128)
        return carry

    lax.fori_loop(0, 16, class_rows, 0)
    store = pltpu.make_async_copy(class_out, class_hbm, out_sem)
    store.start()
    for copy in d_copies:
        copy.wait()
    d_sum = dsend[me].astype(f32)
    for offset in range(1, 16):
        d_sum = d_sum + drecv[offset].astype(f32)
    dx[idp] = d_sum.astype(bf16)
    dx_copies = []
    for offset in LINE:
        device, _ = line(offset)
        dx_copies.append(send(dx.at[idp], dx.at[idp], dx_send.at[offset], dx_recv.at[offset], device))
    for copy in dx_copies:
        copy.start()
    for offset in range(1, 8):
        _, source = line(offset, -1)
        send(dx.at[source], dx.at[source], dx_send.at[offset], dx_recv.at[offset], line(offset)[0]).wait_recv()
    for copy in dx_copies:
        copy.wait_send()
    d_sum = dx[0].astype(f32)
    for index in range(1, 8):
        d_sum = d_sum + dx[index].astype(f32)
    dg_out[me] = d_sum.astype(bf16)
    da_copies = []
    for offset in PLANE:
        device, _ = plane(offset)
        da_copies.append(send(dg_out.at[me], dg_out.at[me], da_send.at[offset], da_recv.at[offset], device))
    for copy in da_copies:
        copy.start()
    for offset in range(1, 16):
        _, source = plane(offset, -1)
        device = plane(offset)[0]
        send(wg_out.at[source], wg_out.at[source], wa_send.at[offset], wa_recv.at[offset], device).wait_recv()
        send(dg_out.at[source], dg_out.at[source], da_send.at[offset], da_recv.at[offset], device).wait_recv()
    for copy in wa_copies + da_copies + roots + smalls:
        copy.wait_send()
    store.wait()


def finish_kernel(
    wg_hbm, dg_hbm, smalls_hbm, grads,
    loss_hbm, depth_hbm, depth_bias_hbm, weight_hbm, bias_hbm, class_weight, class_bias_hbm,
    wg, dg, smalls, buffer, loss, depth_grad, depth_bias, weight, bias, class_bias,
    load_sem, store_sem, class_in, class_out,
):
    loads = [
        pltpu.make_async_copy(src, dst, load_sem.at[i])
        for i, (src, dst) in enumerate([(wg_hbm, wg), (dg_hbm, dg), (smalls_hbm, smalls)])
    ]
    fetches = [pltpu.make_async_copy(grads.at[k], buffer.at[k], class_in.at[k]) for k in range(CLASSES)]
    stores = [pltpu.make_async_copy(buffer.at[k], class_weight.at[k], class_out.at[k]) for k in range(CLASSES)]
    results = [
        pltpu.make_async_copy(src, dst, store_sem.at[i])
        for i, (src, dst) in enumerate([
            (weight, weight_hbm), (depth_grad, depth_hbm), (depth_bias, depth_bias_hbm),
            (bias, bias_hbm), (class_bias, class_bias_hbm), (loss, loss_hbm),
        ])
    ]
    for load in loads + fetches:
        load.start()
    for load in loads:
        load.wait()
    weight[...] = wg[...].astype(f32).reshape(CHANNELS, REDUCED)
    results[0].start()
    for fetch, store in zip(fetches, stores):
        fetch.wait()
        store.start()
    for half in range(2):
        lanes = slice(half * 384, half * 384 + 384)
        for a in range(KERNEL):
            depth_grad[a, :, lanes] = dg[a * 2 + half, 0:7, :].astype(f32)
        depth_bias[lanes] = dg[half, 7:8, :].astype(f32).reshape(384)
    bias[...] = dg[2, 7:8, 0:REDUCED].astype(f32).reshape(REDUCED)
    small = smalls[0]
    for image in range(1, 8):
        small = small + smalls[image]
    class_bias[...] = small[0:1, 0:CLASSES].reshape(CLASSES)
    loss[...] = small[1:2, 0:1] * (1.0 / 8)
    for result in results[1:]:
        result.start()
    for copy in results + stores:
        copy.wait()


def body(
    features, depth_weight, depth_bias, reduce_weight, reduce_bias, class_weight, class_bias, labels
):
    vmem = pl.BlockSpec(memory_space=pltpu.VMEM)
    dma = pltpu.SemaphoreType.DMA
    hbm = pl.BlockSpec(memory_space=pltpu.HBM)
    smem = pl.BlockSpec(memory_space=pltpu.SMEM)
    scratch = [
        pltpu.VMEM((CLASSES, REDUCED, REDUCED), f32),
        pltpu.VMEM((ROWS, COLS, CHANNELS), bf16),
        pltpu.VMEM((KERNEL, KERNEL, CHANNELS), f32),
        pltpu.VMEM((CHANNELS,), f32),
        pltpu.VMEM((CHANNELS, REDUCED), bf16),
        pltpu.VMEM((REDUCED,), f32),
        pltpu.VMEM((CLASSES, REDUCED, REDUCED), bf16),
        pltpu.VMEM((CLASSES,), f32),
        pltpu.VMEM((8, REDUCED, REDUCED), bf16),
        pltpu.VMEM((8 * CLASSES, 8, 128), f32),
        pltpu.VMEM((TILES, LEAVES, LEAF_ROWS * PITCH, 128), f32),
        pltpu.VMEM((LEAVES, 4 * COLS, 128), f32),
        pltpu.VMEM((LEAVES, 2, 8, 128), f32),
        pltpu.VMEM((LEAVES, 2, 8, 128), f32),
        pltpu.VMEM((TILES, (ROWS + 6) * PITCH, 128), f32),
        pltpu.VMEM((TILES, ROWS * 32, 128), f32),
        pltpu.VMEM((ROWS * COLS, CHANNELS), bf16),
        pltpu.VMEM((ROWS * COLS, REDUCED), f32),
        pltpu.VMEM((ROWS * COLS, REDUCED), bf16),
        pltpu.VMEM((ROWS * COLS, REDUCED), bf16),
        pltpu.VMEM((TILES, ROWS * COLS, 128), f32),
        pltpu.VMEM((2, 3, 16, CHANNELS), bf16),
        pltpu.VMEM((4, 3, 8, CHANNELS), bf16),
        pltpu.VMEM((2, 3, COLS, CHANNELS), bf16),
        pltpu.VMEM((2, 3, 16, CHANNELS), bf16),
        pltpu.VMEM((4, 3, 8, CHANNELS), bf16),
        pltpu.VMEM((16, 16, REDUCED), bf16),
        pltpu.VMEM((16, 16, REDUCED), bf16),
        pltpu.VMEM((16, 16, REDUCED), f32),
        pltpu.VMEM((16, 16, REDUCED), bf16),
        pltpu.VMEM((1, REDUCED), f32),
        pltpu.VMEM((16, 1, REDUCED), f32),
        pltpu.VMEM((NEWTON_STEPS, 2, REDUCED, REDUCED), bf16),
        pltpu.VMEM((NEWTON_STEPS, 2, REDUCED, REDUCED), bf16),
        pltpu.VMEM((NEWTON_STEPS, 2, REDUCED, REDUCED), bf16),
        pltpu.VMEM((REDUCED, REDUCED), bf16),
        pltpu.VMEM((8, REDUCED), f32),
        pltpu.VMEM((16, 48, REDUCED), bf16),
        pltpu.VMEM((16, 48, REDUCED), bf16),
        pltpu.VMEM((8, 48, REDUCED), bf16),
        pltpu.VMEM((TILES, 64, 128), f32),
        pltpu.VMEM((16, 8, 384), bf16),
        pltpu.VMEM((16, 8, 384), bf16),
        pltpu.VMEM((8, 8, 384), bf16),
        dma((7,)), dma, dma((12,)), dma((12,)),
        dma((16,)), dma((16,)), dma((16,)), dma((16,)), dma((16,)), dma((16,)),
        dma((8,)), dma((8,)), dma((8,)), dma((8,)),
        dma((16,)), dma((16,)), dma((8,)), dma((8,)), dma((16,)), dma((16,)),
        dma((16,)), dma((16,)), dma((8,)), dma((8,)), dma((16,)), dma((16,)),
    ]
    partial = pl.pallas_call(
        main_kernel,
        out_shape=(
            jax.ShapeDtypeStruct((16, 48, REDUCED), bf16),
            jax.ShapeDtypeStruct((16, 8, 384), bf16),
            jax.ShapeDtypeStruct((8, 8, 128), f32),
            jax.ShapeDtypeStruct((CLASSES, REDUCED, REDUCED), f32),
        ),
        in_specs=[hbm] * 7 + [smem],
        out_specs=(vmem,) * 3 + (hbm,),
        scratch_shapes=scratch,
        compiler_params=pltpu.CompilerParams(
            collective_id=0, has_side_effects=True, vmem_limit_bytes=63 << 20
        ),
        name="pooling_step",
    )(
        features, depth_weight, depth_bias, reduce_weight, reduce_bias, class_weight, class_bias, labels
    )
    loss, *grads = pl.pallas_call(
        finish_kernel,
        out_shape=(
            jax.ShapeDtypeStruct((1, 1), f32),
            jax.ShapeDtypeStruct((KERNEL, KERNEL, CHANNELS), f32),
            jax.ShapeDtypeStruct((CHANNELS,), f32),
            jax.ShapeDtypeStruct((CHANNELS, REDUCED), f32),
            jax.ShapeDtypeStruct((REDUCED,), f32),
            jax.ShapeDtypeStruct((CLASSES, REDUCED, REDUCED), f32),
            jax.ShapeDtypeStruct((CLASSES,), f32),
        ),
        in_specs=[hbm] * 4,
        out_specs=(hbm,) * 7,
        scratch_shapes=[
            pltpu.VMEM((16, 48, REDUCED), bf16), pltpu.VMEM((16, 8, 384), bf16), pltpu.VMEM((8, 8, 128), f32),
            pltpu.VMEM((CLASSES, REDUCED, REDUCED), f32), pltpu.VMEM((1, 1), f32),
            pltpu.VMEM((KERNEL, KERNEL, CHANNELS), f32), pltpu.VMEM((CHANNELS,), f32),
            pltpu.VMEM((CHANNELS, REDUCED), f32), pltpu.VMEM((REDUCED,), f32), pltpu.VMEM((CLASSES,), f32),
            dma((3,)), dma((6,)), dma((CLASSES,)), dma((CLASSES,)),
        ],
        compiler_params=pltpu.CompilerParams(vmem_limit_bytes=63 << 20),
        name="outputs",
    )(*partial)
    return (loss.reshape(()), *grads)


def solution(mesh):
    placed = (P("dp", "sy", "sx", None), P(), P(), P(), P(), P(), P(), P("dp"))
    return jax.shard_map(
        body,
        mesh=mesh,
        in_specs=placed,
        out_specs=(P(), P(), P(), P(), P(), P(), P()),
        check_vma=False,
    )
```

```python
import functools

import jax
import jax.numpy as jnp
from jax import lax
from jax.experimental import pallas as pl
from jax.experimental.pallas import tpu as pltpu
from jax.sharding import PartitionSpec as P

MESH = pl.DeviceIdType.MESH
KERNEL = 7
NEWTON_STEPS = 5
ROWS = 16
COLS = 64
TILES = 6
CHANNELS = 768
REDUCED = 256
CLASSES = 10
PITCH = 80
BLOCK0 = 8
PLANE = sorted(range(1, 16), key=lambda o: -(min(o // 4, 4 - o // 4) + min(o % 4, 4 - o % 4)))
LINE = sorted(range(1, 8), key=lambda o: -min(o, 8 - o))
epsilon = 1e-05
loss_scale = 64.0
f32 = jnp.float32
bf16 = jnp.bfloat16


def lanes_of(tile):
    return pl.ds(pl.multiple_of(tile * 128, 128), 128)


def split(value):
    high = value.astype(bf16)
    return high, (value - high.astype(f32)).astype(bf16)


def plus(a, b):
    return b if a is None else a if b is None else a + b


def minus(a, b):
    return a if b is None else 0.0 - b if a is None else a - b


def part_rows(rows):
    even, odd = rows[0::2], rows[1::2]
    return [
        odd,
        [minus(a, b) for a, b in zip(even, odd)],
        [minus(a, b) for a, b in zip(even[1:], odd)],
    ]


def part_taps(taps):
    even, odd = taps[0::2], taps[1::2]
    both = [plus(a, b) for a, b in zip(even, odd + [None] * (len(even) - len(odd)))]
    return [both, even, odd]


def part_outs(count):
    return [(count + 1) // 2, (count + 1) // 2, count // 2]


def join(parts, count):
    shared, first, second = parts
    return [plus(shared[i // 2], (first, second)[i % 2][i // 2]) for i in range(count)]


def twice(part, value):
    return [leaf for half in part(value) for leaf in part(half)]


def join_twice(leaves, count):
    halves = part_outs(count)
    return join([join(leaves[3 * i : 3 * i + 3], halves[i]) for i in range(3)], count)


LEAF_ROWS = 5
LEAVES = 9


def products(*pairs):
    left, right = [], []
    for (a_high, a_low), (b_high, b_low) in pairs:
        left += [a_low, a_high, a_high]
        right += [b_high, b_low, b_high]
    return jnp.dot(
        jnp.concatenate(left, axis=1), jnp.concatenate(right, axis=0), preferred_element_type=f32
    )


def main_kernel(
    x_hbm, w_hbm, db_hbm, rw_hbm, rb_hbm, cw_hbm, cb_hbm, lab_ref,
    wg_out, dg_out, small_out, class_hbm,
    class_out,
    x_ref, w_ref, db_ref, rw_ref, rb_ref, cw_ref, cb_ref, root_out, factors,
    leaf_rows, leaf_values, leaf_taps, leaf_sums, image, border, conv, before, feat, pre, cgrad,
    csend, ksend, hrow, hcol, hcor,
    gram, grecv, square, gfull, colsum, crecv,
    ys, zs, ts, sym, mean_term,
    wsend, wrecv, wx, depth, dsend, drecv, dx,
    in_sem, out_sem, halo_send, halo_recv, g_send, g_recv, c_send, c_recv, a_send, a_recv,
    x_send, x_recv, s_send, s_recv, w_send, w_recv, wx_send, wx_recv, wa_send, wa_recv,
    d_send, d_recv, dx_send, dx_recv, da_send, da_recv,
):
    idp, iz, iy = lax.axis_index("dp"), lax.axis_index("sy"), lax.axis_index("sx")
    images = 8
    count = ROWS * COLS * 16
    me = iz * 4 + iy

    def plane(offset, sign=1):
        dz, dy = divmod(offset, 4)
        pz, py = lax.rem(iz + 4 + sign * dz, 4), lax.rem(iy + 4 + sign * dy, 4)
        return (idp, pz, py), pz * 4 + py

    def line(offset, sign=1):
        other = lax.rem(idp + 8 + sign * offset, 8)
        return (other, iz, iy), other

    def send(src, dst, send_sem, recv_sem, device):
        copy = pltpu.make_async_remote_copy(
            src_ref=src, dst_ref=dst, send_sem=send_sem, recv_sem=recv_sem,
            device_id=device, device_id_type=MESH,
        )
        return copy

    barrier = pltpu.get_barrier_semaphore()
    for offset in range(1, 16):
        pl.semaphore_signal(barrier, inc=1, device_id=plane(offset)[0], device_id_type=MESH)
    for offset in range(1, 8):
        pl.semaphore_signal(barrier, inc=1, device_id=line(offset)[0], device_id_type=MESH)

    loads = [
        pltpu.make_async_copy(src, dst, in_sem.at[i])
        for i, (src, dst) in enumerate([
            (x_hbm.at[0], x_ref), (w_hbm, w_ref), (db_hbm, db_ref), (rw_hbm, rw_ref),
            (rb_hbm, rb_ref), (cw_hbm, cw_ref), (cb_hbm, cb_ref),
        ])
    ]
    for load in loads:
        load.start()
    loads[0].wait()

    def fill(tile, carry):
        lanes = lanes_of(tile)
        blank = jnp.zeros((8, 128), f32)
        for row in range(ROWS):
            start = (row + 3) * PITCH + BLOCK0
            image[tile, start : start + COLS, :] = x_ref[row, :, lanes].astype(f32)
            image[tile, start - 8 : start, :] = blank
            image[tile, start + COLS : start + COLS + 8, :] = blank
            border[tile, row * 32 : row * 32 + 32, :] = jnp.zeros((32, 128), f32)
        for row in (0, 1, 2, 19, 20, 21):
            image[tile, row * PITCH : row * PITCH + 8, :] = blank
            image[tile, row * PITCH + PITCH - 8 : row * PITCH + PITCH, :] = blank
        for side in range(2):
            for col in range(3):
                at = BLOCK0 + col + (0 if side == 0 else COLS - 3)
                strip = image[tile, pl.ds(3 * PITCH + at, ROWS, stride=PITCH), :]
                csend[side, col, :, lanes] = strip.astype(bf16)
                for end in range(2):
                    ksend[end * 2 + side, col, :, lanes] = strip[8 * end : 8 * end + 8].astype(bf16)
        return carry

    def build_leaves(tile, group, present):
        rows = [
            image[tile, pl.ds(pl.multiple_of(group * 8 + row * PITCH, 8), 8), :] if row in present else None
            for row in range(ROWS + 6)
        ]
        for leaf, values in enumerate(twice(part_rows, rows)):
            for k, value in enumerate(values[:LEAF_ROWS]):
                if value is not None:
                    leaf_rows[tile, leaf, pl.ds(pl.multiple_of(group * 8 + k * PITCH, 8), 8), :] = value

    own_rows = range(3, ROWS + 3)
    own_leaves = twice(part_rows, [0.0 if row in own_rows else None for row in range(ROWS + 6)])

    def fill_leaves(tile, carry):
        for leaf, values in enumerate(own_leaves):
            for k, value in enumerate(values[:LEAF_ROWS]):
                if value is not None:
                    leaf_rows[tile, leaf, k * PITCH : k * PITCH + 8, :] = jnp.zeros((8, 128), f32)
                    leaf_rows[tile, leaf, k * PITCH + 72 : k * PITCH + 80, :] = jnp.zeros((8, 128), f32)

        def group_leaves(group, inner):
            build_leaves(tile, group, own_rows)
            return inner

        lax.fori_loop(1, 9, group_leaves, 0)
        return carry

    lax.fori_loop(0, TILES, fill, 0)
    loads[1].wait()
    loads[2].wait()

    def taps_of(lanes, b):
        return [jnp.broadcast_to(w_ref[a, pl.ds(b, 1), lanes], (8, 128)) for a in range(KERNEL)]

    def accumulate(acc, x, row, taps):
        for a in range(KERNEL):
            if 0 <= row - a < ROWS:
                acc[row - a] = acc[row - a] + x * taps[a]

    def conv_tile(tile, carry):
        lanes = lanes_of(tile)
        fill_leaves(tile, 0)
        taps = twice(part_taps, [w_ref[a, :, lanes] for a in range(KERNEL)])
        for leaf in range(LEAVES):
            for beta, tap in enumerate(taps[leaf]):
                leaf_taps[leaf, beta, 0:KERNEL, :] = tap
        outs = twice(part_outs, ROWS)
        filled = []
        for leaf in range(LEAVES):
            weights = [
                [jnp.broadcast_to(leaf_taps[leaf, beta, b : b + 1, :], (8, 128)) for b in range(KERNEL)]
                for beta in range(len(taps[leaf]))
            ]
            here = [k for k, v in enumerate(own_leaves[leaf][:LEAF_ROWS]) if v is not None]
            filled.append([
                True if any(i + beta in here for beta in range(len(taps[leaf]))) else None
                for i in range(outs[leaf])
            ])

            def pair(index, inner, leaf=leaf, weights=weights, here=here):
                for jg in (index * 2, index * 2 + 1):
                    acc = [None] * outs[leaf]
                    for b in range(KERNEL):
                        for k in here:
                            x = leaf_rows[tile, leaf, pl.ds(jg * 8 + (k * PITCH + BLOCK0 - 3 + b), 8), :]
                            for beta in range(len(weights)):
                                if 0 <= k - beta < outs[leaf]:
                                    acc[k - beta] = plus(acc[k - beta], x * weights[beta][b])
                    for i, value in enumerate(acc):
                        if value is not None:
                            leaf_values[leaf, pl.ds(pl.multiple_of(jg * 8 + i * COLS, 8), 8), :] = value
                return inner

            lax.fori_loop(0, COLS // 16, pair, 0)

        def combine(jg, inner):
            bias = jnp.broadcast_to(db_ref[lanes].reshape(1, 128), (8, 128))
            leaves = [
                [
                    leaf_values[leaf, pl.ds(pl.multiple_of(jg * 8 + i * COLS, 8), 8), :] if here else None
                    for i, here in enumerate(filled[leaf])
                ]
                for leaf in range(LEAVES)
            ]
            for row, value in enumerate(join_twice(leaves, ROWS)):
                cgrad[tile, pl.ds(pl.multiple_of(jg * 8 + row * COLS, 8), 8), :] = value + bias
            return inner

        lax.fori_loop(0, COLS // 8, combine, 0)
        return carry

    lax.fori_loop(0, 1, conv_tile, 0)
    pl.semaphore_wait(barrier, 22)

    up, down = lax.rem(iz + 3, 4), lax.rem(iz + 1, 4)
    left, right = lax.rem(iy + 3, 4), lax.rem(iy + 1, 4)
    strips = [
        (csend.at[1], hcol.at[0], (idp, iz, right)),
        (csend.at[0], hcol.at[1], (idp, iz, left)),
        (ksend.at[3], hcor.at[0], (idp, down, right)),
        (ksend.at[2], hcor.at[1], (idp, down, left)),
        (ksend.at[1], hcor.at[2], (idp, up, right)),
        (ksend.at[0], hcor.at[3], (idp, up, left)),
    ]
    for part in range(3):
        lanes = pl.ds(part * 256, 256)
        strips += [
            (x_ref.at[pl.ds(ROWS - 3, 3), :, lanes], hrow.at[0, :, :, lanes], (idp, down, iy)),
            (x_ref.at[pl.ds(0, 3), :, lanes], hrow.at[1, :, :, lanes], (idp, up, iy)),
        ]
    halo = [
        send(src, dst, halo_send.at[i], halo_recv.at[i], device)
        for i, (src, dst, device) in enumerate(strips)
    ]
    for copy in halo:
        copy.start()
    lax.fori_loop(1, TILES, conv_tile, 0)
    has_up, has_down, has_left, has_right = iz > 0, iz < 3, iy > 0, iy < 3

    def edges(tile, carry):
        lanes = lanes_of(tile)
        for end in range(2):
            has_row = (has_up, has_down)[end]
            for row in range(3):
                start = (row + 19 * end) * PITCH + BLOCK0
                strip = hrow[end, row, :, lanes].astype(f32)
                image[tile, start : start + COLS, :] = jnp.where(has_row, strip, 0.0)
        for side in range(2):
            has_col = (has_left, has_right)[side]
            for col in range(3):
                at = BLOCK0 - 3 + col + side * (COLS + 3)
                strip = hcol[side, col, :, lanes].astype(f32)
                strip = jnp.where(has_col, strip, 0.0)
                image[tile, pl.ds(3 * PITCH + at, ROWS, stride=PITCH), :] = strip
                spot = 21 + col if side == 0 else 8 + col
                border[tile, pl.ds(spot, ROWS, stride=32), :] = strip
                for end in range(2):
                    has_both = jnp.logical_and((has_up, has_down)[end], has_col)
                    strip = hcor[end * 2 + side, col, :, lanes].astype(f32)
                    strip = jnp.where(has_both, strip, 0.0)
                    strip = strip[5:8] if end == 0 else strip[0:3]
                    image[tile, pl.ds(19 * end * PITCH + at, 3, stride=PITCH), :] = strip

        def load_rows(start, rows):
            return {
                row: cgrad[tile, pl.ds(pl.multiple_of(start + row * COLS, 8), 8), :] for row in rows
            }

        def store_rows(start, acc):
            for row, value in acc.items():
                cgrad[tile, pl.ds(pl.multiple_of(start + row * COLS, 8), 8), :] = value

        def group(jg, inner):
            acc = load_rows(jg * 8, (0, 1, 2, 13, 14, 15))
            for b in range(KERNEL):
                taps = taps_of(lanes, b)
                for row in (0, 1, 2, 19, 20, 21):
                    x = image[tile, pl.ds(jg * 8 + (row * PITCH + BLOCK0 - 3 + b), 8), :]
                    accumulate(acc, x, row, taps)
            store_rows(jg * 8, acc)
            return inner

        lax.fori_loop(0, COLS // 8, group, 0)
        for side in range(2):
            acc = load_rows(side * (COLS - 8), range(ROWS))
            for b in (range(3), range(4, 7))[side]:
                taps = taps_of(lanes, b)
                for row in range(ROWS):
                    spot = row * 32 + (21 + b if side == 0 else b - 3)
                    accumulate(acc, border[tile, spot : spot + 8, :], row + 3, taps)
            store_rows(side * (COLS - 8), acc)
        conv[:, lanes] = cgrad[tile].astype(bf16)
        return carry

    for copy in halo[:6]:
        copy.wait_recv()
    for part in range(3):
        for copy in halo[6 + 2 * part : 8 + 2 * part]:
            copy.wait_recv()
        lax.fori_loop(2 * part, 2 * part + 2, edges, 0)
    for copy in halo:
        copy.wait_send()

    colsum[...] = jnp.zeros_like(colsum)
    loads[3].wait()
    loads[4].wait()
    for part in range(4):
        rows = pl.ds(part * 256, 256)
        value = jnp.dot(conv[rows, :], rw_ref[...], preferred_element_type=f32) + rb_ref[...].reshape(1, REDUCED)
        before[rows, :] = value
        active = (value / (1.0 + jnp.exp(-value))).astype(bf16)
        feat[rows, :] = active
        colsum[...] += jnp.sum(active.astype(f32), axis=0, keepdims=True)
    total = lax.dot_general(
        feat[...], feat[...], (((0,), (0,)), ((), ())), preferred_element_type=f32
    )
    own_mean = colsum[...] * (1.0 / (ROWS * COLS))
    wide = jnp.broadcast_to(own_mean, (REDUCED, REDUCED))
    centred = total * (1.0 / (ROWS * COLS)) - wide.T * wide
    gram[...] = centred.astype(bf16).reshape(16, 16, REDUCED)
    colsum[...] = own_mean
    crecv[me] = own_mean

    copies, means = [], []
    for offset in PLANE:
        device, index = plane(offset)
        copies.append(send(gram.at[index], grecv.at[offset], g_send.at[offset], g_recv.at[offset], device))
        means.append(send(colsum, crecv.at[me], c_send.at[offset], c_recv.at[offset], device))
    copies = means + copies
    for copy in copies:
        copy.start()

    def all_leaves(tile, carry):
        def group_leaves(group, inner):
            build_leaves(tile, group, range(ROWS + 6))
            return inner

        return lax.fori_loop(0, PITCH // 8, group_leaves, carry)

    lax.fori_loop(0, TILES, all_leaves, 0)
    leaf_sums[...] = jnp.zeros_like(leaf_sums)
    for offset in range(1, 16):
        _, source = plane(offset, -1)
        send(colsum, crecv.at[source], c_send.at[offset], c_recv.at[offset], plane(offset)[0]).wait_recv()
    mean = crecv[0]
    for index in range(1, 16):
        mean = mean + crecv[index]
    mean = mean * (1.0 / 16)
    between = split(crecv[...].reshape(16, REDUCED) - mean)
    square[...] = sum(
        lax.dot_general(a, b, (((0,), (0,)), ((), ())), preferred_element_type=f32)
        for a, b in ((between[0], between[0]), (between[0], between[1]), (between[1], between[0]))
    ).reshape(16, 16, REDUCED)
    for offset in PLANE:
        send(gram.at[0], grecv.at[offset], g_send.at[offset], g_recv.at[offset], plane(offset)[0]).wait_recv()
    mine = gram[me].astype(f32) + square[me]
    for offset in range(1, 16):
        mine = mine + grecv[offset].astype(f32)
    gfull[me] = (mine * (1.0 / 16)).astype(bf16)
    gathers = []
    for offset in PLANE:
        device, _ = plane(offset)
        gathers.append(send(gfull.at[me], gfull.at[me], a_send.at[offset], a_recv.at[offset], device))
    for copy in gathers:
        copy.start()
    for part in range(4):
        rows = pl.ds(part * 256, 256)
        value = before[rows, :]
        gate = 1.0 / (1.0 + jnp.exp(-value))
        before[rows, :] = gate * (1.0 + value * (1.0 - gate))
    for copy in copies:
        copy.wait_send()
    for offset in range(1, 16):
        _, source = plane(offset, -1)
        send(gfull.at[source], gfull.at[source], a_send.at[offset], a_recv.at[offset], plane(offset)[0]).wait_recv()
    for copy in gathers:
        copy.wait_send()

    sigma = gfull[...].reshape(REDUCED, REDUCED).astype(f32)
    row_id = lax.broadcasted_iota(jnp.int32, (REDUCED, REDUCED), 0)
    col_id = lax.broadcasted_iota(jnp.int32, (REDUCED, REDUCED), 1)
    diagonal = row_id == col_id
    identity15 = jnp.where(diagonal, 1.5, 0.0)
    trace = jnp.sum(
        jnp.sum(jnp.where(diagonal, sigma, 0.0), axis=0, keepdims=True), axis=1, keepdims=True
    ) + epsilon
    start = sigma / trace

    def keep(ref, step, value):
        high, low = split(value)
        ref[step, 0] = high
        ref[step, 1] = low

    def kept(ref, step):
        return ref[step, 0], ref[step, 1]

    keep(ys, 0, start)
    keep(ts, 0, identity15 - 0.5 * start)
    keep(ys, 1, products((kept(ys, 0), kept(ts, 0))))
    for step in range(1, NEWTON_STEPS):
        inverse = kept(ts, 0) if step == 1 else kept(zs, step)
        factor = identity15 - 0.5 * products((inverse, kept(ys, step)))
        keep(ts, step, factor)
        if step < NEWTON_STEPS - 1:
            keep(zs, step + 1, products((kept(ts, step), inverse)))
            keep(ys, step + 1, products((kept(ys, step), kept(ts, step))))
    last = products((kept(ys, NEWTON_STEPS - 1), kept(ts, NEWTON_STEPS - 1)))
    root_scale = jnp.sqrt(trace)
    root = root_scale * last
    root_out[idp] = root.astype(bf16)

    loads[5].wait()
    loads[6].wait()
    class_id = lax.broadcasted_iota(jnp.int32, (1, CLASSES), 1)
    logits = cb_ref[...].reshape(1, CLASSES)
    for k in range(CLASSES):
        weighted = jnp.sum(cw_ref[k].astype(f32) * root, axis=0, keepdims=True)
        logits = logits + jnp.where(class_id == k, jnp.sum(weighted, axis=1, keepdims=True), 0.0)
    onehot = jnp.where(class_id == lab_ref[0], 1.0, 0.0)
    softplus = jnp.maximum(logits, 0.0) + jnp.log(1.0 + jnp.exp(-jnp.abs(logits)))
    loss = jnp.sum(softplus - onehot * logits, axis=1, keepdims=True)
    logit_grad = (loss_scale / images) * (1.0 / (1.0 + jnp.exp(-logits)) - onehot)
    small_out[idp] = jnp.zeros((8, 128), f32)
    small_out[idp, 0:1, 0:CLASSES] = logit_grad
    small_out[idp, 1:2, :] = jnp.broadcast_to(loss, (1, 128))
    roots, smalls = [], []
    for offset in LINE:
        device, _ = line(offset)
        roots.append(send(root_out.at[idp], root_out.at[idp], x_send.at[offset], x_recv.at[offset], device))
        smalls.append(send(small_out.at[idp], small_out.at[idp], s_send.at[offset], s_recv.at[offset], device))
    for copy in smalls + roots:
        copy.start()

    root_grad = jnp.zeros((REDUCED, REDUCED), f32)
    for k in range(CLASSES):
        root_grad = root_grad + logit_grad[:, k : k + 1] * cw_ref[k].astype(f32)
    root_grad = 0.5 * (root_grad + root_grad.T)
    trace_grad = jnp.sum(jnp.sum(root_grad * last, axis=0, keepdims=True), axis=1, keepdims=True)
    trace_grad = trace_grad * 0.5 / root_scale
    seed = root_scale * root_grad
    d_y = split(seed)
    d_t = split(-0.5 * seed)
    d_z = d_t
    d_y = split(products((d_y, kept(ts, 0)), (kept(ys, 0), d_t)))
    for step in range(1, NEWTON_STEPS):
        inverse = kept(ts, 0) if step == 1 else kept(zs, step)
        d_t = split(-0.5 * products((d_z, kept(ys, step)), (inverse, d_y)))
        if step < NEWTON_STEPS - 1:
            d_z = split(products((d_t, inverse), (kept(ts, step), d_z)))
            d_y = split(products((d_y, kept(ts, step)), (kept(ys, step), d_t)))
    start_grad = products((d_y, kept(ts, NEWTON_STEPS - 1)), (kept(ys, NEWTON_STEPS - 1), d_t))
    start_grad = 0.5 * (start_grad + start_grad.T)
    start_value = ys[0, 0].astype(f32) + ys[0, 1].astype(f32)
    inner = jnp.sum(jnp.sum(start_grad * start_value, axis=0, keepdims=True), axis=1, keepdims=True)
    trace_grad = trace_grad - inner / trace
    sigma_grad = start_grad / trace + jnp.where(diagonal, trace_grad, 0.0)
    symmetric = (sigma_grad * (2.0 / count)).astype(bf16)
    sym[...] = symmetric
    mean_high, mean_low = split(jnp.broadcast_to(mean, (8, REDUCED)))
    mean_term[...] = jnp.dot(mean_high, symmetric, preferred_element_type=f32) + jnp.dot(
        mean_low, symmetric, preferred_element_type=f32
    )

    depth[...] = jnp.zeros_like(depth)
    bias_grad = jnp.zeros((1, REDUCED), f32)
    for part in range(4):
        rows = pl.ds(part * 256, 256)
        feat_grad = jnp.dot(feat[rows, :], sym[...], preferred_element_type=f32) - mean_term[0:1, :]
        pre_grad = (feat_grad * before[rows, :]).astype(bf16)
        pre[rows, :] = pre_grad
        bias_grad = bias_grad + jnp.sum(pre_grad.astype(f32), axis=0, keepdims=True)
        conv_grad = lax.dot_general(
            pre_grad, rw_ref[...], (((1,), (1,)), ((), ())), preferred_element_type=f32
        ).astype(bf16).astype(f32)
        for tile in range(TILES):
            cgrad[tile, rows, :] = conv_grad[:, tile * 128 : tile * 128 + 128]
    weight_grad = lax.dot_general(
        conv[...], pre[...], (((0,), (0,)), ((), ())), preferred_element_type=f32
    )
    wsend[...] = weight_grad.astype(bf16).reshape(16, 48, REDUCED)
    depth[0, 15:16, :] = bias_grad[:, 0:128]
    depth[1, 15:16, :] = bias_grad[:, 128:256]

    w_copies = []
    for offset in PLANE:
        device, index = plane(offset)
        w_copies.append(send(wsend.at[index], wrecv.at[offset], w_send.at[offset], w_recv.at[offset], device))
    for copy in w_copies:
        copy.start()

    def depth_tile(tile, carry):
        def grads(jg, inner):
            rows = [
                cgrad[tile, pl.ds(pl.multiple_of(jg * 8 + row * COLS, 8), 8), :] for row in range(ROWS)
            ]
            for leaf, values in enumerate(twice(part_taps, rows)):
                for k, value in enumerate(values):
                    leaf_values[leaf, pl.ds(pl.multiple_of(jg * 8 + k * COLS, 8), 8), :] = value
            return inner

        lax.fori_loop(0, COLS // 8, grads, 0)
        outs = twice(part_outs, KERNEL)
        zero = jnp.zeros((8, 128), f32)
        for leaf in range(LEAVES):
            count_out = outs[leaf]

            def group(jg, acc, leaf=leaf, count_out=count_out):
                acc = list(acc)
                taps = [
                    leaf_values[leaf, pl.ds(pl.multiple_of(jg * 8 + k * COLS, 8), 8), :] for k in range(4)
                ]
                for b in range(KERNEL):
                    for k in range(count_out + 3):
                        x = leaf_rows[tile, leaf, pl.ds(jg * 8 + (k * PITCH + BLOCK0 - 3 + b), 8), :]
                        for i in range(count_out):
                            if 0 <= k - i < 4:
                                acc[b * count_out + i] = acc[b * count_out + i] + x * taps[k - i]
                if leaf == 0:
                    acc[-1] = acc[-1] + ((taps[0] + taps[1]) + (taps[2] + taps[3]))
                return tuple(acc)

            sums = lax.fori_loop(0, COLS // 8, group, (zero,) * (KERNEL * count_out + (leaf == 0)))
            for b in range(KERNEL):
                for i in range(count_out):
                    leaf_sums[leaf, i, b : b + 1, :] = jnp.sum(sums[b * count_out + i], axis=0, keepdims=True)
            if leaf == 0:
                total = jnp.sum(sums[-1], axis=0, keepdims=True)
        leaves = [[leaf_sums[leaf, i] for i in range(outs[leaf])] for leaf in range(LEAVES)]
        for a, value in enumerate(join_twice(leaves, KERNEL)):
            depth[tile, a * 8 : a * 8 + 7, :] = value[0:7]
        depth[tile, 7:8, :] = total
        return carry

    lax.fori_loop(0, 5, depth_tile, 0)

    for copy in w_copies:
        copy.wait()
    w_sum = wsend[me].astype(f32)
    for offset in range(1, 16):
        w_sum = w_sum + wrecv[offset].astype(f32)
    wx[idp] = w_sum.astype(bf16)
    wx_copies = []
    for offset in LINE:
        device, _ = line(offset)
        wx_copies.append(send(wx.at[idp], wx.at[idp], wx_send.at[offset], wx_recv.at[offset], device))
    for copy in wx_copies:
        copy.start()
    lax.fori_loop(5, TILES, depth_tile, 0)

    for group8 in range(8):
        for half in range(2):
            for third in range(3):
                dsend[group8 * 2 + half, :, third * 128 : third * 128 + 128] = depth[
                    half * 3 + third, group8 * 8 : group8 * 8 + 8, :
                ].astype(bf16)
    d_copies = []
    for offset in PLANE:
        device, index = plane(offset)
        d_copies.append(send(dsend.at[index], drecv.at[offset], d_send.at[offset], d_recv.at[offset], device))
    for copy in d_copies:
        copy.start()

    for offset in range(1, 8):
        _, source = line(offset, -1)
        send(wx.at[source], wx.at[source], wx_send.at[offset], wx_recv.at[offset], line(offset)[0]).wait_recv()
    for copy in wx_copies:
        copy.wait_send()
    w_sum = wx[0].astype(f32)
    for index in range(1, 8):
        w_sum = w_sum + wx[index].astype(f32)
    wg_out[me] = w_sum.astype(bf16)
    wa_copies = []
    for offset in PLANE:
        device, _ = plane(offset)
        wa_copies.append(send(wg_out.at[me], wg_out.at[me], wa_send.at[offset], wa_recv.at[offset], device))
    for copy in wa_copies:
        copy.start()

    for offset in range(1, 8):
        _, source = line(offset, -1)
        device = line(offset)[0]
        send(root_out.at[source], root_out.at[source], x_send.at[offset], x_recv.at[offset], device).wait_recv()
        send(small_out.at[source], small_out.at[source], s_send.at[offset], s_recv.at[offset], device).wait_recv()
    for index in range(8):
        for k in range(CLASSES):
            factors[index * CLASSES + k] = jnp.broadcast_to(small_out[index, 0:1, k : k + 1], (8, 128))

    def class_rows(block, carry):
        rows = pl.ds(pl.multiple_of(block * 16, 16), 16)
        for half in range(2):
            lanes = slice(half * 128, half * 128 + 128)
            blocks = [root_out[index, rows, lanes].astype(f32).reshape(2, 8, 128) for index in range(8)]
            for k in range(CLASSES):
                total = blocks[0] * factors[k]
                for index in range(1, 8):
                    total = total + blocks[index] * factors[index * CLASSES + k]
                class_out[k, rows, lanes] = total.reshape(16, 128)
        return carry

    lax.fori_loop(0, 16, class_rows, 0)
    store = pltpu.make_async_copy(class_out, class_hbm, out_sem)
    store.start()
    for copy in d_copies:
        copy.wait()
    d_sum = dsend[me].astype(f32)
    for offset in range(1, 16):
        d_sum = d_sum + drecv[offset].astype(f32)
    dx[idp] = d_sum.astype(bf16)
    dx_copies = []
    for offset in LINE:
        device, _ = line(offset)
        dx_copies.append(send(dx.at[idp], dx.at[idp], dx_send.at[offset], dx_recv.at[offset], device))
    for copy in dx_copies:
        copy.start()
    for offset in range(1, 8):
        _, source = line(offset, -1)
        send(dx.at[source], dx.at[source], dx_send.at[offset], dx_recv.at[offset], line(offset)[0]).wait_recv()
    for copy in dx_copies:
        copy.wait_send()
    d_sum = dx[0].astype(f32)
    for index in range(1, 8):
        d_sum = d_sum + dx[index].astype(f32)
    dg_out[me] = d_sum.astype(bf16)
    da_copies = []
    for offset in PLANE:
        device, _ = plane(offset)
        da_copies.append(send(dg_out.at[me], dg_out.at[me], da_send.at[offset], da_recv.at[offset], device))
    for copy in da_copies:
        copy.start()
    for offset in range(1, 16):
        _, source = plane(offset, -1)
        device = plane(offset)[0]
        send(wg_out.at[source], wg_out.at[source], wa_send.at[offset], wa_recv.at[offset], device).wait_recv()
        send(dg_out.at[source], dg_out.at[source], da_send.at[offset], da_recv.at[offset], device).wait_recv()
    for copy in wa_copies + da_copies + roots + smalls:
        copy.wait_send()
    store.wait()


def finish_kernel(
    wg_hbm, dg_hbm, smalls_hbm, grads,
    loss_hbm, depth_hbm, depth_bias_hbm, weight_hbm, bias_hbm, class_weight, class_bias_hbm,
    wg, dg, smalls, buffer, loss, depth_grad, depth_bias, weight, bias, class_bias,
    load_sem, store_sem, class_in, class_out,
):
    loads = [
        pltpu.make_async_copy(src, dst, load_sem.at[i])
        for i, (src, dst) in enumerate([(wg_hbm, wg), (dg_hbm, dg), (smalls_hbm, smalls)])
    ]
    fetches = [pltpu.make_async_copy(grads.at[k], buffer.at[k], class_in.at[k]) for k in range(CLASSES)]
    stores = [pltpu.make_async_copy(buffer.at[k], class_weight.at[k], class_out.at[k]) for k in range(CLASSES)]
    results = [
        pltpu.make_async_copy(src, dst, store_sem.at[i])
        for i, (src, dst) in enumerate([
            (weight, weight_hbm), (depth_grad, depth_hbm), (depth_bias, depth_bias_hbm),
            (bias, bias_hbm), (class_bias, class_bias_hbm), (loss, loss_hbm),
        ])
    ]
    for load in loads + fetches:
        load.start()
    for load in loads:
        load.wait()
    weight[...] = wg[...].astype(f32).reshape(CHANNELS, REDUCED)
    results[0].start()
    for fetch, store in zip(fetches, stores):
        fetch.wait()
        store.start()
    for half in range(2):
        lanes = slice(half * 384, half * 384 + 384)
        for a in range(KERNEL):
            depth_grad[a, :, lanes] = dg[a * 2 + half, 0:7, :].astype(f32)
        depth_bias[lanes] = dg[half, 7:8, :].astype(f32).reshape(384)
    bias[...] = dg[2, 7:8, 0:REDUCED].astype(f32).reshape(REDUCED)
    small = smalls[0]
    for image in range(1, 8):
        small = small + smalls[image]
    class_bias[...] = small[0:1, 0:CLASSES].reshape(CLASSES)
    loss[...] = small[1:2, 0:1] * (1.0 / 8)
    for result in results[1:]:
        result.start()
    for copy in results + stores:
        copy.wait()


def body(
    features, depth_weight, depth_bias, reduce_weight, reduce_bias, class_weight, class_bias, labels
):
    vmem = pl.BlockSpec(memory_space=pltpu.VMEM)
    dma = pltpu.SemaphoreType.DMA
    hbm = pl.BlockSpec(memory_space=pltpu.HBM)
    smem = pl.BlockSpec(memory_space=pltpu.SMEM)
    scratch = [
        pltpu.VMEM((CLASSES, REDUCED, REDUCED), f32),
        pltpu.VMEM((ROWS, COLS, CHANNELS), bf16),
        pltpu.VMEM((KERNEL, KERNEL, CHANNELS), f32),
        pltpu.VMEM((CHANNELS,), f32),
        pltpu.VMEM((CHANNELS, REDUCED), bf16),
        pltpu.VMEM((REDUCED,), f32),
        pltpu.VMEM((CLASSES, REDUCED, REDUCED), bf16),
        pltpu.VMEM((CLASSES,), f32),
        pltpu.VMEM((8, REDUCED, REDUCED), bf16),
        pltpu.VMEM((8 * CLASSES, 8, 128), f32),
        pltpu.VMEM((TILES, LEAVES, LEAF_ROWS * PITCH, 128), f32),
        pltpu.VMEM((LEAVES, 4 * COLS, 128), f32),
        pltpu.VMEM((LEAVES, 2, 8, 128), f32),
        pltpu.VMEM((LEAVES, 2, 8, 128), f32),
        pltpu.VMEM((TILES, (ROWS + 12) * PITCH, 128), f32),
        pltpu.VMEM((TILES, ROWS * 32, 128), f32),
        pltpu.VMEM((ROWS * COLS, CHANNELS), bf16),
        pltpu.VMEM((ROWS * COLS, REDUCED), f32),
        pltpu.VMEM((ROWS * COLS, REDUCED), bf16),
        pltpu.VMEM((ROWS * COLS, REDUCED), bf16),
        pltpu.VMEM((TILES, ROWS * COLS, 128), f32),
        pltpu.VMEM((2, 3, 16, CHANNELS), bf16),
        pltpu.VMEM((4, 3, 8, CHANNELS), bf16),
        pltpu.VMEM((2, 3, COLS, CHANNELS), bf16),
        pltpu.VMEM((2, 3, 16, CHANNELS), bf16),
        pltpu.VMEM((4, 3, 8, CHANNELS), bf16),
        pltpu.VMEM((16, 16, REDUCED), bf16),
        pltpu.VMEM((16, 16, REDUCED), bf16),
        pltpu.VMEM((16, 16, REDUCED), f32),
        pltpu.VMEM((16, 16, REDUCED), bf16),
        pltpu.VMEM((1, REDUCED), f32),
        pltpu.VMEM((16, 1, REDUCED), f32),
        pltpu.VMEM((NEWTON_STEPS, 2, REDUCED, REDUCED), bf16),
        pltpu.VMEM((NEWTON_STEPS, 2, REDUCED, REDUCED), bf16),
        pltpu.VMEM((NEWTON_STEPS, 2, REDUCED, REDUCED), bf16),
        pltpu.VMEM((REDUCED, REDUCED), bf16),
        pltpu.VMEM((8, REDUCED), f32),
        pltpu.VMEM((16, 48, REDUCED), bf16),
        pltpu.VMEM((16, 48, REDUCED), bf16),
        pltpu.VMEM((8, 48, REDUCED), bf16),
        pltpu.VMEM((TILES, 64, 128), f32),
        pltpu.VMEM((16, 8, 384), bf16),
        pltpu.VMEM((16, 8, 384), bf16),
        pltpu.VMEM((8, 8, 384), bf16),
        dma((7,)), dma, dma((12,)), dma((12,)),
        dma((16,)), dma((16,)), dma((16,)), dma((16,)), dma((16,)), dma((16,)),
        dma((8,)), dma((8,)), dma((8,)), dma((8,)),
        dma((16,)), dma((16,)), dma((8,)), dma((8,)), dma((16,)), dma((16,)),
        dma((16,)), dma((16,)), dma((8,)), dma((8,)), dma((16,)), dma((16,)),
    ]
    partial = pl.pallas_call(
        main_kernel,
        out_shape=(
            jax.ShapeDtypeStruct((16, 48, REDUCED), bf16),
            jax.ShapeDtypeStruct((16, 8, 384), bf16),
            jax.ShapeDtypeStruct((8, 8, 128), f32),
            jax.ShapeDtypeStruct((CLASSES, REDUCED, REDUCED), f32),
        ),
        in_specs=[hbm] * 7 + [smem],
        out_specs=(vmem,) * 3 + (hbm,),
        scratch_shapes=scratch,
        compiler_params=pltpu.CompilerParams(
            collective_id=0, has_side_effects=True, vmem_limit_bytes=63 << 20
        ),
        name="pooling_step",
    )(
        features, depth_weight, depth_bias, reduce_weight, reduce_bias, class_weight, class_bias, labels
    )
    loss, *grads = pl.pallas_call(
        finish_kernel,
        out_shape=(
            jax.ShapeDtypeStruct((1, 1), f32),
            jax.ShapeDtypeStruct((KERNEL, KERNEL, CHANNELS), f32),
            jax.ShapeDtypeStruct((CHANNELS,), f32),
            jax.ShapeDtypeStruct((CHANNELS, REDUCED), f32),
            jax.ShapeDtypeStruct((REDUCED,), f32),
            jax.ShapeDtypeStruct((CLASSES, REDUCED, REDUCED), f32),
            jax.ShapeDtypeStruct((CLASSES,), f32),
        ),
        in_specs=[hbm] * 4,
        out_specs=(hbm,) * 7,
        scratch_shapes=[
            pltpu.VMEM((16, 48, REDUCED), bf16), pltpu.VMEM((16, 8, 384), bf16), pltpu.VMEM((8, 8, 128), f32),
            pltpu.VMEM((CLASSES, REDUCED, REDUCED), f32), pltpu.VMEM((1, 1), f32),
            pltpu.VMEM((KERNEL, KERNEL, CHANNELS), f32), pltpu.VMEM((CHANNELS,), f32),
            pltpu.VMEM((CHANNELS, REDUCED), f32), pltpu.VMEM((REDUCED,), f32), pltpu.VMEM((CLASSES,), f32),
            dma((3,)), dma((6,)), dma((CLASSES,)), dma((CLASSES,)),
        ],
        compiler_params=pltpu.CompilerParams(vmem_limit_bytes=63 << 20),
        name="outputs",
    )(*partial)
    return (loss.reshape(()), *grads)


def solution(mesh):
    placed = (P("dp", "sy", "sx", None), P(), P(), P(), P(), P(), P(), P("dp"))
    return jax.shard_map(
        body,
        mesh=mesh,
        in_specs=placed,
        out_specs=(P(), P(), P(), P(), P(), P(), P()),
        check_vma=False,
    )
```
